32 devices in a mesh: grp: 2 (over x), seq: 16 (over z, y, core).
Axes of the slice: x: 2, y: 2, z: 4, core: 2. Of those that a mesh axis runs over, the one named last changes fastest.
Arguments:
- query_rows: bfloat16 [4096, 16, 128], P(('grp', 'seq')), parts along dimension 0, may hold values from -120 to 120
- key_rows: bfloat16 [4096, 16, 128], P(('grp', 'seq')), parts along dimension 0, may hold values from -6 to 6
- value_rows: bfloat16 [4096, 16, 128], P(('grp', 'seq')), parts along dimension 0, may hold values from -6 to 6
- out_grad: bfloat16 [4096, 16, 128], P(('grp', 'seq')), parts along dimension 0, may hold values from -6 to 6
- window_blocks: int32 [16], replicated, may hold values from 1 to 3, as said below
- section_heads: int32 [4, 4], replicated, may hold values from 0 to 15, as said below
Outputs:
- attended: bfloat16 [4096, 16, 128], P(('grp', 'seq')), parts along dimension 0
- query_grad: bfloat16 [4096, 16, 128], P(('grp', 'seq')), parts along dimension 0
- key_grad: bfloat16 [4096, 16, 128], P(('grp', 'seq')), parts along dimension 0
- value_grad: bfloat16 [4096, 16, 128], P(('grp', 'seq')), parts along dimension 0
The draws below stay inside these ranges and needn't reach their ends.
There are 2 independent parts, one for each index of `grp`. The reference program is written for one: setup_inputs(seed, part) draws one part's arguments, and reference() takes and returns one part's arrays. A program takes and returns all parts, laid end to end along the dimension named above; an argument that names none is the same for every part. Nothing has to cross between parts.
Inputs may be any that keep to these rules, and one draw needn't show every extreme that they name: `section_heads`: row s lists 4 different heads; every head appears in some row. `window_blocks`: some head has width 1 and some head has width 3.
All inputs are finite; a program needn't handle non-finite values.
Results may differ from the reference program's by a relative error of at most 0.03.
Values may be sent and summed in bfloat16 or wider, within the bound.
No kernel may reach another device: no remote copies, remote signals or barrier semaphores. Data moves between devices by JAX's collectives and lax.ppermute only.
A program may use at most 128 MiB of HBM per device.

```python
import math
import jax
import jax.numpy as jnp
from jax import lax

H = 16
DH = 128
BLK = 128
WB = 3
HS = 4
LOGNB = 4
NB = 16
TOKENS = 2048


def paired_rows(key):
    base_keys = jax.random.normal(jax.random.fold_in(key, 11), (TOKENS, H, DH), jnp.float32)
    base_queries = jax.random.normal(jax.random.fold_in(key, 12), (TOKENS, H, DH), jnp.float32)
    return (jnp.clip(base_queries, -120.0, 120.0), jnp.clip(base_keys, -6.0, 6.0))


def draw_query_rows(key, part):
    queries, unused_keys = paired_rows(key)
    return queries.astype(jnp.bfloat16)


def draw_key_rows(key, part):
    unused_queries, keys_drawn = paired_rows(key)
    return keys_drawn.astype(jnp.bfloat16)


def draw_window_blocks(key, part):
    widths = jax.random.randint(jax.random.fold_in(key, 21), (H,), 1, WB + 1)
    widest = jax.random.randint(jax.random.fold_in(key, 22), (), 0, H)
    narrow = (widest + 1 + jax.random.randint(jax.random.fold_in(key, 23), (), 0, H - 1)) % H
    head_ids = jnp.arange(H, dtype=jnp.int32)
    widths = jnp.where(head_ids == widest, WB, widths)
    widths = jnp.where(head_ids == narrow, 1, widths)
    return widths.astype(jnp.int32)


def draw_section_heads(key, part):
    needed = LOGNB * HS
    copies = needed // H + 1
    orders = jnp.concatenate([jax.random.permutation(jax.random.fold_in(key, 31 + number), H) for number in range(copies)])
    return orders[:needed].reshape(LOGNB, HS).astype(jnp.int32)


def level_of(rng, dims, cuts, smallest, top_value):
    gain = 1.0
    for dim, parts in cuts:
        steps = jax.random.uniform(jax.random.fold_in(jax.random.fold_in(rng, 6), dim), (parts,), jnp.float32, smallest / len(cuts), top_value / len(cuts))
        gain = gain * jnp.repeat(jnp.exp(steps), dims[dim] // parts).reshape((-1,) + (1,) * (len(dims) - 1 - dim))
    return gain


def scatter_about(stream_key, shape, spread, most, split=(), held_as=jnp.bfloat16):
    entries = spread * jax.random.normal(stream_key, shape, jnp.float32)
    if split:
        entries = entries * level_of(stream_key, shape, split, -0.22, 0.18)
    return jnp.clip(entries, -most, most).astype(held_as)


def setup_inputs(seed: int = 0, part: int = 0) -> dict:
    arg_keys = jax.random.split(jax.random.key(seed), 7)
    part_splits = jax.random.split(jax.random.fold_in(arg_keys[6], part), 7)
    return {
        "query_rows": draw_query_rows(jax.random.fold_in(jax.random.fold_in(arg_keys[6], part), 71), part),
        "key_rows": draw_key_rows(jax.random.fold_in(jax.random.fold_in(arg_keys[6], part), 71), part),
        "value_rows": scatter_about(part_splits[2], (TOKENS, H, DH), 1.0, 6.0, ((0, 16),)),
        "out_grad": scatter_about(part_splits[3], (TOKENS, H, DH), 1.0, 6.0, ((0, 16),)),
        "window_blocks": draw_window_blocks(jax.random.fold_in(arg_keys[6], 71), part),
        "section_heads": draw_section_heads(jax.random.fold_in(arg_keys[6], 71), part),
    }


blocked_score = -1e+30

def reference(query_rows, key_rows, value_rows, out_grad, window_blocks, section_heads):
    score_scale = 1.0 / math.sqrt(DH)
    head_ids = jnp.arange(H, dtype=jnp.int32)
    section_used = jnp.any(section_heads[:, :, None] == head_ids[None, None, :], axis=1)
    section_span = (2 ** jnp.arange(LOGNB, dtype=jnp.int32)).astype(jnp.int32)
    far_valid = section_used & (section_span[:, None] >= window_blocks[None, :])
    offsets = jnp.arange(2 * WB - 1, dtype=jnp.int32) - (WB - 1)
    near_heads = jnp.abs(offsets)[None, :] < window_blocks[:, None]

    def take_block(source, block_id):
        row_start = (jnp.clip(block_id, 0, NB - 1) * BLK).astype(jnp.int32)
        return lax.dynamic_slice_in_dim(source, row_start, BLK, 0)

    def one_block(totals, block_index):
        key_total, value_total = totals
        near_index = block_index + offsets
        far_index = jnp.bitwise_xor(block_index, section_span)
        linked = jnp.concatenate([near_index, far_index]).astype(jnp.int32)
        in_range = (near_index >= 0) & (near_index < NB)
        linked_valid = jnp.concatenate([near_heads & in_range[None, :], far_valid.T], axis=1)
        link_mask = linked_valid[:, None, :, None]
        queries = take_block(query_rows, block_index).astype(jnp.float32)
        grad_rows = take_block(out_grad, block_index).astype(jnp.float32)
        key_sets = jax.vmap(lambda block_id: take_block(key_rows, block_id))(linked).astype(jnp.float32)
        value_sets = jax.vmap(lambda block_id: take_block(value_rows, block_id))(linked).astype(jnp.float32)
        scores = jnp.einsum('qhd,ckhd->hqck', queries, key_sets) * score_scale
        scores = jnp.where(link_mask, scores, blocked_score)
        row_top = lax.optimization_barrier(jnp.max(scores, axis=(2, 3), keepdims=True))
        row_total = lax.optimization_barrier(jnp.sum(jnp.where(link_mask, jnp.exp(scores - row_top), 0.0), axis=(2, 3), keepdims=True))
        log_total = row_top + jnp.log(row_total)
        attn_probs = jnp.where(link_mask, jnp.exp(scores - log_total), 0.0).astype(jnp.bfloat16)
        attn_probs = lax.optimization_barrier(attn_probs).astype(jnp.float32)
        attended = jnp.einsum('hqck,ckhd->qhd', attn_probs, value_sets).astype(jnp.bfloat16)
        attended_wide = lax.optimization_barrier(attended).astype(jnp.float32)
        row_delta = lax.optimization_barrier(jnp.sum(grad_rows * attended_wide, axis=-1)).T
        dprobs = jnp.einsum('qhd,ckhd->hqck', grad_rows, value_sets)
        dscores = (attn_probs * (dprobs - row_delta[:, :, None, None])).astype(jnp.bfloat16)
        dscores = lax.optimization_barrier(dscores).astype(jnp.float32)
        query_grad = (jnp.einsum('hqck,ckhd->qhd', dscores, key_sets) * score_scale).astype(jnp.bfloat16)
        key_part = jnp.einsum('hqck,qhd->ckhd', dscores, queries) * score_scale
        value_part = jnp.einsum('hqck,qhd->ckhd', attn_probs, grad_rows)
        for column in range(linked.shape[0]):
            row_start = (jnp.clip(linked[column], 0, NB - 1) * BLK).astype(jnp.int32)
            current = lax.dynamic_slice_in_dim(key_total, row_start, BLK, 0)
            key_total = lax.dynamic_update_slice_in_dim(key_total, current + key_part[column], row_start, 0)
            current = lax.dynamic_slice_in_dim(value_total, row_start, BLK, 0)
            value_total = lax.dynamic_update_slice_in_dim(value_total, current + value_part[column], row_start, 0)
        return ((key_total, value_total), (attended, query_grad))
    zeros_init = jnp.zeros((TOKENS, H, DH), jnp.float32)
    block_list = jnp.arange(NB, dtype=jnp.int32)
    (key_total, value_total), (attended, query_grad) = lax.scan(one_block, (zeros_init, zeros_init), block_list)
    attended = attended.reshape(TOKENS, H, DH)
    query_grad = query_grad.reshape(TOKENS, H, DH)
    return (attended, query_grad, key_total.astype(jnp.bfloat16), value_total.astype(jnp.bfloat16))
```

```python
import functools
import math

import jax
import jax.numpy as jnp
from jax import lax
from jax.experimental import pallas as pl
from jax.experimental.pallas import tpu as pltpu
from jax.sharding import PartitionSpec as P

BLK = 128
WB = 3
HALO = WB - 1
NT = (((1,), (1,)), ((), ()))
NN = (((1,), (0,)), ((), ()))
blocked_score = -1e30


def mm(a, b, dims=NN):
    return lax.dot_general(a, b, dims, preferred_element_type=jnp.float32)


def pack_kernel(*refs):
    out = refs[-1]
    for i, ref in enumerate(refs[:-1]):
        out[:, i] = jnp.transpose(ref[...], (1, 0, 2))


def pack(arrays):
    tokens, heads, width = arrays[0].shape
    chunk = 64
    count = len(arrays)
    return pl.pallas_call(
        pack_kernel,
        grid=(tokens // chunk,),
        in_specs=[pl.BlockSpec((chunk, heads, width), lambda i: (i, 0, 0))] * count,
        out_specs=pl.BlockSpec((heads, count, chunk, width), lambda i: (0, 0, i, 0)),
        out_shape=jax.ShapeDtypeStruct((heads, count, tokens, width), jnp.bfloat16),
        cost_estimate=pl.CostEstimate(
            flops=0, transcendentals=0, bytes_accessed=4 * count * tokens * heads * width
        ),
    )(*arrays)


def unpack_kernel(src, *outs):
    for i, out in enumerate(outs):
        out[...] = jnp.transpose(src[:, i], (1, 0, 2))


def unpack(stacked):
    heads, count, tokens, width = stacked.shape
    chunk = 64
    return pl.pallas_call(
        unpack_kernel,
        grid=(tokens // chunk,),
        in_specs=[pl.BlockSpec((heads, count, chunk, width), lambda i: (0, 0, i, 0))],
        out_specs=[pl.BlockSpec((chunk, heads, width), lambda i: (i, 0, 0))] * count,
        out_shape=[jax.ShapeDtypeStruct((tokens, heads, width), jnp.bfloat16)] * count,
        cost_estimate=pl.CostEstimate(
            flops=0, transcendentals=0, bytes_accessed=4 * count * tokens * heads * width
        ),
    )(stacked)


def attend_kernel(info, x, out, keys, values, key_acc, value_acc, *, blocks, unroll):
    width = info[0]
    far_valid = info[1]
    far_bit = info[2]
    scale = 1.0 / math.sqrt(x.shape[-1])
    scale2 = scale * math.log2(math.e)
    span = (2 * HALO + 1) * BLK
    zero = jnp.zeros((HALO * BLK, x.shape[-1]), jnp.bfloat16)
    for ref, part in ((keys, 1), (values, 2)):
        ref[: HALO * BLK] = zero
        ref[(HALO + blocks) * BLK :] = zero
        for b in range(blocks):
            ref[(HALO + b) * BLK : (HALO + b + 1) * BLK] = x[b, part]
    key_acc[...] = jnp.zeros_like(key_acc)
    value_acc[...] = jnp.zeros_like(value_acc)
    offset = lax.broadcasted_iota(jnp.int32, (1, span), 1) // BLK - HALO
    near = jnp.abs(offset) < width
    far_on = jnp.full((1, BLK), far_valid, jnp.int32) > 0

    def one(b):
        q, g = x[b, 0], x[b, 3]
        start = pl.multiple_of(b * BLK, BLK)
        far_start = pl.multiple_of((HALO + (b ^ far_bit)) * BLK, BLK)
        kw, vw = keys[pl.ds(start, span)], values[pl.ds(start, span)]
        kf, vf = keys[pl.ds(far_start, BLK)], values[pl.ds(far_start, BLK)]
        link = near & (offset + b >= 0) & (offset + b < blocks)
        sw = jnp.where(link, mm(q, kw, NT) * scale2, blocked_score)
        sf = jnp.where(far_on, mm(q, kf, NT) * scale2, blocked_score)
        top = jnp.maximum(jnp.max(sw, axis=1, keepdims=True), jnp.max(sf, axis=1, keepdims=True))
        ew, ef = jnp.exp2(sw - top), jnp.exp2(sf - top)
        total = jnp.sum(ew, axis=1, keepdims=True) + jnp.sum(ef, axis=1, keepdims=True)
        inverse = 1.0 / total
        pw, pf = (ew * inverse).astype(jnp.bfloat16), (ef * inverse).astype(jnp.bfloat16)
        attended = (mm(pw, vw) + mm(pf, vf)).astype(jnp.bfloat16)
        delta = jnp.sum(
            g.astype(jnp.float32) * attended.astype(jnp.float32), axis=1, keepdims=True
        )
        dw = (pw.astype(jnp.float32) * (mm(g, vw, NT) - delta)).astype(jnp.bfloat16)
        df = (pf.astype(jnp.float32) * (mm(g, vf, NT) - delta)).astype(jnp.bfloat16)
        out[b, 0] = attended
        out[b, 1] = ((mm(dw, kw) + mm(df, kf)) * scale).astype(jnp.bfloat16)
        qt, gt = jnp.transpose(q), jnp.transpose(g)
        key_acc[:, pl.ds(start, span)] += mm(qt, dw)
        value_acc[:, pl.ds(start, span)] += mm(gt, pw)
        key_acc[:, pl.ds(far_start, BLK)] += mm(qt, df)
        value_acc[:, pl.ds(far_start, BLK)] += mm(gt, pf)

    def step(i, carry):
        for u in range(unroll):
            one(i * unroll + u)
        return carry

    lax.fori_loop(0, blocks // unroll, step, 0)
    for b in range(blocks):
        cols = slice((HALO + b) * BLK, (HALO + b + 1) * BLK)
        out[b, 2] = jnp.transpose(key_acc[:, cols] * scale).astype(jnp.bfloat16)
        out[b, 3] = jnp.transpose(value_acc[:, cols]).astype(jnp.bfloat16)


def attend(info, x, unroll=2):
    blocks, _, _, width = x.shape
    padded = (blocks + 2 * HALO) * BLK
    return pl.pallas_call(
        functools.partial(attend_kernel, blocks=blocks, unroll=unroll),
        in_specs=[
            pl.BlockSpec(memory_space=pltpu.SMEM),
            pl.BlockSpec(memory_space=pltpu.VMEM),
        ],
        out_specs=pl.BlockSpec(memory_space=pltpu.VMEM),
        out_shape=jax.ShapeDtypeStruct(x.shape, jnp.bfloat16),
        scratch_shapes=[
            pltpu.VMEM((padded, width), jnp.bfloat16),
            pltpu.VMEM((padded, width), jnp.bfloat16),
            pltpu.VMEM((width, padded), jnp.float32),
            pltpu.VMEM((width, padded), jnp.float32),
        ],
        cost_estimate=pl.CostEstimate(
            flops=blocks * 6 * 6 * 2 * BLK**3,
            transcendentals=blocks * 6 * BLK * BLK,
            bytes_accessed=2 * x.size * 2,
        ),
    )(info, x)


def partner(value, axis, apart):
    return lax.ppermute(value, axis, [(i, i ^ 1 << apart) for i in range(lax.axis_size(axis))])


def passed_along(value, axis, by):
    peers = lax.axis_size(axis)
    pairs = [(i, i + by) for i in range(peers) if 0 <= i + by < peers]
    return lax.ppermute(value, axis, pairs)


def to_slots(values, picker):
    return jnp.sum(jnp.where(picker[None, :, :, None], values[:, None, :, :], 0.0), axis=2)


def to_heads(values, picker, filler):
    covered = jnp.any(picker, axis=0)
    summed = jnp.sum(jnp.where(picker[None, :, :, None], values[:, :, None, :], 0.0), axis=1)
    return jnp.where(covered[None, :, None], summed, filler)


def rows_to_heads(values, picker):
    return jnp.einsum(
        "jqid,ih->jqhd", values, picker.astype(jnp.float32), precision=lax.Precision.HIGHEST
    )


def pick_heads(values, picker):
    chooser = picker.astype(jnp.bfloat16)
    return jnp.einsum("ih,jqhd->jqid", chooser, values, preferred_element_type=jnp.float32).astype(
        jnp.bfloat16
    )


def partner_route(values, section_index, low_bits):
    return partner(values, "seq", section_index - low_bits)


def partner_back(values, section_index, low_bits):
    return partner(values, "seq", section_index - low_bits)


def extend_blocks(values, reach, halo_blocks, blocks_dev, mover):
    pieces = [mover(values, distance) for distance in range(reach, 0, -1)]
    pieces = pieces + [values] + [mover(values, -distance) for distance in range(1, reach + 1)]
    start = reach * blocks_dev - halo_blocks
    whole = jnp.concatenate(pieces, axis=1)
    return whole


def move_keys(values, distance):
    return passed_along(values, "seq", distance)


def window_sets(extended, blocks_dev, spread):
    return jnp.stack(
        [extended[:, offset : offset + blocks_dev] for offset in range(spread)], axis=2
    )


def per_device(query_rows, key_rows, value_rows, out_grad, window_blocks, section_heads):
    tokens_dev, head_count, head_width = query_rows.shape
    blocks_dev = tokens_dev // BLK
    low_bits = blocks_dev.bit_length() - 1
    seq_count = lax.axis_size("seq")
    section_total = low_bits + seq_count.bit_length() - 1
    halo_blocks = WB - 1
    reach = (halo_blocks + blocks_dev - 1) // blocks_dev
    padding = reach * blocks_dev
    spread = 2 * WB - 1
    score_scale = 1.0 / math.sqrt(head_width)
    first_block = lax.axis_index("seq") * blocks_dev + jnp.arange(blocks_dev, dtype=jnp.int32)
    all_blocks = blocks_dev * seq_count
    query_blocks = query_rows.reshape(blocks_dev, BLK, head_count, head_width)
    key_blocks = key_rows.reshape(blocks_dev, BLK, head_count, head_width)
    value_blocks = value_rows.reshape(blocks_dev, BLK, head_count, head_width)
    grad_blocks = out_grad.reshape(blocks_dev, BLK, head_count, head_width)
    offsets = jnp.arange(spread, dtype=jnp.int32) - halo_blocks
    near_block = first_block[:, None] + offsets[None, :]
    in_range = (near_block >= 0) & (near_block < all_blocks)
    near_mask = in_range[:, None, :] & (
        jnp.abs(offsets)[None, None, :] < window_blocks[None, :, None]
    )
    wide_mask = near_mask[:, :, None, :, None]
    head_ids = jnp.arange(head_count, dtype=jnp.int32)
    paired = jnp.stack([key_blocks, value_blocks])
    extended = extend_blocks(paired, reach, halo_blocks, blocks_dev, move_keys)
    near_sets = window_sets(extended, blocks_dev, spread)
    near_keys = near_sets[0]
    near_values = near_sets[1]
    near_scores = (
        jnp.einsum("jqhd,jckhd->jhqck", query_blocks, near_keys, preferred_element_type=jnp.float32)
        * score_scale
    )
    near_scores = jnp.where(wide_mask, near_scores, blocked_score)
    top_score = jnp.max(near_scores, axis=(3, 4))
    records = []
    for section_index in range(section_total):
        picker = section_heads[section_index][:, None] == head_ids[None, :]
        slot_width = jnp.sum(jnp.where(picker, window_blocks[None, :], 0), axis=1)
        slot_valid = 2**section_index >= slot_width
        chosen_query = pick_heads(query_blocks, picker)
        chosen_grad = pick_heads(grad_blocks, picker)
        chosen_pair = jnp.stack([pick_heads(key_blocks, picker), pick_heads(value_blocks, picker)])
        partner_pair = partner_route(chosen_pair, section_index, low_bits)
        far_scores = (
            jnp.einsum(
                "jqid,jkid->jiqk", chosen_query, partner_pair[0], preferred_element_type=jnp.float32
            )
            * score_scale
        )
        far_scores = jnp.where(slot_valid[None, :, None, None], far_scores, blocked_score)
        top_score = jnp.maximum(
            top_score, to_heads(jnp.max(far_scores, axis=3), picker, blocked_score)
        )
        records.append(
            (
                section_index,
                picker,
                slot_valid,
                chosen_query,
                chosen_grad,
                chosen_pair,
                partner_pair,
                far_scores,
            )
        )
    row_total = jnp.sum(
        jnp.where(wide_mask, jnp.exp(near_scores - top_score[:, :, :, None, None]), 0.0),
        axis=(3, 4),
    )
    for record in records:
        picker = record[1]
        slot_top = to_slots(top_score, picker)
        far_sum = jnp.sum(
            jnp.where(
                record[2][None, :, None, None], jnp.exp(record[7] - slot_top[:, :, :, None]), 0.0
            ),
            axis=3,
        )
        row_total = row_total + to_heads(far_sum, picker, 0.0)
    log_total = top_score + jnp.log(row_total)
    near_probs = jnp.where(
        wide_mask, jnp.exp(near_scores - log_total[:, :, :, None, None]), 0.0
    ).astype(jnp.bfloat16)
    attended_sum = jnp.einsum(
        "jhqck,jckhd->jqhd", near_probs, near_values, preferred_element_type=jnp.float32
    )
    far_probs_list = []
    for record in records:
        picker = record[1]
        slot_lse = to_slots(log_total, picker)
        far_probs = jnp.where(
            record[2][None, :, None, None], jnp.exp(record[7] - slot_lse[:, :, :, None]), 0.0
        ).astype(jnp.bfloat16)
        far_probs_list.append((far_probs, slot_lse))
        attended_sum = attended_sum + rows_to_heads(
            jnp.einsum(
                "jiqk,jkid->jqid", far_probs, record[6][1], preferred_element_type=jnp.float32
            ),
            picker,
        )
    attended = attended_sum.astype(jnp.bfloat16)
    row_delta = jnp.transpose(
        jnp.sum(grad_blocks.astype(jnp.float32) * attended.astype(jnp.float32), axis=-1), (0, 2, 1)
    )
    near_dprob = jnp.einsum(
        "jqhd,jckhd->jhqck", grad_blocks, near_values, preferred_element_type=jnp.float32
    )
    near_dscore = (
        near_probs.astype(jnp.float32) * (near_dprob - row_delta[:, :, :, None, None])
    ).astype(jnp.bfloat16)
    query_sum = jnp.einsum(
        "jhqck,jckhd->jqhd", near_dscore, near_keys, preferred_element_type=jnp.float32
    )
    far_dscores = []
    for record, probs_pair in zip(records, far_probs_list):
        picker = record[1]
        slot_delta = to_slots(row_delta, picker)
        far_dprob = jnp.einsum(
            "jqid,jkid->jiqk", record[4], record[6][1], preferred_element_type=jnp.float32
        )
        far_dscore = (
            probs_pair[0].astype(jnp.float32) * (far_dprob - slot_delta[:, :, :, None])
        ).astype(jnp.bfloat16)
        far_dscores.append((far_dscore, slot_delta))
        query_sum = query_sum + rows_to_heads(
            jnp.einsum(
                "jiqk,jkid->jqid", far_dscore, record[6][0], preferred_element_type=jnp.float32
            ),
            picker,
        )
    query_grad = (
        (query_sum * score_scale).astype(jnp.bfloat16).reshape(tokens_dev, head_count, head_width)
    )
    near_key_part = (
        jnp.einsum(
            "jhqck,jqhd->jckhd", near_dscore, query_blocks, preferred_element_type=jnp.float32
        )
        * score_scale
    )
    near_value_part = jnp.einsum(
        "jhqck,jqhd->jckhd", near_probs, grad_blocks, preferred_element_type=jnp.float32
    )
    stacked_parts = jnp.stack([near_key_part, near_value_part])
    extended_count = blocks_dev + 2 * padding
    base = padding - halo_blocks
    extended_ids = jnp.arange(extended_count, dtype=jnp.int32)
    own_ids = jnp.arange(blocks_dev, dtype=jnp.int32)
    spread_ids = jnp.arange(spread, dtype=jnp.int32)
    placer = (
        extended_ids[:, None, None] == base + own_ids[None, :, None] + spread_ids[None, None, :]
    ).astype(jnp.float32)
    gathered = jnp.einsum(
        "ejc,xjckhd->xekhd", placer, stacked_parts, precision=lax.Precision.HIGHEST
    )
    own_grads = gathered[:, padding : padding + blocks_dev]
    for distance in range(1, reach + 1):
        lower_slab = gathered[
            :, padding - distance * blocks_dev : padding - (distance - 1) * blocks_dev
        ]
        own_grads = own_grads + passed_along(
            lower_slab.astype(jnp.bfloat16), "seq", -distance
        ).astype(lower_slab.dtype)
        upper_start = padding + blocks_dev + (distance - 1) * blocks_dev
        upper_slab = gathered[:, upper_start : upper_start + blocks_dev]
        own_grads = own_grads + passed_along(
            upper_slab.astype(jnp.bfloat16), "seq", distance
        ).astype(upper_slab.dtype)
    for record, probs_pair, dscore_pair in zip(records, far_probs_list, far_dscores):
        picker = record[1]
        key_part = (
            jnp.einsum(
                "jiqk,jqid->jkid", dscore_pair[0], record[3], preferred_element_type=jnp.float32
            )
            * score_scale
        )
        value_part = jnp.einsum(
            "jiqk,jqid->jkid", probs_pair[0], record[4], preferred_element_type=jnp.float32
        )
        returned = partner_back(jnp.stack([key_part, value_part]), record[0], low_bits)
        own_grads = own_grads + jnp.stack(
            [rows_to_heads(returned[0], picker), rows_to_heads(returned[1], picker)]
        )
    key_grad = own_grads[0].astype(jnp.bfloat16).reshape(tokens_dev, head_count, head_width)
    value_grad = own_grads[1].astype(jnp.bfloat16).reshape(tokens_dev, head_count, head_width)
    return (attended.reshape(tokens_dev, head_count, head_width), query_grad, key_grad, value_grad)


def sharded_by_head(query_rows, key_rows, value_rows, out_grad, window_blocks, section_heads):
    head = lax.axis_index("seq")
    sections = section_heads.shape[0]
    span = 2 ** jnp.arange(sections, dtype=jnp.int32)
    used = jnp.any(section_heads == head, axis=1)
    width = jnp.sum(jnp.where(jnp.arange(window_blocks.shape[0]) == head, window_blocks, 0))
    bit = jnp.sum(jnp.where(used, span, 0))
    valid = (bit >= width).astype(jnp.int32)
    info = jnp.stack([width, valid, bit]).astype(jnp.int32)
    sent = pack([query_rows, key_rows, value_rows, out_grad])
    mine = lax.all_to_all(sent, "seq", 0, 0, tiled=True)
    back = lax.all_to_all(attend(info, mine), "seq", 0, 0, tiled=True)
    return tuple(unpack(back))


def solution(mesh):
    spec = P(("grp", "seq"), None, None)
    peers = mesh.shape["seq"]

    def per_device_any(*args):
        tokens, heads, width = args[0].shape
        sections, listed = args[5].shape
        once = sections * listed == heads
        if tokens == BLK and heads == peers and once and 1 << sections == peers:
            return sharded_by_head(*args)
        return per_device(*args)

    return jax.shard_map(
        per_device_any,
        mesh=mesh,
        in_specs=(spec, spec, spec, spec, P(), P()),
        out_specs=(spec,) * 4,
        check_vma=False,
    )
```

```python
import functools
import math

import jax
import jax.numpy as jnp
from jax import lax
from jax.experimental import pallas as pl
from jax.experimental.pallas import tpu as pltpu
from jax.sharding import PartitionSpec as P

BLK = 128
WB = 3
HALO = WB - 1
SPAN = (2 * HALO + 1) * BLK
LINKED = SPAN + BLK
NT = (((1,), (1,)), ((), ()))
NN = (((1,), (0,)), ((), ()))
blocked_score = -1e30


def mm(a, b, dims=NN):
    return lax.dot_general(a, b, dims, preferred_element_type=jnp.float32)


def moved_cost(arrays):
    return pl.CostEstimate(
        flops=0, transcendentals=0, bytes_accessed=4 * sum(a.size for a in arrays)
    )


def pack_kernel(*refs):
    out = refs[-1]
    for i, ref in enumerate(refs[:-1]):
        out[:, i] = jnp.transpose(ref[...], (1, 0, 2))


def pack(arrays):
    tokens, heads, width = arrays[0].shape
    chunk = 64
    count = len(arrays)
    return pl.pallas_call(
        pack_kernel,
        grid=(tokens // chunk,),
        in_specs=[pl.BlockSpec((chunk, heads, width), lambda i: (i, 0, 0))] * count,
        out_specs=pl.BlockSpec((heads, count, chunk, width), lambda i: (0, 0, i, 0)),
        out_shape=jax.ShapeDtypeStruct((heads, count, tokens, width), jnp.bfloat16),
        cost_estimate=moved_cost(arrays),
    )(*arrays)


def unpack_kernel(src, *outs):
    for i, out in enumerate(outs):
        out[...] = jnp.transpose(src[:, i], (1, 0, 2))


def unpack(stacked):
    heads, count, tokens, width = stacked.shape
    chunk = 64
    return pl.pallas_call(
        unpack_kernel,
        grid=(tokens // chunk,),
        in_specs=[pl.BlockSpec((heads, count, chunk, width), lambda i: (0, 0, i, 0))],
        out_specs=[pl.BlockSpec((chunk, heads, width), lambda i: (i, 0, 0))] * count,
        out_shape=[jax.ShapeDtypeStruct((tokens, heads, width), jnp.bfloat16)] * count,
        cost_estimate=moved_cost([stacked]),
    )(stacked)


def padded_copy(ref, x, part, blocks):
    zero = jnp.zeros((HALO * BLK, x.shape[-1]), jnp.bfloat16)
    ref[: HALO * BLK] = zero
    ref[(HALO + blocks) * BLK :] = zero
    for b in range(blocks):
        ref[(HALO + b) * BLK : (HALO + b + 1) * BLK] = x[b, part]


def starts(b, far_bit):
    near = pl.multiple_of(b * BLK, BLK)
    far = pl.multiple_of((HALO + (b ^ far_bit)) * BLK, BLK)
    return near, far


def forward_kernel(info, x, out, probs, keys, values, *, blocks, group):
    width, far_valid, far_bit = info[0], info[1], info[2]
    scale2 = math.log2(math.e) / math.sqrt(x.shape[-1])

    @pl.when(pl.program_id(0) == 0)
    def _():
        padded_copy(keys, x, 1, blocks)
        padded_copy(values, x, 2, blocks)

    offset = lax.broadcasted_iota(jnp.int32, (1, SPAN), 1) // BLK - HALO
    near = jnp.abs(offset) < width
    far_on = jnp.full((1, BLK), far_valid, jnp.int32) > 0
    for u in range(group):
        b = pl.program_id(0) * group + u
        q = x[b, 0]
        at, far_at = starts(b, far_bit)
        link = near & (offset + b >= 0) & (offset + b < blocks)
        sw = jnp.where(link, mm(q, keys[pl.ds(at, SPAN)], NT) * scale2, blocked_score)
        sf = jnp.where(far_on, mm(q, keys[pl.ds(far_at, BLK)], NT) * scale2, blocked_score)
        top = jnp.maximum(jnp.max(sw, axis=1, keepdims=True), jnp.max(sf, axis=1, keepdims=True))
        ew, ef = jnp.exp2(sw - top), jnp.exp2(sf - top)
        total = jnp.sum(ew, axis=1, keepdims=True) + jnp.sum(ef, axis=1, keepdims=True)
        inverse = 1.0 / total
        pw, pf = (ew * inverse).astype(jnp.bfloat16), (ef * inverse).astype(jnp.bfloat16)
        out[u, 0] = (mm(pw, values[pl.ds(at, SPAN)]) + mm(pf, values[pl.ds(far_at, BLK)])).astype(
            jnp.bfloat16
        )
        probs[u, :, :SPAN] = pw
        probs[u, :, SPAN:] = pf


def forward(info, x, group=2):
    blocks, count, _, width = x.shape
    padded = (blocks + 2 * HALO) * BLK
    return pl.pallas_call(
        functools.partial(forward_kernel, blocks=blocks, group=group),
        grid=(blocks // group,),
        in_specs=[
            pl.BlockSpec(memory_space=pltpu.SMEM),
            pl.BlockSpec(x.shape, lambda i: (0, 0, 0, 0)),
        ],
        out_specs=[
            pl.BlockSpec((group, 1, BLK, width), lambda i: (i, 0, 0, 0)),
            pl.BlockSpec((group, BLK, LINKED), lambda i: (i, 0, 0)),
        ],
        out_shape=[
            jax.ShapeDtypeStruct((blocks, 1, BLK, width), jnp.bfloat16),
            jax.ShapeDtypeStruct((blocks, BLK, LINKED), jnp.bfloat16),
        ],
        scratch_shapes=[pltpu.VMEM((padded, width), jnp.bfloat16)] * 2,
        cost_estimate=pl.CostEstimate(
            flops=blocks * 4 * BLK * LINKED * width,
            transcendentals=blocks * BLK * LINKED,
            bytes_accessed=2 * (x.size + blocks * BLK * (LINKED + width)),
        ),
    )(info, x)


def backward_kernel(
    info, x, g_all, o_all, probs, out, keys, values, key_acc, value_acc, *, blocks, group
):
    far_bit = info[2]
    scale = 1.0 / math.sqrt(x.shape[-1])
    i = pl.program_id(0)

    @pl.when(i == 0)
    def _():
        padded_copy(keys, x, 1, blocks)
        padded_copy(values, x, 2, blocks)
        key_acc[...] = jnp.zeros_like(key_acc)
        value_acc[...] = jnp.zeros_like(value_acc)

    for u in range(group):
        b = i * group + u
        q, g, o = x[b, 0], g_all[b, 0], o_all[u, 0]
        at, far_at = starts(b, far_bit)
        pw, pf = probs[u, :, :SPAN], probs[u, :, SPAN:]
        delta = jnp.sum(g.astype(jnp.float32) * o.astype(jnp.float32), axis=1, keepdims=True)
        dw = pw.astype(jnp.float32) * (mm(g, values[pl.ds(at, SPAN)], NT) - delta)
        df = pf.astype(jnp.float32) * (mm(g, values[pl.ds(far_at, BLK)], NT) - delta)
        dw, df = dw.astype(jnp.bfloat16), df.astype(jnp.bfloat16)
        dq = mm(dw, keys[pl.ds(at, SPAN)]) + mm(df, keys[pl.ds(far_at, BLK)])
        out[b, 0] = (dq * scale).astype(jnp.bfloat16)
        qt, gt = jnp.transpose(q), jnp.transpose(g)
        key_acc[:, pl.ds(at, SPAN)] += mm(qt, dw)
        value_acc[:, pl.ds(at, SPAN)] += mm(gt, pw)
        key_acc[:, pl.ds(far_at, BLK)] += mm(qt, df)
        value_acc[:, pl.ds(far_at, BLK)] += mm(gt, pf)

    @pl.when(i == pl.num_programs(0) - 1)
    def _():
        for b in range(blocks):
            cols = slice((HALO + b) * BLK, (HALO + b + 1) * BLK)
            out[b, 1] = jnp.transpose(key_acc[:, cols] * scale).astype(jnp.bfloat16)
            out[b, 2] = jnp.transpose(value_acc[:, cols]).astype(jnp.bfloat16)


def backward(info, x, g, o, probs, group=2):
    blocks, count, _, width = x.shape
    padded = (blocks + 2 * HALO) * BLK
    return pl.pallas_call(
        functools.partial(backward_kernel, blocks=blocks, group=group),
        grid=(blocks // group,),
        in_specs=[
            pl.BlockSpec(memory_space=pltpu.SMEM),
            pl.BlockSpec(x.shape, lambda i: (0, 0, 0, 0)),
            pl.BlockSpec(g.shape, lambda i: (0, 0, 0, 0)),
            pl.BlockSpec((group, 1, BLK, width), lambda i: (i, 0, 0, 0)),
            pl.BlockSpec((group, BLK, LINKED), lambda i: (i, 0, 0)),
        ],
        out_specs=pl.BlockSpec(x.shape, lambda i: (0, 0, 0, 0)),
        out_shape=jax.ShapeDtypeStruct(x.shape, jnp.bfloat16),
        scratch_shapes=[pltpu.VMEM((padded, width), jnp.bfloat16)] * 2
        + [pltpu.VMEM((width, padded), jnp.float32)] * 2,
        cost_estimate=pl.CostEstimate(
            flops=blocks * 8 * BLK * LINKED * width,
            transcendentals=0,
            bytes_accessed=2 * (2 * x.size + 2 * g.size + probs.size),
        ),
    )(info, x, g, o, probs)


def partner(value, axis, apart):
    return lax.ppermute(value, axis, [(i, i ^ 1 << apart) for i in range(lax.axis_size(axis))])


def passed_along(value, axis, by):
    peers = lax.axis_size(axis)
    pairs = [(i, i + by) for i in range(peers) if 0 <= i + by < peers]
    return lax.ppermute(value, axis, pairs)


def to_slots(values, picker):
    return jnp.sum(jnp.where(picker[None, :, :, None], values[:, None, :, :], 0.0), axis=2)


def slots_to_heads(values, picker, filler):
    covered = jnp.any(picker, axis=0)
    summed = jnp.sum(jnp.where(picker[None, :, :, None], values[:, :, None, :], 0.0), axis=1)
    return jnp.where(covered[None, :, None], summed, filler)


def rows_slots_to_heads(values, picker):
    return jnp.einsum(
        "jqid,ih->jqhd", values, picker.astype(jnp.float32), precision=lax.Precision.HIGHEST
    )


def pick_heads(values, picker):
    chooser = picker.astype(jnp.bfloat16)
    return jnp.einsum("ih,jqhd->jqid", chooser, values, preferred_element_type=jnp.float32).astype(
        jnp.bfloat16
    )


def partner_route(values, section_index, low_bits):
    return partner(values, "seq", section_index - low_bits)


def partner_back(values, section_index, low_bits):
    return partner(values, "seq", section_index - low_bits)


def extend_blocks(values, reach, halo_blocks, blocks_dev, mover):
    pieces = [mover(values, distance) for distance in range(reach, 0, -1)]
    pieces = pieces + [values] + [mover(values, -distance) for distance in range(1, reach + 1)]
    start = reach * blocks_dev - halo_blocks
    whole = jnp.concatenate(pieces, axis=1)
    return whole


def move_keys(values, distance):
    return passed_along(values, "seq", distance)


def window_sets(extended, blocks_dev, spread):
    return jnp.stack(
        [extended[:, offset : offset + blocks_dev] for offset in range(spread)], axis=2
    )


def per_device(query_rows, key_rows, value_rows, out_grad, window_blocks, section_heads):
    tokens_dev, head_count, head_width = query_rows.shape
    blocks_dev = tokens_dev // BLK
    low_bits = blocks_dev.bit_length() - 1
    seq_count = lax.axis_size("seq")
    section_total = low_bits + seq_count.bit_length() - 1
    halo_blocks = WB - 1
    reach = (halo_blocks + blocks_dev - 1) // blocks_dev
    padding = reach * blocks_dev
    spread = 2 * WB - 1
    score_scale = 1.0 / math.sqrt(head_width)
    first_block = lax.axis_index("seq") * blocks_dev + jnp.arange(blocks_dev, dtype=jnp.int32)
    all_blocks = blocks_dev * seq_count
    query_blocks = query_rows.reshape(blocks_dev, BLK, head_count, head_width)
    key_blocks = key_rows.reshape(blocks_dev, BLK, head_count, head_width)
    value_blocks = value_rows.reshape(blocks_dev, BLK, head_count, head_width)
    grad_blocks = out_grad.reshape(blocks_dev, BLK, head_count, head_width)
    offsets = jnp.arange(spread, dtype=jnp.int32) - halo_blocks
    near_block = first_block[:, None] + offsets[None, :]
    in_range = (near_block >= 0) & (near_block < all_blocks)
    near_mask = in_range[:, None, :] & (
        jnp.abs(offsets)[None, None, :] < window_blocks[None, :, None]
    )
    wide_mask = near_mask[:, :, None, :, None]
    head_ids = jnp.arange(head_count, dtype=jnp.int32)
    paired = jnp.stack([key_blocks, value_blocks])
    extended = extend_blocks(paired, reach, halo_blocks, blocks_dev, move_keys)
    near_sets = window_sets(extended, blocks_dev, spread)
    near_keys = near_sets[0]
    near_values = near_sets[1]
    near_scores = (
        jnp.einsum("jqhd,jckhd->jhqck", query_blocks, near_keys, preferred_element_type=jnp.float32)
        * score_scale
    )
    near_scores = jnp.where(wide_mask, near_scores, blocked_score)
    top_score = jnp.max(near_scores, axis=(3, 4))
    records = []
    for section_index in range(section_total):
        picker = section_heads[section_index][:, None] == head_ids[None, :]
        slot_width = jnp.sum(jnp.where(picker, window_blocks[None, :], 0), axis=1)
        slot_valid = 2**section_index >= slot_width
        chosen_query = pick_heads(query_blocks, picker)
        chosen_grad = pick_heads(grad_blocks, picker)
        chosen_pair = jnp.stack([pick_heads(key_blocks, picker), pick_heads(value_blocks, picker)])
        partner_pair = partner_route(chosen_pair, section_index, low_bits)
        far_scores = (
            jnp.einsum(
                "jqid,jkid->jiqk", chosen_query, partner_pair[0], preferred_element_type=jnp.float32
            )
            * score_scale
        )
        far_scores = jnp.where(slot_valid[None, :, None, None], far_scores, blocked_score)
        top_score = jnp.maximum(
            top_score, slots_to_heads(jnp.max(far_scores, axis=3), picker, blocked_score)
        )
        records.append(
            (
                section_index,
                picker,
                slot_valid,
                chosen_query,
                chosen_grad,
                chosen_pair,
                partner_pair,
                far_scores,
            )
        )
    row_total = jnp.sum(
        jnp.where(wide_mask, jnp.exp(near_scores - top_score[:, :, :, None, None]), 0.0),
        axis=(3, 4),
    )
    for record in records:
        picker = record[1]
        slot_top = to_slots(top_score, picker)
        far_sum = jnp.sum(
            jnp.where(
                record[2][None, :, None, None], jnp.exp(record[7] - slot_top[:, :, :, None]), 0.0
            ),
            axis=3,
        )
        row_total = row_total + slots_to_heads(far_sum, picker, 0.0)
    log_total = top_score + jnp.log(row_total)
    near_probs = jnp.where(
        wide_mask, jnp.exp(near_scores - log_total[:, :, :, None, None]), 0.0
    ).astype(jnp.bfloat16)
    attended_sum = jnp.einsum(
        "jhqck,jckhd->jqhd", near_probs, near_values, preferred_element_type=jnp.float32
    )
    far_probs_list = []
    for record in records:
        picker = record[1]
        slot_lse = to_slots(log_total, picker)
        far_probs = jnp.where(
            record[2][None, :, None, None], jnp.exp(record[7] - slot_lse[:, :, :, None]), 0.0
        ).astype(jnp.bfloat16)
        far_probs_list.append((far_probs, slot_lse))
        attended_sum = attended_sum + rows_slots_to_heads(
            jnp.einsum(
                "jiqk,jkid->jqid", far_probs, record[6][1], preferred_element_type=jnp.float32
            ),
            picker,
        )
    attended = attended_sum.astype(jnp.bfloat16)
    row_delta = jnp.transpose(
        jnp.sum(grad_blocks.astype(jnp.float32) * attended.astype(jnp.float32), axis=-1), (0, 2, 1)
    )
    near_dprob = jnp.einsum(
        "jqhd,jckhd->jhqck", grad_blocks, near_values, preferred_element_type=jnp.float32
    )
    near_dscore = (
        near_probs.astype(jnp.float32) * (near_dprob - row_delta[:, :, :, None, None])
    ).astype(jnp.bfloat16)
    query_sum = jnp.einsum(
        "jhqck,jckhd->jqhd", near_dscore, near_keys, preferred_element_type=jnp.float32
    )
    far_dscores = []
    for record, probs_pair in zip(records, far_probs_list):
        picker = record[1]
        slot_delta = to_slots(row_delta, picker)
        far_dprob = jnp.einsum(
            "jqid,jkid->jiqk", record[4], record[6][1], preferred_element_type=jnp.float32
        )
        far_dscore = (
            probs_pair[0].astype(jnp.float32) * (far_dprob - slot_delta[:, :, :, None])
        ).astype(jnp.bfloat16)
        far_dscores.append((far_dscore, slot_delta))
        query_sum = query_sum + rows_slots_to_heads(
            jnp.einsum(
                "jiqk,jkid->jqid", far_dscore, record[6][0], preferred_element_type=jnp.float32
            ),
            picker,
        )
    query_grad = (
        (query_sum * score_scale).astype(jnp.bfloat16).reshape(tokens_dev, head_count, head_width)
    )
    near_key_part = (
        jnp.einsum(
            "jhqck,jqhd->jckhd", near_dscore, query_blocks, preferred_element_type=jnp.float32
        )
        * score_scale
    )
    near_value_part = jnp.einsum(
        "jhqck,jqhd->jckhd", near_probs, grad_blocks, preferred_element_type=jnp.float32
    )
    stacked_parts = jnp.stack([near_key_part, near_value_part])
    extended_count = blocks_dev + 2 * padding
    base = padding - halo_blocks
    extended_ids = jnp.arange(extended_count, dtype=jnp.int32)
    own_ids = jnp.arange(blocks_dev, dtype=jnp.int32)
    spread_ids = jnp.arange(spread, dtype=jnp.int32)
    placer = (
        extended_ids[:, None, None] == base + own_ids[None, :, None] + spread_ids[None, None, :]
    ).astype(jnp.float32)
    gathered = jnp.einsum(
        "ejc,xjckhd->xekhd", placer, stacked_parts, precision=lax.Precision.HIGHEST
    )
    own_grads = gathered[:, padding : padding + blocks_dev]
    for distance in range(1, reach + 1):
        lower_slab = gathered[
            :, padding - distance * blocks_dev : padding - (distance - 1) * blocks_dev
        ]
        own_grads = own_grads + passed_along(
            lower_slab.astype(jnp.bfloat16), "seq", -distance
        ).astype(lower_slab.dtype)
        upper_start = padding + blocks_dev + (distance - 1) * blocks_dev
        upper_slab = gathered[:, upper_start : upper_start + blocks_dev]
        own_grads = own_grads + passed_along(
            upper_slab.astype(jnp.bfloat16), "seq", distance
        ).astype(upper_slab.dtype)
    for record, probs_pair, dscore_pair in zip(records, far_probs_list, far_dscores):
        picker = record[1]
        key_part = (
            jnp.einsum(
                "jiqk,jqid->jkid", dscore_pair[0], record[3], preferred_element_type=jnp.float32
            )
            * score_scale
        )
        value_part = jnp.einsum(
            "jiqk,jqid->jkid", probs_pair[0], record[4], preferred_element_type=jnp.float32
        )
        returned = partner_back(jnp.stack([key_part, value_part]), record[0], low_bits)
        own_grads = own_grads + jnp.stack(
            [rows_slots_to_heads(returned[0], picker), rows_slots_to_heads(returned[1], picker)]
        )
    key_grad = own_grads[0].astype(jnp.bfloat16).reshape(tokens_dev, head_count, head_width)
    value_grad = own_grads[1].astype(jnp.bfloat16).reshape(tokens_dev, head_count, head_width)
    return (attended.reshape(tokens_dev, head_count, head_width), query_grad, key_grad, value_grad)


def to_heads(packed):
    return lax.all_to_all(packed, "seq", 0, 0, tiled=True)


def sharded_by_head(query_rows, key_rows, value_rows, out_grad, window_blocks, section_heads):
    head = lax.axis_index("seq")
    sections = section_heads.shape[0]
    span = 2 ** jnp.arange(sections, dtype=jnp.int32)
    used = jnp.any(section_heads == head, axis=1)
    width = jnp.sum(jnp.where(jnp.arange(window_blocks.shape[0]) == head, window_blocks, 0))
    bit = jnp.sum(jnp.where(used, span, 0))
    valid = (bit >= width).astype(jnp.int32)
    info = jnp.stack([width, valid, bit]).astype(jnp.int32)
    x = to_heads(pack([query_rows, key_rows, value_rows]))
    x, g_sent = lax.optimization_barrier((x, pack([out_grad])))
    g = to_heads(g_sent)
    o, probs = forward(info, x)
    o_back = to_heads(o)
    grads = backward(info, x, g, o, probs)
    grads, o_back = lax.optimization_barrier((grads, o_back))
    grads_back = to_heads(grads)
    return (*unpack(o_back), *unpack(grads_back))


def solution(mesh):
    spec = P(("grp", "seq"), None, None)
    peers = mesh.shape["seq"]

    def per_device_any(*args):
        tokens, heads, width = args[0].shape
        sections, listed = args[5].shape
        once = sections * listed == heads
        if tokens == BLK and heads == peers and once and 1 << sections == peers:
            return sharded_by_head(*args)
        return per_device(*args)

    return jax.shard_map(
        per_device_any,
        mesh=mesh,
        in_specs=(spec, spec, spec, spec, P(), P()),
        out_specs=(spec,) * 4,
        check_vma=False,
    )
```

```python
import functools
import math

import jax
import jax.numpy as jnp
from jax import lax
from jax.experimental import pallas as pl
from jax.experimental.pallas import tpu as pltpu
from jax.sharding import PartitionSpec as P

BLK = 128
WB = 3
HALO = WB - 1
SPAN = (2 * HALO + 1) * BLK
LINKED = SPAN + BLK
NT = (((1,), (1,)), ((), ()))
NN = (((1,), (0,)), ((), ()))
blocked_score = -1e30


def mm(a, b, dims=NN):
    return lax.dot_general(a, b, dims, preferred_element_type=jnp.float32)


def moved_cost(arrays):
    return pl.CostEstimate(
        flops=0, transcendentals=0, bytes_accessed=4 * sum(a.size for a in arrays)
    )


def pack_kernel(*refs):
    out = refs[-1]
    for i, ref in enumerate(refs[:-1]):
        out[:, i] = jnp.transpose(ref[...], (1, 0, 2))


def pack(arrays):
    tokens, heads, width = arrays[0].shape
    chunk = 64
    count = len(arrays)
    return pl.pallas_call(
        pack_kernel,
        grid=(tokens // chunk,),
        in_specs=[pl.BlockSpec((chunk, heads, width), lambda i: (i, 0, 0))] * count,
        out_specs=pl.BlockSpec((heads, count, chunk, width), lambda i: (0, 0, i, 0)),
        out_shape=jax.ShapeDtypeStruct((heads, count, tokens, width), jnp.bfloat16),
        cost_estimate=moved_cost(arrays),
    )(*arrays)


def unpack_kernel(src, *outs):
    for i, out in enumerate(outs):
        out[...] = jnp.transpose(src[:, i], (1, 0, 2))


def unpack(stacked):
    heads, count, tokens, width = stacked.shape
    chunk = 64
    return pl.pallas_call(
        unpack_kernel,
        grid=(tokens // chunk,),
        in_specs=[pl.BlockSpec((heads, count, chunk, width), lambda i: (0, 0, i, 0))],
        out_specs=[pl.BlockSpec((chunk, heads, width), lambda i: (i, 0, 0))] * count,
        out_shape=[jax.ShapeDtypeStruct((tokens, heads, width), jnp.bfloat16)] * count,
        cost_estimate=moved_cost([stacked]),
    )(stacked)


def softmax_pair(score, far_score, biases, far_bias, scale2):
    near_parts, far_parts = [], []
    gap = jnp.zeros((BLK, BLK), jnp.bfloat16)
    for r in range(2):
        rows = slice(r * BLK, (r + 1) * BLK)
        sw = score[rows, r * BLK : r * BLK + SPAN] * scale2 + biases[r]
        sf = far_score[r] * scale2 + far_bias
        top = jnp.maximum(jnp.max(sw, axis=1, keepdims=True), jnp.max(sf, axis=1, keepdims=True))
        ew, ef = jnp.exp2(sw - top), jnp.exp2(sf - top)
        total = jnp.sum(ew, axis=1, keepdims=True) + jnp.sum(ef, axis=1, keepdims=True)
        inverse = 1.0 / total
        near = (ew * inverse).astype(jnp.bfloat16)
        near_parts.append(jnp.concatenate([near, gap] if r == 0 else [gap, near], axis=1))
        far_parts.append((ef * inverse).astype(jnp.bfloat16))
    return jnp.concatenate(near_parts, axis=0), far_parts


def attend_pair(q, g, kw, vw, kf, vf, biases, far_bias):
    scale = 1.0 / math.sqrt(q.shape[-1])
    scale2 = scale * math.log2(math.e)
    half = [slice(0, BLK), slice(BLK, 2 * BLK)]
    far_score = [mm(q[half[r]], kf[r], NT) for r in range(2)]
    near, far = softmax_pair(mm(q, kw, NT), far_score, biases, far_bias, scale2)
    far_out = jnp.concatenate([mm(far[r], vf[r]) for r in range(2)], axis=0)
    attended = (mm(near, vw) + far_out).astype(jnp.bfloat16)
    delta = jnp.sum(g.astype(jnp.float32) * attended.astype(jnp.float32), axis=1, keepdims=True)
    d_near = (near.astype(jnp.float32) * (mm(g, vw, NT) - delta)).astype(jnp.bfloat16)
    d_far = [
        (far[r].astype(jnp.float32) * (mm(g[half[r]], vf[r], NT) - delta[half[r]])).astype(
            jnp.bfloat16
        )
        for r in range(2)
    ]
    far_dq = jnp.concatenate([mm(d_far[r], kf[r]) for r in range(2)], axis=0)
    query_grad = ((mm(d_near, kw) + far_dq) * scale).astype(jnp.bfloat16)
    qt, gt = jnp.transpose(q), jnp.transpose(g)
    key_near, value_near = mm(qt, d_near), mm(gt, near)
    key_far = [mm(qt[:, half[r]], d_far[r]) for r in range(2)]
    value_far = [mm(gt[:, half[r]], far[r]) for r in range(2)]
    return attended, query_grad, key_near, value_near, key_far, value_far


def near_biases(b, width, low, high):
    offset = lax.broadcasted_iota(jnp.int32, (1, SPAN), 1) // BLK - HALO
    inside = jnp.abs(offset) < width
    out = []
    for r in range(2):
        there = offset + b + r
        out.append(jnp.where(inside & (there >= low) & (there < high), 0.0, blocked_score))
    return out


def attend_kernel(
    head_ref, widths, sections, x, out, keys, values, key_acc, value_acc, *, blocks, unroll
):
    head = head_ref[0]
    width = widths[head]
    far_bit = jnp.int32(0)
    for s in range(sections.shape[0]):
        for i in range(sections.shape[1]):
            far_bit = jnp.where(sections[s, i] == head, 1 << s, far_bit)
    far_bias = jnp.where(far_bit >= width, 0.0, blocked_score).astype(jnp.float32)
    scale = 1.0 / math.sqrt(x.shape[-1])
    zero = jnp.zeros((HALO * BLK, x.shape[-1]), jnp.bfloat16)
    for ref, part in ((keys, 1), (values, 2)):
        ref[: HALO * BLK] = zero
        ref[(HALO + blocks) * BLK :] = zero
        for b in range(blocks):
            ref[(HALO + b) * BLK : (HALO + b + 1) * BLK] = x[b, part]
    key_acc[...] = jnp.zeros_like(key_acc)
    value_acc[...] = jnp.zeros_like(value_acc)
    pair_span = SPAN + BLK

    def one(b):
        q = jnp.concatenate([x[b, 0], x[b + 1, 0]], axis=0)
        g = jnp.concatenate([x[b, 3], x[b + 1, 3]], axis=0)
        at = pl.multiple_of(b * BLK, BLK)
        far_at = [pl.multiple_of((HALO + ((b + r) ^ far_bit)) * BLK, BLK) for r in range(2)]
        attended, dq, key_near, value_near, key_far, value_far = attend_pair(
            q,
            g,
            keys[pl.ds(at, pair_span)],
            values[pl.ds(at, pair_span)],
            [keys[pl.ds(far_at[r], BLK)] for r in range(2)],
            [values[pl.ds(far_at[r], BLK)] for r in range(2)],
            near_biases(b, width, 0, blocks),
            far_bias,
        )
        for r in range(2):
            rows = slice(r * BLK, (r + 1) * BLK)
            out[b + r, 0] = attended[rows]
            out[b + r, 1] = dq[rows]
        key_acc[:, pl.ds(at, pair_span)] += key_near
        value_acc[:, pl.ds(at, pair_span)] += value_near
        for r in range(2):
            key_acc[:, pl.ds(far_at[r], BLK)] += key_far[r]
            value_acc[:, pl.ds(far_at[r], BLK)] += value_far[r]

    def step(i, carry):
        for u in range(unroll):
            one((i * unroll + u) * 2)
        return carry

    lax.fori_loop(0, blocks // (2 * unroll), step, 0)
    for b in range(blocks):
        cols = slice((HALO + b) * BLK, (HALO + b + 1) * BLK)
        out[b, 2] = jnp.transpose((key_acc[:, cols] * scale).astype(jnp.bfloat16))
        out[b, 3] = jnp.transpose(value_acc[:, cols].astype(jnp.bfloat16))


def attend(head, window_blocks, section_heads, x, unroll=2):
    blocks, _, _, width = x.shape
    padded = (blocks + 2 * HALO) * BLK
    return pl.pallas_call(
        functools.partial(attend_kernel, blocks=blocks, unroll=unroll),
        in_specs=[pl.BlockSpec(memory_space=pltpu.SMEM)] * 3
        + [pl.BlockSpec(memory_space=pltpu.VMEM)],
        out_specs=pl.BlockSpec(memory_space=pltpu.VMEM),
        out_shape=jax.ShapeDtypeStruct(x.shape, jnp.bfloat16),
        scratch_shapes=[pltpu.VMEM((padded, width), jnp.bfloat16)] * 2
        + [pltpu.VMEM((width, padded), jnp.float32)] * 2,
        compiler_params=pltpu.CompilerParams(vmem_limit_bytes=24 << 20),
        cost_estimate=pl.CostEstimate(
            flops=blocks * 12 * BLK * LINKED * width,
            transcendentals=blocks * BLK * LINKED,
            bytes_accessed=4 * x.size,
        ),
    )(head, window_blocks, section_heads, x)


def partner(value, axis, apart):
    return lax.ppermute(value, axis, [(i, i ^ 1 << apart) for i in range(lax.axis_size(axis))])


def passed_along(value, axis, by):
    peers = lax.axis_size(axis)
    pairs = [(i, i + by) for i in range(peers) if 0 <= i + by < peers]
    return lax.ppermute(value, axis, pairs)


def to_slots(values, picker):
    return jnp.sum(jnp.where(picker[None, :, :, None], values[:, None, :, :], 0.0), axis=2)


def slots_to_heads(values, picker, filler):
    covered = jnp.any(picker, axis=0)
    summed = jnp.sum(jnp.where(picker[None, :, :, None], values[:, :, None, :], 0.0), axis=1)
    return jnp.where(covered[None, :, None], summed, filler)


def rows_slots_to_heads(values, picker):
    return jnp.einsum(
        "jqid,ih->jqhd", values, picker.astype(jnp.float32), precision=lax.Precision.HIGHEST
    )


def pick_heads(values, picker):
    chooser = picker.astype(jnp.bfloat16)
    return jnp.einsum("ih,jqhd->jqid", chooser, values, preferred_element_type=jnp.float32).astype(
        jnp.bfloat16
    )


def partner_route(values, section_index, low_bits):
    return partner(values, "seq", section_index - low_bits)


def partner_back(values, section_index, low_bits):
    return partner(values, "seq", section_index - low_bits)


def extend_blocks(values, reach, halo_blocks, blocks_dev, mover):
    pieces = [mover(values, distance) for distance in range(reach, 0, -1)]
    pieces = pieces + [values] + [mover(values, -distance) for distance in range(1, reach + 1)]
    start = reach * blocks_dev - halo_blocks
    whole = jnp.concatenate(pieces, axis=1)
    return whole


def move_keys(values, distance):
    return passed_along(values, "seq", distance)


def window_sets(extended, blocks_dev, spread):
    return jnp.stack(
        [extended[:, offset : offset + blocks_dev] for offset in range(spread)], axis=2
    )


def per_device(query_rows, key_rows, value_rows, out_grad, window_blocks, section_heads):
    tokens_dev, head_count, head_width = query_rows.shape
    blocks_dev = tokens_dev // BLK
    low_bits = blocks_dev.bit_length() - 1
    seq_count = lax.axis_size("seq")
    section_total = low_bits + seq_count.bit_length() - 1
    halo_blocks = WB - 1
    reach = (halo_blocks + blocks_dev - 1) // blocks_dev
    padding = reach * blocks_dev
    spread = 2 * WB - 1
    score_scale = 1.0 / math.sqrt(head_width)
    first_block = lax.axis_index("seq") * blocks_dev + jnp.arange(blocks_dev, dtype=jnp.int32)
    all_blocks = blocks_dev * seq_count
    query_blocks = query_rows.reshape(blocks_dev, BLK, head_count, head_width)
    key_blocks = key_rows.reshape(blocks_dev, BLK, head_count, head_width)
    value_blocks = value_rows.reshape(blocks_dev, BLK, head_count, head_width)
    grad_blocks = out_grad.reshape(blocks_dev, BLK, head_count, head_width)
    offsets = jnp.arange(spread, dtype=jnp.int32) - halo_blocks
    near_block = first_block[:, None] + offsets[None, :]
    in_range = (near_block >= 0) & (near_block < all_blocks)
    near_mask = in_range[:, None, :] & (
        jnp.abs(offsets)[None, None, :] < window_blocks[None, :, None]
    )
    wide_mask = near_mask[:, :, None, :, None]
    head_ids = jnp.arange(head_count, dtype=jnp.int32)
    paired = jnp.stack([key_blocks, value_blocks])
    extended = extend_blocks(paired, reach, halo_blocks, blocks_dev, move_keys)
    near_sets = window_sets(extended, blocks_dev, spread)
    near_keys = near_sets[0]
    near_values = near_sets[1]
    near_scores = (
        jnp.einsum("jqhd,jckhd->jhqck", query_blocks, near_keys, preferred_element_type=jnp.float32)
        * score_scale
    )
    near_scores = jnp.where(wide_mask, near_scores, blocked_score)
    top_score = jnp.max(near_scores, axis=(3, 4))
    records = []
    for section_index in range(section_total):
        picker = section_heads[section_index][:, None] == head_ids[None, :]
        slot_width = jnp.sum(jnp.where(picker, window_blocks[None, :], 0), axis=1)
        slot_valid = 2**section_index >= slot_width
        chosen_query = pick_heads(query_blocks, picker)
        chosen_grad = pick_heads(grad_blocks, picker)
        chosen_pair = jnp.stack([pick_heads(key_blocks, picker), pick_heads(value_blocks, picker)])
        partner_pair = partner_route(chosen_pair, section_index, low_bits)
        far_scores = (
            jnp.einsum(
                "jqid,jkid->jiqk", chosen_query, partner_pair[0], preferred_element_type=jnp.float32
            )
            * score_scale
        )
        far_scores = jnp.where(slot_valid[None, :, None, None], far_scores, blocked_score)
        top_score = jnp.maximum(
            top_score, slots_to_heads(jnp.max(far_scores, axis=3), picker, blocked_score)
        )
        records.append(
            (
                section_index,
                picker,
                slot_valid,
                chosen_query,
                chosen_grad,
                chosen_pair,
                partner_pair,
                far_scores,
            )
        )
    row_total = jnp.sum(
        jnp.where(wide_mask, jnp.exp(near_scores - top_score[:, :, :, None, None]), 0.0),
        axis=(3, 4),
    )
    for record in records:
        picker = record[1]
        slot_top = to_slots(top_score, picker)
        far_sum = jnp.sum(
            jnp.where(
                record[2][None, :, None, None], jnp.exp(record[7] - slot_top[:, :, :, None]), 0.0
            ),
            axis=3,
        )
        row_total = row_total + slots_to_heads(far_sum, picker, 0.0)
    log_total = top_score + jnp.log(row_total)
    near_probs = jnp.where(
        wide_mask, jnp.exp(near_scores - log_total[:, :, :, None, None]), 0.0
    ).astype(jnp.bfloat16)
    attended_sum = jnp.einsum(
        "jhqck,jckhd->jqhd", near_probs, near_values, preferred_element_type=jnp.float32
    )
    far_probs_list = []
    for record in records:
        picker = record[1]
        slot_lse = to_slots(log_total, picker)
        far_probs = jnp.where(
            record[2][None, :, None, None], jnp.exp(record[7] - slot_lse[:, :, :, None]), 0.0
        ).astype(jnp.bfloat16)
        far_probs_list.append((far_probs, slot_lse))
        attended_sum = attended_sum + rows_slots_to_heads(
            jnp.einsum(
                "jiqk,jkid->jqid", far_probs, record[6][1], preferred_element_type=jnp.float32
            ),
            picker,
        )
    attended = attended_sum.astype(jnp.bfloat16)
    row_delta = jnp.transpose(
        jnp.sum(grad_blocks.astype(jnp.float32) * attended.astype(jnp.float32), axis=-1), (0, 2, 1)
    )
    near_dprob = jnp.einsum(
        "jqhd,jckhd->jhqck", grad_blocks, near_values, preferred_element_type=jnp.float32
    )
    near_dscore = (
        near_probs.astype(jnp.float32) * (near_dprob - row_delta[:, :, :, None, None])
    ).astype(jnp.bfloat16)
    query_sum = jnp.einsum(
        "jhqck,jckhd->jqhd", near_dscore, near_keys, preferred_element_type=jnp.float32
    )
    far_dscores = []
    for record, probs_pair in zip(records, far_probs_list):
        picker = record[1]
        slot_delta = to_slots(row_delta, picker)
        far_dprob = jnp.einsum(
            "jqid,jkid->jiqk", record[4], record[6][1], preferred_element_type=jnp.float32
        )
        far_dscore = (
            probs_pair[0].astype(jnp.float32) * (far_dprob - slot_delta[:, :, :, None])
        ).astype(jnp.bfloat16)
        far_dscores.append((far_dscore, slot_delta))
        query_sum = query_sum + rows_slots_to_heads(
            jnp.einsum(
                "jiqk,jkid->jqid", far_dscore, record[6][0], preferred_element_type=jnp.float32
            ),
            picker,
        )
    query_grad = (
        (query_sum * score_scale).astype(jnp.bfloat16).reshape(tokens_dev, head_count, head_width)
    )
    near_key_part = (
        jnp.einsum(
            "jhqck,jqhd->jckhd", near_dscore, query_blocks, preferred_element_type=jnp.float32
        )
        * score_scale
    )
    near_value_part = jnp.einsum(
        "jhqck,jqhd->jckhd", near_probs, grad_blocks, preferred_element_type=jnp.float32
    )
    stacked_parts = jnp.stack([near_key_part, near_value_part])
    extended_count = blocks_dev + 2 * padding
    base = padding - halo_blocks
    extended_ids = jnp.arange(extended_count, dtype=jnp.int32)
    own_ids = jnp.arange(blocks_dev, dtype=jnp.int32)
    spread_ids = jnp.arange(spread, dtype=jnp.int32)
    placer = (
        extended_ids[:, None, None] == base + own_ids[None, :, None] + spread_ids[None, None, :]
    ).astype(jnp.float32)
    gathered = jnp.einsum(
        "ejc,xjckhd->xekhd", placer, stacked_parts, precision=lax.Precision.HIGHEST
    )
    own_grads = gathered[:, padding : padding + blocks_dev]
    for distance in range(1, reach + 1):
        lower_slab = gathered[
            :, padding - distance * blocks_dev : padding - (distance - 1) * blocks_dev
        ]
        own_grads = own_grads + passed_along(
            lower_slab.astype(jnp.bfloat16), "seq", -distance
        ).astype(lower_slab.dtype)
        upper_start = padding + blocks_dev + (distance - 1) * blocks_dev
        upper_slab = gathered[:, upper_start : upper_start + blocks_dev]
        own_grads = own_grads + passed_along(
            upper_slab.astype(jnp.bfloat16), "seq", distance
        ).astype(upper_slab.dtype)
    for record, probs_pair, dscore_pair in zip(records, far_probs_list, far_dscores):
        picker = record[1]
        key_part = (
            jnp.einsum(
                "jiqk,jqid->jkid", dscore_pair[0], record[3], preferred_element_type=jnp.float32
            )
            * score_scale
        )
        value_part = jnp.einsum(
            "jiqk,jqid->jkid", probs_pair[0], record[4], preferred_element_type=jnp.float32
        )
        returned = partner_back(jnp.stack([key_part, value_part]), record[0], low_bits)
        own_grads = own_grads + jnp.stack(
            [rows_slots_to_heads(returned[0], picker), rows_slots_to_heads(returned[1], picker)]
        )
    key_grad = own_grads[0].astype(jnp.bfloat16).reshape(tokens_dev, head_count, head_width)
    value_grad = own_grads[1].astype(jnp.bfloat16).reshape(tokens_dev, head_count, head_width)
    return (attended.reshape(tokens_dev, head_count, head_width), query_grad, key_grad, value_grad)


def sharded_by_head(query_rows, key_rows, value_rows, out_grad, window_blocks, section_heads):
    head = lax.axis_index("seq").astype(jnp.int32).reshape(1)
    sent = pack([query_rows, key_rows, value_rows, out_grad])
    x = lax.all_to_all(sent, "seq", 0, 0, tiled=True)
    grads = attend(head, window_blocks, section_heads, x)
    return tuple(unpack(lax.all_to_all(grads, "seq", 0, 0, tiled=True)))


def solution(mesh):
    spec = P(("grp", "seq"), None, None)
    peers = mesh.shape["seq"]

    def per_device_any(*args):
        tokens, heads, width = args[0].shape
        sections, listed = args[5].shape
        once = sections * listed == heads
        if tokens == BLK and heads == peers and once and 1 << sections == peers:
            return sharded_by_head(*args)
        return per_device(*args)

    return jax.shard_map(
        per_device_any,
        mesh=mesh,
        in_specs=(spec, spec, spec, spec, P(), P()),
        out_specs=(spec,) * 4,
        check_vma=False,
    )
```

```python
import functools
import math

import jax
import jax.numpy as jnp
from jax import lax
from jax.experimental import pallas as pl
from jax.experimental.pallas import tpu as pltpu
from jax.sharding import PartitionSpec as P

BLK = 128
WB = 3
HALO = WB - 1
SPAN = (2 * HALO + 1) * BLK
LINKED = SPAN + BLK
PLANE = 2 * HALO
PADDED = PLANE + 2 * HALO
NT = (((1,), (1,)), ((), ()))
NN = (((1,), (0,)), ((), ()))
blocked_score = -1e30


def mm(a, b, dims=NN):
    return lax.dot_general(a, b, dims, preferred_element_type=jnp.float32)


def moved_cost(arrays):
    return pl.CostEstimate(
        flops=0, transcendentals=0, bytes_accessed=4 * sum(a.size for a in arrays)
    )


def softmax_pair(score, far_score, biases, far_bias, scale2):
    near_parts, far_parts = [], []
    gap = jnp.zeros((BLK, BLK), jnp.bfloat16)
    for r in range(2):
        rows = slice(r * BLK, (r + 1) * BLK)
        sw = score[rows, r * BLK : r * BLK + SPAN] * scale2 + biases[r]
        sf = far_score[r] * scale2 + far_bias
        top = jnp.maximum(jnp.max(sw, axis=1, keepdims=True), jnp.max(sf, axis=1, keepdims=True))
        ew, ef = jnp.exp2(sw - top), jnp.exp2(sf - top)
        total = jnp.sum(ew, axis=1, keepdims=True) + jnp.sum(ef, axis=1, keepdims=True)
        inverse = 1.0 / total
        near = (ew * inverse).astype(jnp.bfloat16)
        near_parts.append(jnp.concatenate([near, gap] if r == 0 else [gap, near], axis=1))
        far_parts.append((ef * inverse).astype(jnp.bfloat16))
    return jnp.concatenate(near_parts, axis=0), far_parts


def attend_pair(q, g, kw, vw, kf, vf, biases, far_bias):
    scale = 1.0 / math.sqrt(q.shape[-1])
    scale2 = scale * math.log2(math.e)
    half = [slice(0, BLK), slice(BLK, 2 * BLK)]
    far_score = [mm(q[half[r]], kf[r], NT) for r in range(2)]
    near, far = softmax_pair(mm(q, kw, NT), far_score, biases, far_bias, scale2)
    far_out = jnp.concatenate([mm(far[r], vf[r]) for r in range(2)], axis=0)
    attended = (mm(near, vw) + far_out).astype(jnp.bfloat16)
    delta = jnp.sum(g.astype(jnp.float32) * attended.astype(jnp.float32), axis=1, keepdims=True)
    d_near = (near.astype(jnp.float32) * (mm(g, vw, NT) - delta)).astype(jnp.bfloat16)
    d_far = [
        (far[r].astype(jnp.float32) * (mm(g[half[r]], vf[r], NT) - delta[half[r]])).astype(
            jnp.bfloat16
        )
        for r in range(2)
    ]
    far_dq = jnp.concatenate([mm(d_far[r], kf[r]) for r in range(2)], axis=0)
    query_grad = ((mm(d_near, kw) + far_dq) * scale).astype(jnp.bfloat16)
    qt, gt = jnp.transpose(q), jnp.transpose(g)
    key_near, value_near = mm(qt, d_near), mm(gt, near)
    key_far = [mm(qt[:, half[r]], d_far[r]) for r in range(2)]
    value_far = [mm(gt[:, half[r]], far[r]) for r in range(2)]
    return attended, query_grad, key_near, value_near, key_far, value_far


def near_biases(b, width, low, high):
    offset = lax.broadcasted_iota(jnp.int32, (1, SPAN), 1) // BLK - HALO
    inside = jnp.abs(offset) < width
    out = []
    for r in range(2):
        there = offset + b + r
        out.append(jnp.where(inside & (there >= low) & (there < high), 0.0, blocked_score))
    return out


def rows_of(block):
    return pl.ds(pl.multiple_of(block * BLK, BLK), BLK)


def whole(shape):
    return pl.BlockSpec(shape, lambda *_: (0,) * len(shape))


SMEM = pl.BlockSpec(memory_space=pltpu.SMEM)
VMEM = pl.BlockSpec(memory_space=pltpu.VMEM)
LIMIT = pltpu.CompilerParams(vmem_limit_bytes=20 << 20)


def pack_kernel(place, sections, *refs, groups, count):
    ins, outs, held = refs[:count], refs[count:-1], refs[-1]
    for i in range(count):
        held[i] = jnp.transpose(ins[i][...], (1, 0, 2))
    for number, group in enumerate(groups):
        for m in range(PLANE):
            for k, s in enumerate(group):
                head = sections[s, place[0] ^ m]
                for i in range(count):
                    outs[number * PLANE + m][k, i] = held[i, head]


def pack(place, sections, arrays, groups):
    tokens, heads, width = arrays[0].shape
    chunk = tokens // 2
    count = len(arrays)
    shapes = [(len(group), count, tokens, width) for group in groups for _ in range(PLANE)]
    outs = pl.pallas_call(
        functools.partial(pack_kernel, groups=groups, count=count),
        grid=(tokens // chunk,),
        in_specs=[SMEM, SMEM]
        + [pl.BlockSpec((chunk, heads, width), lambda i: (i, 0, 0))] * count,
        out_specs=[
            pl.BlockSpec((*shape[:2], chunk, width), lambda i: (0, 0, i, 0)) for shape in shapes
        ],
        out_shape=[jax.ShapeDtypeStruct(shape, jnp.bfloat16) for shape in shapes],
        scratch_shapes=[pltpu.VMEM((count, heads, chunk, width), jnp.bfloat16)],
        compiler_params=LIMIT,
        cost_estimate=moved_cost(arrays),
    )(place, sections, *arrays)
    return [outs[i * PLANE : (i + 1) * PLANE] for i in range(len(groups))]


def unpack_kernel(place, sections, *refs, groups, count):
    pieces, outs, held = refs[: len(groups) * PLANE], refs[len(groups) * PLANE : -1], refs[-1]
    for number, group in enumerate(groups):
        for m in range(PLANE):
            for k, s in enumerate(group):
                head = sections[s, place[0] ^ m]
                for i in range(count):
                    held[i, head] = pieces[number * PLANE + m][k, i]
    for i in range(count):
        outs[i][...] = jnp.transpose(held[i], (1, 0, 2))


def unpack(place, sections, pieces, groups):
    flat = [piece for group in pieces for piece in group]
    _, count, tokens, width = flat[0].shape
    heads = sections.size
    chunk = tokens // 2
    return pl.pallas_call(
        functools.partial(unpack_kernel, groups=groups, count=count),
        grid=(tokens // chunk,),
        in_specs=[SMEM, SMEM]
        + [
            pl.BlockSpec((*piece.shape[:2], chunk, width), lambda i: (0, 0, i, 0))
            for piece in flat
        ],
        out_specs=[pl.BlockSpec((chunk, heads, width), lambda i: (i, 0, 0))] * count,
        out_shape=[jax.ShapeDtypeStruct((tokens, heads, width), jnp.bfloat16)] * count,
        scratch_shapes=[pltpu.VMEM((count, heads, chunk, width), jnp.bfloat16)],
        compiler_params=LIMIT,
        cost_estimate=moved_cost(flat),
    )(place, sections, *flat)


def far_kernel(*refs):
    pieces, outs = refs[:PLANE], refs[PLANE:]
    for k, out in enumerate(outs):
        for m, piece in enumerate(pieces):
            out[m] = piece[k]


def far_parts(pieces):
    group, *rest = pieces[0].shape
    return pl.pallas_call(
        far_kernel,
        in_specs=[VMEM] * PLANE,
        out_specs=[VMEM] * group,
        out_shape=[jax.ShapeDtypeStruct((PLANE, *rest), jnp.bfloat16)] * group,
        compiler_params=LIMIT,
        cost_estimate=moved_cost(pieces),
    )(*pieces)


def halo_kernel(place, *refs, groups):
    pieces, (up, down) = refs[:-2], refs[-2:]
    upper_chip = place[0] // HALO

    def fill(high, low):
        for m in range(HALO):
            slot = 0
            for number in range(groups):
                for k in range(pieces[number * PLANE].shape[0]):
                    up[m, slot] = pieces[number * PLANE + high + m][k]
                    down[m, slot] = pieces[number * PLANE + low + m][k]
                    slot += 1

    @pl.when(upper_chip == 1)
    def _():
        fill(0, HALO)

    @pl.when(upper_chip == 0)
    def _():
        fill(HALO, 0)


def halo_parts(place, pieces):
    flat = [piece for group in pieces for piece in group]
    slots = sum(group[0].shape[0] for group in pieces)
    shape = jax.ShapeDtypeStruct((HALO, slots, *flat[0].shape[1:]), jnp.bfloat16)
    return pl.pallas_call(
        functools.partial(halo_kernel, groups=len(pieces)),
        in_specs=[SMEM] + [VMEM] * len(flat),
        out_specs=[VMEM] * 2,
        out_shape=[shape] * 2,
        compiler_params=LIMIT,
        cost_estimate=moved_cost(flat),
    )(place, *flat)


def attend_kernel(place, widths, sections, *refs, first, remote, blocks):
    pairs, graded = refs[:PLANE], refs[PLANE : 2 * PLANE]
    below, above = refs[2 * PLANE : 2 * PLANE + 2]
    rest = refs[2 * PLANE + 2 :]
    far_in, rest = rest[:remote], rest[remote:]
    outs, rest = rest[:PLANE], rest[PLANE:]
    (part, to_below, to_above), rest = rest[:3], rest[3:]
    far_out, rest = rest[:remote], rest[remote:]
    keys, values, far_keys, far_values, queries, grads, attended, dq = rest[:8]
    accs, far_accs = rest[8:10], rest[10:12]
    k = pl.program_id(0)
    section = first + k
    me = place[0]
    width = widths[sections[section, me]]
    bit = jnp.left_shift(jnp.int32(1), section)
    far_bias = jnp.where(bit >= width, 0.0, blocked_score).astype(jnp.float32)
    scales = (1.0 / math.sqrt(keys.shape[-1]), 1.0)
    for m in range(PLANE):
        b = me ^ m
        keys[rows_of(HALO + b)] = pairs[m][0, 0]
        values[rows_of(HALO + b)] = pairs[m][0, 1]
        queries[rows_of(b)] = graded[m][0, 0]
        grads[rows_of(b)] = graded[m][0, 1]
    for m in range(HALO):
        b = (me % HALO) ^ m
        keys[rows_of(b)] = below[m, 0, 0]
        values[rows_of(b)] = below[m, 0, 1]
        keys[rows_of(HALO + PLANE + b)] = above[m, 0, 0]
        values[rows_of(HALO + PLANE + b)] = above[m, 0, 1]
    if remote:
        for n in range(remote):

            @pl.when(k == n)
            def _(n=n):
                for m in range(PLANE):
                    far_keys[rows_of(me ^ m)] = far_in[n][m, 0]
                    far_values[rows_of(me ^ m)] = far_in[n][m, 1]
    else:
        for b in range(PLANE):
            far_keys[rows_of(b)] = keys[rows_of(HALO + (b ^ bit))]
            far_values[rows_of(b)] = values[rows_of(HALO + (b ^ bit))]
    for acc in accs:
        acc[...] = jnp.zeros_like(acc)
    for b in range(0, PLANE, 2):
        own = slice(b * BLK, (b + 2) * BLK)
        seen = slice(b * BLK, (b + 2 * HALO + 2) * BLK)
        one = [slice((b + r) * BLK, (b + r + 1) * BLK) for r in range(2)]
        o, d, key_near, value_near, key_far, value_far = attend_pair(
            queries[own],
            grads[own],
            keys[seen],
            values[seen],
            [far_keys[one[r]] for r in range(2)],
            [far_values[one[r]] for r in range(2)],
            near_biases(place[1] * PLANE + b, width, 0, blocks),
            far_bias,
        )
        attended[own] = o
        dq[own] = d
        for acc, near in zip(accs, (key_near, value_near)):
            acc[:, seen] += near
        for acc, far in zip(far_accs, (key_far, value_far)):
            for r in range(2):
                acc[:, one[r]] = far[r]
    for i, (acc, far_acc) in enumerate(zip(accs, far_accs)):
        if not remote:
            for b in range(PLANE):
                acc[:, rows_of(HALO + (b ^ bit))] += far_acc[:, b * BLK : (b + 1) * BLK]
        for n in range(remote):

            @pl.when(k == n)
            def _(n=n, i=i, far_acc=far_acc):
                for m in range(PLANE):
                    far_out[n][m, i] = (far_acc[:, rows_of(me ^ m)] * scales[i]).astype(
                        jnp.bfloat16
                    )

        for m in range(PLANE):
            part[0, m, i] = acc[:, rows_of(HALO + (me ^ m))] * scales[i]
        for m in range(HALO):
            b = (me % HALO) ^ m
            to_below[m, 0, i] = (acc[:, rows_of(b)] * scales[i]).astype(jnp.bfloat16)
            to_above[m, 0, i] = (acc[:, rows_of(HALO + PLANE + b)] * scales[i]).astype(
                jnp.bfloat16
            )
    for m in range(PLANE):
        outs[m][0, 0] = attended[rows_of(me ^ m)]
        outs[m][0, 1] = dq[rows_of(me ^ m)]


def attend(place, widths, sections, pairs, graded, below, above, far, first, slot, blocks):
    group, count, _, width = pairs[0].shape
    tile = (BLK, width)
    remote = len(far)
    piece = pl.BlockSpec((1, count, *tile), lambda k: (k, 0, 0, 0))
    graded_piece = pl.BlockSpec((1, count, *tile), lambda k: (slot + k, 0, 0, 0))
    halo_in = pl.BlockSpec((HALO, 1, count, *tile), lambda k: (0, slot + k, 0, 0, 0))
    halo_out = pl.BlockSpec((HALO, 1, count, *tile), lambda k: (0, k, 0, 0, 0))
    far_spec = whole((PLANE, count, *tile))
    bf16 = jnp.bfloat16
    outs = pl.pallas_call(
        functools.partial(attend_kernel, first=first, remote=remote, blocks=blocks),
        grid=(group,),
        in_specs=[SMEM] * 3
        + [piece] * PLANE
        + [graded_piece] * PLANE
        + [halo_in] * 2
        + [far_spec] * remote,
        out_specs=[piece] * PLANE
        + [pl.BlockSpec((1, PLANE, count, *tile), lambda k: (k, 0, 0, 0, 0))]
        + [halo_out] * 2
        + [far_spec] * remote,
        out_shape=[jax.ShapeDtypeStruct((group, count, *tile), bf16)] * PLANE
        + [jax.ShapeDtypeStruct((group, PLANE, count, *tile), jnp.float32)]
        + [jax.ShapeDtypeStruct((HALO, group, count, *tile), bf16)] * 2
        + [jax.ShapeDtypeStruct((PLANE, count, *tile), bf16)] * remote,
        scratch_shapes=[pltpu.VMEM((PADDED * BLK, width), bf16)] * 2
        + [pltpu.VMEM((PLANE * BLK, width), bf16)] * 6
        + [pltpu.VMEM((width, PADDED * BLK), jnp.float32)] * 2
        + [pltpu.VMEM((width, PLANE * BLK), jnp.float32)] * 2,
        compiler_params=LIMIT,
        cost_estimate=pl.CostEstimate(
            flops=group * PLANE * 12 * BLK * LINKED * width,
            transcendentals=group * PLANE * BLK * LINKED,
            bytes_accessed=40 * group * PLANE * BLK * width,
        ),
    )(place, widths, sections, *pairs, *graded, below, above, *far)
    return outs[:PLANE], outs[PLANE], outs[PLANE + 1], outs[PLANE + 2], outs[PLANE + 3 :]


def combine_kernel(place, part, above, below, *refs, remote):
    far, outs = refs[:remote], refs[remote:]
    for m in range(PLANE):
        upper = (m // HALO) ^ (place[0] // HALO)
        for k in range(part.shape[0]):
            for i in range(part.shape[2]):
                owed = jnp.where(upper == 1, above[m % HALO, k, i], below[m % HALO, k, i])
                total = part[k, m, i] + owed.astype(jnp.float32)
                if remote:
                    total += far[k][m, i].astype(jnp.float32)
                outs[m][k, i] = jnp.transpose(total.astype(jnp.bfloat16))


def combine(place, part, above, below, far):
    group, _, *rest = part.shape
    return pl.pallas_call(
        functools.partial(combine_kernel, remote=len(far)),
        in_specs=[SMEM] + [VMEM] * (3 + len(far)),
        out_specs=[VMEM] * PLANE,
        out_shape=[jax.ShapeDtypeStruct((group, *rest), jnp.bfloat16)] * PLANE,
        compiler_params=LIMIT,
        cost_estimate=moved_cost([part, above, below, *far]),
    )(place, part, above, below, *far)


def partner(value, axis, apart):
    return lax.ppermute(value, axis, [(i, i ^ 1 << apart) for i in range(lax.axis_size(axis))])


def passed_along(value, axis, by):
    peers = lax.axis_size(axis)
    pairs = [(i, i + by) for i in range(peers) if 0 <= i + by < peers]
    return lax.ppermute(value, axis, pairs)


def to_slots(values, picker):
    return jnp.sum(jnp.where(picker[None, :, :, None], values[:, None, :, :], 0.0), axis=2)


def slots_to_heads(values, picker, filler):
    covered = jnp.any(picker, axis=0)
    summed = jnp.sum(jnp.where(picker[None, :, :, None], values[:, :, None, :], 0.0), axis=1)
    return jnp.where(covered[None, :, None], summed, filler)


def rows_slots_to_heads(values, picker):
    return jnp.einsum(
        "jqid,ih->jqhd", values, picker.astype(jnp.float32), precision=lax.Precision.HIGHEST
    )


def pick_heads(values, picker):
    chooser = picker.astype(jnp.bfloat16)
    return jnp.einsum("ih,jqhd->jqid", chooser, values, preferred_element_type=jnp.float32).astype(
        jnp.bfloat16
    )


def partner_route(values, section_index, low_bits):
    return partner(values, "seq", section_index - low_bits)


def partner_back(values, section_index, low_bits):
    return partner(values, "seq", section_index - low_bits)


def extend_blocks(values, reach, halo_blocks, blocks_dev, mover):
    pieces = [mover(values, distance) for distance in range(reach, 0, -1)]
    pieces = pieces + [values] + [mover(values, -distance) for distance in range(1, reach + 1)]
    start = reach * blocks_dev - halo_blocks
    whole = jnp.concatenate(pieces, axis=1)
    return whole


def move_keys(values, distance):
    return passed_along(values, "seq", distance)


def window_sets(extended, blocks_dev, spread):
    return jnp.stack(
        [extended[:, offset : offset + blocks_dev] for offset in range(spread)], axis=2
    )


def per_device(query_rows, key_rows, value_rows, out_grad, window_blocks, section_heads):
    tokens_dev, head_count, head_width = query_rows.shape
    blocks_dev = tokens_dev // BLK
    low_bits = blocks_dev.bit_length() - 1
    seq_count = lax.axis_size("seq")
    section_total = low_bits + seq_count.bit_length() - 1
    halo_blocks = WB - 1
    reach = (halo_blocks + blocks_dev - 1) // blocks_dev
    padding = reach * blocks_dev
    spread = 2 * WB - 1
    score_scale = 1.0 / math.sqrt(head_width)
    first_block = lax.axis_index("seq") * blocks_dev + jnp.arange(blocks_dev, dtype=jnp.int32)
    all_blocks = blocks_dev * seq_count
    query_blocks = query_rows.reshape(blocks_dev, BLK, head_count, head_width)
    key_blocks = key_rows.reshape(blocks_dev, BLK, head_count, head_width)
    value_blocks = value_rows.reshape(blocks_dev, BLK, head_count, head_width)
    grad_blocks = out_grad.reshape(blocks_dev, BLK, head_count, head_width)
    offsets = jnp.arange(spread, dtype=jnp.int32) - halo_blocks
    near_block = first_block[:, None] + offsets[None, :]
    in_range = (near_block >= 0) & (near_block < all_blocks)
    near_mask = in_range[:, None, :] & (
        jnp.abs(offsets)[None, None, :] < window_blocks[None, :, None]
    )
    wide_mask = near_mask[:, :, None, :, None]
    head_ids = jnp.arange(head_count, dtype=jnp.int32)
    paired = jnp.stack([key_blocks, value_blocks])
    extended = extend_blocks(paired, reach, halo_blocks, blocks_dev, move_keys)
    near_sets = window_sets(extended, blocks_dev, spread)
    near_keys = near_sets[0]
    near_values = near_sets[1]
    near_scores = (
        jnp.einsum("jqhd,jckhd->jhqck", query_blocks, near_keys, preferred_element_type=jnp.float32)
        * score_scale
    )
    near_scores = jnp.where(wide_mask, near_scores, blocked_score)
    top_score = jnp.max(near_scores, axis=(3, 4))
    records = []
    for section_index in range(section_total):
        picker = section_heads[section_index][:, None] == head_ids[None, :]
        slot_width = jnp.sum(jnp.where(picker, window_blocks[None, :], 0), axis=1)
        slot_valid = 2**section_index >= slot_width
        chosen_query = pick_heads(query_blocks, picker)
        chosen_grad = pick_heads(grad_blocks, picker)
        chosen_pair = jnp.stack([pick_heads(key_blocks, picker), pick_heads(value_blocks, picker)])
        partner_pair = partner_route(chosen_pair, section_index, low_bits)
        far_scores = (
            jnp.einsum(
                "jqid,jkid->jiqk", chosen_query, partner_pair[0], preferred_element_type=jnp.float32
            )
            * score_scale
        )
        far_scores = jnp.where(slot_valid[None, :, None, None], far_scores, blocked_score)
        top_score = jnp.maximum(
            top_score, slots_to_heads(jnp.max(far_scores, axis=3), picker, blocked_score)
        )
        records.append(
            (
                section_index,
                picker,
                slot_valid,
                chosen_query,
                chosen_grad,
                chosen_pair,
                partner_pair,
                far_scores,
            )
        )
    row_total = jnp.sum(
        jnp.where(wide_mask, jnp.exp(near_scores - top_score[:, :, :, None, None]), 0.0),
        axis=(3, 4),
    )
    for record in records:
        picker = record[1]
        slot_top = to_slots(top_score, picker)
        far_sum = jnp.sum(
            jnp.where(
                record[2][None, :, None, None], jnp.exp(record[7] - slot_top[:, :, :, None]), 0.0
            ),
            axis=3,
        )
        row_total = row_total + slots_to_heads(far_sum, picker, 0.0)
    log_total = top_score + jnp.log(row_total)
    near_probs = jnp.where(
        wide_mask, jnp.exp(near_scores - log_total[:, :, :, None, None]), 0.0
    ).astype(jnp.bfloat16)
    attended_sum = jnp.einsum(
        "jhqck,jckhd->jqhd", near_probs, near_values, preferred_element_type=jnp.float32
    )
    far_probs_list = []
    for record in records:
        picker = record[1]
        slot_lse = to_slots(log_total, picker)
        far_probs = jnp.where(
            record[2][None, :, None, None], jnp.exp(record[7] - slot_lse[:, :, :, None]), 0.0
        ).astype(jnp.bfloat16)
        far_probs_list.append((far_probs, slot_lse))
        attended_sum = attended_sum + rows_slots_to_heads(
            jnp.einsum(
                "jiqk,jkid->jqid", far_probs, record[6][1], preferred_element_type=jnp.float32
            ),
            picker,
        )
    attended = attended_sum.astype(jnp.bfloat16)
    row_delta = jnp.transpose(
        jnp.sum(grad_blocks.astype(jnp.float32) * attended.astype(jnp.float32), axis=-1), (0, 2, 1)
    )
    near_dprob = jnp.einsum(
        "jqhd,jckhd->jhqck", grad_blocks, near_values, preferred_element_type=jnp.float32
    )
    near_dscore = (
        near_probs.astype(jnp.float32) * (near_dprob - row_delta[:, :, :, None, None])
    ).astype(jnp.bfloat16)
    query_sum = jnp.einsum(
        "jhqck,jckhd->jqhd", near_dscore, near_keys, preferred_element_type=jnp.float32
    )
    far_dscores = []
    for record, probs_pair in zip(records, far_probs_list):
        picker = record[1]
        slot_delta = to_slots(row_delta, picker)
        far_dprob = jnp.einsum(
            "jqid,jkid->jiqk", record[4], record[6][1], preferred_element_type=jnp.float32
        )
        far_dscore = (
            probs_pair[0].astype(jnp.float32) * (far_dprob - slot_delta[:, :, :, None])
        ).astype(jnp.bfloat16)
        far_dscores.append((far_dscore, slot_delta))
        query_sum = query_sum + rows_slots_to_heads(
            jnp.einsum(
                "jiqk,jkid->jqid", far_dscore, record[6][0], preferred_element_type=jnp.float32
            ),
            picker,
        )
    query_grad = (
        (query_sum * score_scale).astype(jnp.bfloat16).reshape(tokens_dev, head_count, head_width)
    )
    near_key_part = (
        jnp.einsum(
            "jhqck,jqhd->jckhd", near_dscore, query_blocks, preferred_element_type=jnp.float32
        )
        * score_scale
    )
    near_value_part = jnp.einsum(
        "jhqck,jqhd->jckhd", near_probs, grad_blocks, preferred_element_type=jnp.float32
    )
    stacked_parts = jnp.stack([near_key_part, near_value_part])
    extended_count = blocks_dev + 2 * padding
    base = padding - halo_blocks
    extended_ids = jnp.arange(extended_count, dtype=jnp.int32)
    own_ids = jnp.arange(blocks_dev, dtype=jnp.int32)
    spread_ids = jnp.arange(spread, dtype=jnp.int32)
    placer = (
        extended_ids[:, None, None] == base + own_ids[None, :, None] + spread_ids[None, None, :]
    ).astype(jnp.float32)
    gathered = jnp.einsum(
        "ejc,xjckhd->xekhd", placer, stacked_parts, precision=lax.Precision.HIGHEST
    )
    own_grads = gathered[:, padding : padding + blocks_dev]
    for distance in range(1, reach + 1):
        lower_slab = gathered[
            :, padding - distance * blocks_dev : padding - (distance - 1) * blocks_dev
        ]
        own_grads = own_grads + passed_along(
            lower_slab.astype(jnp.bfloat16), "seq", -distance
        ).astype(lower_slab.dtype)
        upper_start = padding + blocks_dev + (distance - 1) * blocks_dev
        upper_slab = gathered[:, upper_start : upper_start + blocks_dev]
        own_grads = own_grads + passed_along(
            upper_slab.astype(jnp.bfloat16), "seq", distance
        ).astype(upper_slab.dtype)
    for record, probs_pair, dscore_pair in zip(records, far_probs_list, far_dscores):
        picker = record[1]
        key_part = (
            jnp.einsum(
                "jiqk,jqid->jkid", dscore_pair[0], record[3], preferred_element_type=jnp.float32
            )
            * score_scale
        )
        value_part = jnp.einsum(
            "jiqk,jqid->jkid", probs_pair[0], record[4], preferred_element_type=jnp.float32
        )
        returned = partner_back(jnp.stack([key_part, value_part]), record[0], low_bits)
        own_grads = own_grads + jnp.stack(
            [rows_slots_to_heads(returned[0], picker), rows_slots_to_heads(returned[1], picker)]
        )
    key_grad = own_grads[0].astype(jnp.bfloat16).reshape(tokens_dev, head_count, head_width)
    value_grad = own_grads[1].astype(jnp.bfloat16).reshape(tokens_dev, head_count, head_width)
    return (attended.reshape(tokens_dev, head_count, head_width), query_grad, key_grad, value_grad)


def in_plane(pieces):
    peers = lax.axis_size("seq")
    return [pieces[0]] + [
        lax.ppermute(pieces[m], "seq", [(i, i ^ m) for i in range(peers)])
        for m in range(1, PLANE)
    ]


def between_planes(value, by):
    return passed_along(value, "seq", by * PLANE)


def sharded_by_plane(query_rows, key_rows, value_rows, out_grad, widths, sections):
    position = lax.axis_index("seq").astype(jnp.int32)
    place = jnp.stack([position % PLANE, position // PLANE])
    blocks = lax.axis_size("seq")
    local = PLANE.bit_length() - 1
    total = sections.shape[0]
    groups = [tuple(range(local, total)), tuple(range(local))]
    order = tuple(s for group in groups for s in group)
    sent_far, sent_near = pack(place, sections, [key_rows, value_rows], groups)
    pairs_far, pairs_near = in_plane(sent_far), in_plane(sent_near)
    far_sent = far_parts(pairs_far)
    (sent,) = pack(place, sections, [query_rows, out_grad], [order])
    far_sent, sent = lax.optimization_barrier((far_sent, sent))
    far = [partner(value, "seq", local + n) for n, value in enumerate(far_sent)]
    up, down = halo_parts(place, [pairs_far, pairs_near])
    below, above = between_planes(up, 1), between_planes(down, -1)
    graded = in_plane(sent)
    shared = (place, widths, sections)
    outs_far, part_far, low_far, high_far, far_owed = attend(
        *shared, pairs_far, graded, below, above, far, local, 0, blocks
    )
    far_back = [partner(value, "seq", local + n) for n, value in enumerate(far_owed)]
    above_far, below_far = between_planes(low_far, -1), between_planes(high_far, 1)
    outs_near, part_near, low_near, high_near, _ = attend(
        *shared, pairs_near, graded, below, above, [], 0, total - local, blocks
    )
    above_near, below_near = between_planes(low_near, -1), between_planes(high_near, 1)
    rows = [in_plane(outs_far), in_plane(outs_near)]
    columns = [
        in_plane(combine(place, part_far, above_far, below_far, far_back)),
        in_plane(combine(place, part_near, above_near, below_near, [])),
    ]
    attended, query_grad = unpack(place, sections, rows, groups)
    key_grad, value_grad = unpack(place, sections, columns, groups)
    return attended, query_grad, key_grad, value_grad


def solution(mesh):
    spec = P(("grp", "seq"), None, None)
    peers = mesh.shape["seq"]

    def per_device_any(*args):
        tokens, heads, width = args[0].shape
        sections, listed = args[5].shape
        once = sections * listed == heads
        if tokens == BLK and once and listed == PLANE and 1 << sections == peers == PLANE**2:
            return sharded_by_plane(*args)
        return per_device(*args)

    return jax.shard_map(
        per_device_any,
        mesh=mesh,
        in_specs=(spec, spec, spec, spec, P(), P()),
        out_specs=(spec,) * 4,
        check_vma=False,
    )
```

```python
import functools
import math

import jax
import jax.numpy as jnp
from jax import lax
from jax.experimental import pallas as pl
from jax.experimental.pallas import tpu as pltpu
from jax.sharding import PartitionSpec as P

BLK = 128
WB = 3
HALO = WB - 1
SPAN = (2 * HALO + 1) * BLK
LINKED = SPAN + BLK
PLANE = 2 * HALO
PADDED = PLANE + 2 * HALO
NT = (((1,), (1,)), ((), ()))
NN = (((1,), (0,)), ((), ()))
blocked_score = -1e30


def mm(a, b, dims=NN):
    return lax.dot_general(a, b, dims, preferred_element_type=jnp.float32)


def moved_cost(arrays):
    return pl.CostEstimate(
        flops=0, transcendentals=0, bytes_accessed=4 * sum(a.size for a in arrays)
    )


def softmax_pair(score, far_score, biases, far_bias, scale2):
    near_parts, far_parts = [], []
    gap = jnp.zeros((BLK, BLK), jnp.bfloat16)
    for r in range(2):
        rows = slice(r * BLK, (r + 1) * BLK)
        sw = score[rows, r * BLK : r * BLK + SPAN] * scale2 + biases[r]
        sf = far_score[r] * scale2 + far_bias
        top = jnp.maximum(jnp.max(sw, axis=1, keepdims=True), jnp.max(sf, axis=1, keepdims=True))
        ew, ef = jnp.exp2(sw - top), jnp.exp2(sf - top)
        total = jnp.sum(ew, axis=1, keepdims=True) + jnp.sum(ef, axis=1, keepdims=True)
        inverse = 1.0 / total
        near = (ew * inverse).astype(jnp.bfloat16)
        near_parts.append(jnp.concatenate([near, gap] if r == 0 else [gap, near], axis=1))
        far_parts.append((ef * inverse).astype(jnp.bfloat16))
    return jnp.concatenate(near_parts, axis=0), far_parts


def attend_pair(q, g, kw, vw, kf, vf, biases, far_bias):
    scale = 1.0 / math.sqrt(q.shape[-1])
    scale2 = scale * math.log2(math.e)
    half = [slice(0, BLK), slice(BLK, 2 * BLK)]
    far_score = [mm(q[half[r]], kf[r], NT) for r in range(2)]
    near, far = softmax_pair(mm(q, kw, NT), far_score, biases, far_bias, scale2)
    far_out = jnp.concatenate([mm(far[r], vf[r]) for r in range(2)], axis=0)
    attended = (mm(near, vw) + far_out).astype(jnp.bfloat16)
    delta = jnp.sum(g.astype(jnp.float32) * attended.astype(jnp.float32), axis=1, keepdims=True)
    d_near = (near.astype(jnp.float32) * (mm(g, vw, NT) - delta)).astype(jnp.bfloat16)
    d_far = [
        (far[r].astype(jnp.float32) * (mm(g[half[r]], vf[r], NT) - delta[half[r]])).astype(
            jnp.bfloat16
        )
        for r in range(2)
    ]
    far_dq = jnp.concatenate([mm(d_far[r], kf[r]) for r in range(2)], axis=0)
    query_grad = ((mm(d_near, kw) + far_dq) * scale).astype(jnp.bfloat16)
    qt, gt = jnp.transpose(q), jnp.transpose(g)
    key_near, value_near = mm(qt, d_near), mm(gt, near)
    key_far = [mm(qt[:, half[r]], d_far[r]) for r in range(2)]
    value_far = [mm(gt[:, half[r]], far[r]) for r in range(2)]
    return attended, query_grad, key_near, value_near, key_far, value_far


def near_biases(b, width, low, high):
    offset = lax.broadcasted_iota(jnp.int32, (1, SPAN), 1) // BLK - HALO
    inside = jnp.abs(offset) < width
    out = []
    for r in range(2):
        there = offset + b + r
        out.append(jnp.where(inside & (there >= low) & (there < high), 0.0, blocked_score))
    return out


def rows_of(block):
    return pl.ds(pl.multiple_of(block * BLK, BLK), BLK)


def whole(shape):
    return pl.BlockSpec(shape, lambda *_: (0,) * len(shape))


SMEM = pl.BlockSpec(memory_space=pltpu.SMEM)
VMEM = pl.BlockSpec(memory_space=pltpu.VMEM)
LIMIT = pltpu.CompilerParams(vmem_limit_bytes=20 << 20)


def pack_kernel(place, sections, *refs, groups, count):
    ins, outs, held = refs[:count], refs[count:-1], refs[-1]
    for i in range(count):
        held[i] = jnp.transpose(ins[i][...], (1, 0, 2))
    for number, group in enumerate(groups):
        for m in range(PLANE):
            for k, s in enumerate(group):
                head = sections[s, place[0] ^ m]
                for i in range(count):
                    outs[number * PLANE + m][k, i] = held[i, head]


def pack(place, sections, arrays, groups):
    tokens, heads, width = arrays[0].shape
    chunk = tokens // 2
    count = len(arrays)
    shapes = [(len(group), count, tokens, width) for group in groups for _ in range(PLANE)]
    outs = pl.pallas_call(
        functools.partial(pack_kernel, groups=groups, count=count),
        grid=(tokens // chunk,),
        in_specs=[SMEM, SMEM]
        + [pl.BlockSpec((chunk, heads, width), lambda i: (i, 0, 0))] * count,
        out_specs=[
            pl.BlockSpec((*shape[:2], chunk, width), lambda i: (0, 0, i, 0)) for shape in shapes
        ],
        out_shape=[jax.ShapeDtypeStruct(shape, jnp.bfloat16) for shape in shapes],
        scratch_shapes=[pltpu.VMEM((count, heads, chunk, width), jnp.bfloat16)],
        cost_estimate=moved_cost(arrays),
    )(place, sections, *arrays)
    return [outs[i * PLANE : (i + 1) * PLANE] for i in range(len(groups))]


def unpack_kernel(place, sections, *refs, groups, count):
    pieces, outs, held = refs[: len(groups) * PLANE], refs[len(groups) * PLANE : -1], refs[-1]
    for number, group in enumerate(groups):
        for m in range(PLANE):
            for k, s in enumerate(group):
                head = sections[s, place[0] ^ m]
                for i in range(count):
                    held[i, head] = pieces[number * PLANE + m][k, i]
    for i in range(count):
        outs[i][...] = jnp.transpose(held[i], (1, 0, 2))


def unpack(place, sections, pieces, groups):
    flat = [piece for group in pieces for piece in group]
    _, count, tokens, width = flat[0].shape
    heads = sections.size
    chunk = tokens // 2
    return pl.pallas_call(
        functools.partial(unpack_kernel, groups=groups, count=count),
        grid=(tokens // chunk,),
        in_specs=[SMEM, SMEM]
        + [
            pl.BlockSpec((*piece.shape[:2], chunk, width), lambda i: (0, 0, i, 0))
            for piece in flat
        ],
        out_specs=[pl.BlockSpec((chunk, heads, width), lambda i: (i, 0, 0))] * count,
        out_shape=[jax.ShapeDtypeStruct((tokens, heads, width), jnp.bfloat16)] * count,
        scratch_shapes=[pltpu.VMEM((count, heads, chunk, width), jnp.bfloat16)],
        compiler_params=LIMIT,
        cost_estimate=moved_cost(flat),
    )(place, sections, *flat)


def facing(place):
    return place[0] // HALO == 1 - place[1] % 2


def collect_far_kernel(place, *refs):
    pieces, (with_next, with_other) = refs[:PLANE], refs[PLANE:]
    group = pieces[0].shape[0]
    for m in range(PLANE):
        with_next[m] = pieces[m][0]
        with_other[m] = pieces[m][1]

    def fill(base):
        for m in range(HALO):
            for k in range(group):
                with_next[PLANE + m * group + k] = pieces[base + m][k]

    @pl.when(facing(place))
    def _():
        fill(0)

    @pl.when(jnp.logical_not(facing(place)))
    def _():
        fill(HALO)


def collect_far(place, pieces):
    group, *rest = pieces[0].shape
    return pl.pallas_call(
        collect_far_kernel,
        in_specs=[SMEM] + [VMEM] * PLANE,
        out_specs=[VMEM] * 2,
        out_shape=[
            jax.ShapeDtypeStruct((PLANE + HALO * group, *rest), jnp.bfloat16),
            jax.ShapeDtypeStruct((PLANE, *rest), jnp.bfloat16),
        ],
        compiler_params=LIMIT,
        cost_estimate=moved_cost(pieces),
    )(place, *pieces)


def collect_near_kernel(place, *refs):
    far, near, (with_next, with_last) = refs[:PLANE], refs[PLANE:-2], refs[-2:]
    group = near[0].shape[0]

    def fill(base, other):
        for m in range(HALO):
            for k in range(group):
                with_next[m * group + k] = near[base + m][k]
                with_last[m * group + k] = far[other + m][k]
                with_last[(HALO + m) * group + k] = near[other + m][k]

    @pl.when(facing(place))
    def _():
        fill(0, HALO)

    @pl.when(jnp.logical_not(facing(place)))
    def _():
        fill(HALO, 0)


def collect_near(place, far, near):
    group, *rest = near[0].shape
    return pl.pallas_call(
        collect_near_kernel,
        in_specs=[SMEM] + [VMEM] * (2 * PLANE),
        out_specs=[VMEM] * 2,
        out_shape=[
            jax.ShapeDtypeStruct((HALO * group, *rest), jnp.bfloat16),
            jax.ShapeDtypeStruct((2 * HALO * group, *rest), jnp.bfloat16),
        ],
        compiler_params=LIMIT,
        cost_estimate=moved_cost([*far, *near]),
    )(place, *far, *near)


def attend_kernel(place, widths, sections, *refs, first, remote, base, blocks, aliased):
    pairs, graded = refs[:PLANE], refs[PLANE : 2 * PLANE]
    (with_next, with_last), rest = refs[2 * PLANE : 2 * PLANE + 2], refs[2 * PLANE + 2 :]
    if remote:
        with_other, rest = rest[0], rest[1:]
    rest = rest[aliased:]
    outs, rest = rest[:PLANE], rest[PLANE:]
    (part, to_next, to_last), rest = rest[:3], rest[3:]
    if remote:
        to_other, rest = rest[0], rest[1:]
    keys, values, far_keys, far_values, queries, grads, attended, dq = rest[:8]
    accs, far_accs = rest[8:10], rest[10:12]
    k = pl.program_id(0)
    group = pl.num_programs(0)
    section = first + k
    me = place[0]
    width = widths[sections[section, me]]
    bit = jnp.left_shift(jnp.int32(1), section)
    far_bias = jnp.where(bit >= width, 0.0, blocked_score).astype(jnp.float32)
    scales = (1.0 / math.sqrt(keys.shape[-1]), 1.0)
    lead = PLANE if remote else 0
    next_at = jnp.where(place[1] % 2 == 0, HALO + PLANE, 0)
    last_at = HALO + PLANE - next_at
    for m in range(PLANE):
        b = me ^ m
        keys[rows_of(HALO + b)] = pairs[m][0, 0]
        values[rows_of(HALO + b)] = pairs[m][0, 1]
        queries[rows_of(b)] = graded[m][0, 0]
        grads[rows_of(b)] = graded[m][0, 1]
    for m in range(HALO):
        b = (me % HALO) ^ m
        slot = m * group + k
        keys[rows_of(next_at + b)] = with_next[lead + slot, 0]
        values[rows_of(next_at + b)] = with_next[lead + slot, 1]
        keys[rows_of(last_at + b)] = with_last[base + slot, 0]
        values[rows_of(last_at + b)] = with_last[base + slot, 1]
    if remote:
        for n, source in enumerate((with_next, with_other)):

            @pl.when(k == n)
            def _(source=source):
                for m in range(PLANE):
                    far_keys[rows_of(me ^ m)] = source[m, 0]
                    far_values[rows_of(me ^ m)] = source[m, 1]
    else:
        for b in range(PLANE):
            far_keys[rows_of(b)] = keys[rows_of(HALO + (b ^ bit))]
            far_values[rows_of(b)] = values[rows_of(HALO + (b ^ bit))]
    for acc in accs:
        acc[...] = jnp.zeros_like(acc)
    for b in range(0, PLANE, 2):
        own = slice(b * BLK, (b + 2) * BLK)
        seen = slice(b * BLK, (b + 2 * HALO + 2) * BLK)
        one = [slice((b + r) * BLK, (b + r + 1) * BLK) for r in range(2)]
        o, d, key_near, value_near, key_far, value_far = attend_pair(
            queries[own],
            grads[own],
            keys[seen],
            values[seen],
            [far_keys[one[r]] for r in range(2)],
            [far_values[one[r]] for r in range(2)],
            near_biases(place[1] * PLANE + b, width, 0, blocks),
            far_bias,
        )
        attended[own] = o
        dq[own] = d
        for acc, near in zip(accs, (key_near, value_near)):
            acc[:, seen] += near
        for acc, far in zip(far_accs, (key_far, value_far)):
            for r in range(2):
                acc[:, one[r]] = far[r]
    for i, (acc, far_acc) in enumerate(zip(accs, far_accs)):
        if remote:
            for n, target in enumerate((to_next, to_other)):

                @pl.when(k == n)
                def _(target=target, i=i, far_acc=far_acc):
                    for m in range(PLANE):
                        target[m, i] = (far_acc[:, rows_of(me ^ m)] * scales[i]).astype(
                            jnp.bfloat16
                        )
        else:
            for b in range(PLANE):
                acc[:, rows_of(HALO + (b ^ bit))] += far_acc[:, b * BLK : (b + 1) * BLK]
        for m in range(PLANE):
            part[0, m, i] = acc[:, rows_of(HALO + (me ^ m))] * scales[i]
        for m in range(HALO):
            b = (me % HALO) ^ m
            slot = m * group + k
            to_next[lead + slot, i] = (acc[:, rows_of(next_at + b)] * scales[i]).astype(
                jnp.bfloat16
            )
            to_last[slot, i] = (acc[:, rows_of(last_at + b)] * scales[i]).astype(jnp.bfloat16)
    for m in range(PLANE):
        outs[m][0, 0] = attended[rows_of(me ^ m)]
        outs[m][0, 1] = dq[rows_of(me ^ m)]


def attend(place, widths, sections, pairs, graded, halos, first, slot, blocks, rows=()):
    group, count, _, width = pairs[0].shape
    tile = (BLK, width)
    remote = len(halos) > 2
    piece = pl.BlockSpec((1, count, *tile), lambda k: (k, 0, 0, 0))
    graded_piece = pl.BlockSpec((1, count, *tile), lambda k: (slot + k, 0, 0, 0))
    bf16 = jnp.bfloat16
    owed = [(HALO * group + (PLANE if remote else 0), count, *tile), (HALO * group, count, *tile)]
    if remote:
        owed.append((PLANE, count, *tile))
    outs = pl.pallas_call(
        functools.partial(
            attend_kernel,
            first=first,
            remote=remote,
            base=HALO * slot,
            blocks=blocks,
            aliased=len(rows),
        ),
        grid=(group,),
        in_specs=[SMEM] * 3
        + [piece] * PLANE
        + [graded_piece] * PLANE
        + [whole(halo.shape) for halo in halos]
        + [pl.BlockSpec(memory_space=pl.ANY)] * len(rows),
        out_specs=[graded_piece] * PLANE
        + [pl.BlockSpec((1, PLANE, count, *tile), lambda k: (k, 0, 0, 0, 0))]
        + [whole(shape) for shape in owed],
        out_shape=[jax.ShapeDtypeStruct(graded[0].shape, bf16)] * PLANE
        + [jax.ShapeDtypeStruct((group, PLANE, count, *tile), jnp.float32)]
        + [jax.ShapeDtypeStruct(shape, bf16) for shape in owed],
        scratch_shapes=[pltpu.VMEM((PADDED * BLK, width), bf16)] * 2
        + [pltpu.VMEM((PLANE * BLK, width), bf16)] * 6
        + [pltpu.VMEM((width, PADDED * BLK), jnp.float32)] * 2
        + [pltpu.VMEM((width, PLANE * BLK), jnp.float32)] * 2,
        input_output_aliases={3 + 2 * PLANE + len(halos) + m: m for m in range(len(rows))},
        compiler_params=LIMIT,
        cost_estimate=pl.CostEstimate(
            flops=group * PLANE * 12 * BLK * LINKED * width,
            transcendentals=group * PLANE * BLK * LINKED,
            bytes_accessed=40 * group * PLANE * BLK * width,
        ),
    )(place, widths, sections, *pairs, *graded, *halos, *rows)
    return outs[:PLANE], outs[PLANE], outs[PLANE + 1 :]


def combine_kernel(place, part, with_next, with_last, *refs, remote):
    outs = refs[remote:]
    group = part.shape[0]
    lead = PLANE if remote else 0
    for m in range(PLANE):
        own_chip = m < HALO
        next_side = facing(place) if own_chip else jnp.logical_not(facing(place))
        for k in range(group):
            slot = (m % HALO) * group + k
            for i in range(part.shape[2]):
                owed = jnp.where(next_side, with_next[lead + slot, i], with_last[slot, i])
                total = part[k, m, i] + owed.astype(jnp.float32)
                if remote:
                    far = (with_next, refs[0])[k]
                    total += far[m, i].astype(jnp.float32)
                outs[m][k, i] = jnp.transpose(total.astype(jnp.bfloat16))


def combine(place, part, owed):
    group, _, *rest = part.shape
    return pl.pallas_call(
        functools.partial(combine_kernel, remote=len(owed) - 2),
        in_specs=[SMEM] + [VMEM] * (1 + len(owed)),
        out_specs=[VMEM] * PLANE,
        out_shape=[jax.ShapeDtypeStruct((group, *rest), jnp.bfloat16)] * PLANE,
        compiler_params=LIMIT,
        cost_estimate=moved_cost([part, *owed]),
    )(place, part, *owed)


def partner(value, axis, apart):
    return lax.ppermute(value, axis, [(i, i ^ 1 << apart) for i in range(lax.axis_size(axis))])


def passed_along(value, axis, by):
    peers = lax.axis_size(axis)
    pairs = [(i, i + by) for i in range(peers) if 0 <= i + by < peers]
    return lax.ppermute(value, axis, pairs)


def to_slots(values, picker):
    return jnp.sum(jnp.where(picker[None, :, :, None], values[:, None, :, :], 0.0), axis=2)


def slots_to_heads(values, picker, filler):
    covered = jnp.any(picker, axis=0)
    summed = jnp.sum(jnp.where(picker[None, :, :, None], values[:, :, None, :], 0.0), axis=1)
    return jnp.where(covered[None, :, None], summed, filler)


def rows_slots_to_heads(values, picker):
    return jnp.einsum(
        "jqid,ih->jqhd", values, picker.astype(jnp.float32), precision=lax.Precision.HIGHEST
    )


def pick_heads(values, picker):
    chooser = picker.astype(jnp.bfloat16)
    return jnp.einsum("ih,jqhd->jqid", chooser, values, preferred_element_type=jnp.float32).astype(
        jnp.bfloat16
    )


def partner_route(values, section_index, low_bits):
    return partner(values, "seq", section_index - low_bits)


def partner_back(values, section_index, low_bits):
    return partner(values, "seq", section_index - low_bits)


def extend_blocks(values, reach, halo_blocks, blocks_dev, mover):
    pieces = [mover(values, distance) for distance in range(reach, 0, -1)]
    pieces = pieces + [values] + [mover(values, -distance) for distance in range(1, reach + 1)]
    start = reach * blocks_dev - halo_blocks
    whole = jnp.concatenate(pieces, axis=1)
    return whole


def move_keys(values, distance):
    return passed_along(values, "seq", distance)


def window_sets(extended, blocks_dev, spread):
    return jnp.stack(
        [extended[:, offset : offset + blocks_dev] for offset in range(spread)], axis=2
    )


def per_device(query_rows, key_rows, value_rows, out_grad, window_blocks, section_heads):
    tokens_dev, head_count, head_width = query_rows.shape
    blocks_dev = tokens_dev // BLK
    low_bits = blocks_dev.bit_length() - 1
    seq_count = lax.axis_size("seq")
    section_total = low_bits + seq_count.bit_length() - 1
    halo_blocks = WB - 1
    reach = (halo_blocks + blocks_dev - 1) // blocks_dev
    padding = reach * blocks_dev
    spread = 2 * WB - 1
    score_scale = 1.0 / math.sqrt(head_width)
    first_block = lax.axis_index("seq") * blocks_dev + jnp.arange(blocks_dev, dtype=jnp.int32)
    all_blocks = blocks_dev * seq_count
    query_blocks = query_rows.reshape(blocks_dev, BLK, head_count, head_width)
    key_blocks = key_rows.reshape(blocks_dev, BLK, head_count, head_width)
    value_blocks = value_rows.reshape(blocks_dev, BLK, head_count, head_width)
    grad_blocks = out_grad.reshape(blocks_dev, BLK, head_count, head_width)
    offsets = jnp.arange(spread, dtype=jnp.int32) - halo_blocks
    near_block = first_block[:, None] + offsets[None, :]
    in_range = (near_block >= 0) & (near_block < all_blocks)
    near_mask = in_range[:, None, :] & (
        jnp.abs(offsets)[None, None, :] < window_blocks[None, :, None]
    )
    wide_mask = near_mask[:, :, None, :, None]
    head_ids = jnp.arange(head_count, dtype=jnp.int32)
    paired = jnp.stack([key_blocks, value_blocks])
    extended = extend_blocks(paired, reach, halo_blocks, blocks_dev, move_keys)
    near_sets = window_sets(extended, blocks_dev, spread)
    near_keys = near_sets[0]
    near_values = near_sets[1]
    near_scores = (
        jnp.einsum("jqhd,jckhd->jhqck", query_blocks, near_keys, preferred_element_type=jnp.float32)
        * score_scale
    )
    near_scores = jnp.where(wide_mask, near_scores, blocked_score)
    top_score = jnp.max(near_scores, axis=(3, 4))
    records = []
    for section_index in range(section_total):
        picker = section_heads[section_index][:, None] == head_ids[None, :]
        slot_width = jnp.sum(jnp.where(picker, window_blocks[None, :], 0), axis=1)
        slot_valid = 2**section_index >= slot_width
        chosen_query = pick_heads(query_blocks, picker)
        chosen_grad = pick_heads(grad_blocks, picker)
        chosen_pair = jnp.stack([pick_heads(key_blocks, picker), pick_heads(value_blocks, picker)])
        partner_pair = partner_route(chosen_pair, section_index, low_bits)
        far_scores = (
            jnp.einsum(
                "jqid,jkid->jiqk", chosen_query, partner_pair[0], preferred_element_type=jnp.float32
            )
            * score_scale
        )
        far_scores = jnp.where(slot_valid[None, :, None, None], far_scores, blocked_score)
        top_score = jnp.maximum(
            top_score, slots_to_heads(jnp.max(far_scores, axis=3), picker, blocked_score)
        )
        records.append(
            (
                section_index,
                picker,
                slot_valid,
                chosen_query,
                chosen_grad,
                chosen_pair,
                partner_pair,
                far_scores,
            )
        )
    row_total = jnp.sum(
        jnp.where(wide_mask, jnp.exp(near_scores - top_score[:, :, :, None, None]), 0.0),
        axis=(3, 4),
    )
    for record in records:
        picker = record[1]
        slot_top = to_slots(top_score, picker)
        far_sum = jnp.sum(
            jnp.where(
                record[2][None, :, None, None], jnp.exp(record[7] - slot_top[:, :, :, None]), 0.0
            ),
            axis=3,
        )
        row_total = row_total + slots_to_heads(far_sum, picker, 0.0)
    log_total = top_score + jnp.log(row_total)
    near_probs = jnp.where(
        wide_mask, jnp.exp(near_scores - log_total[:, :, :, None, None]), 0.0
    ).astype(jnp.bfloat16)
    attended_sum = jnp.einsum(
        "jhqck,jckhd->jqhd", near_probs, near_values, preferred_element_type=jnp.float32
    )
    far_probs_list = []
    for record in records:
        picker = record[1]
        slot_lse = to_slots(log_total, picker)
        far_probs = jnp.where(
            record[2][None, :, None, None], jnp.exp(record[7] - slot_lse[:, :, :, None]), 0.0
        ).astype(jnp.bfloat16)
        far_probs_list.append((far_probs, slot_lse))
        attended_sum = attended_sum + rows_slots_to_heads(
            jnp.einsum(
                "jiqk,jkid->jqid", far_probs, record[6][1], preferred_element_type=jnp.float32
            ),
            picker,
        )
    attended = attended_sum.astype(jnp.bfloat16)
    row_delta = jnp.transpose(
        jnp.sum(grad_blocks.astype(jnp.float32) * attended.astype(jnp.float32), axis=-1), (0, 2, 1)
    )
    near_dprob = jnp.einsum(
        "jqhd,jckhd->jhqck", grad_blocks, near_values, preferred_element_type=jnp.float32
    )
    near_dscore = (
        near_probs.astype(jnp.float32) * (near_dprob - row_delta[:, :, :, None, None])
    ).astype(jnp.bfloat16)
    query_sum = jnp.einsum(
        "jhqck,jckhd->jqhd", near_dscore, near_keys, preferred_element_type=jnp.float32
    )
    far_dscores = []
    for record, probs_pair in zip(records, far_probs_list):
        picker = record[1]
        slot_delta = to_slots(row_delta, picker)
        far_dprob = jnp.einsum(
            "jqid,jkid->jiqk", record[4], record[6][1], preferred_element_type=jnp.float32
        )
        far_dscore = (
            probs_pair[0].astype(jnp.float32) * (far_dprob - slot_delta[:, :, :, None])
        ).astype(jnp.bfloat16)
        far_dscores.append((far_dscore, slot_delta))
        query_sum = query_sum + rows_slots_to_heads(
            jnp.einsum(
                "jiqk,jkid->jqid", far_dscore, record[6][0], preferred_element_type=jnp.float32
            ),
            picker,
        )
    query_grad = (
        (query_sum * score_scale).astype(jnp.bfloat16).reshape(tokens_dev, head_count, head_width)
    )
    near_key_part = (
        jnp.einsum(
            "jhqck,jqhd->jckhd", near_dscore, query_blocks, preferred_element_type=jnp.float32
        )
        * score_scale
    )
    near_value_part = jnp.einsum(
        "jhqck,jqhd->jckhd", near_probs, grad_blocks, preferred_element_type=jnp.float32
    )
    stacked_parts = jnp.stack([near_key_part, near_value_part])
    extended_count = blocks_dev + 2 * padding
    base = padding - halo_blocks
    extended_ids = jnp.arange(extended_count, dtype=jnp.int32)
    own_ids = jnp.arange(blocks_dev, dtype=jnp.int32)
    spread_ids = jnp.arange(spread, dtype=jnp.int32)
    placer = (
        extended_ids[:, None, None] == base + own_ids[None, :, None] + spread_ids[None, None, :]
    ).astype(jnp.float32)
    gathered = jnp.einsum(
        "ejc,xjckhd->xekhd", placer, stacked_parts, precision=lax.Precision.HIGHEST
    )
    own_grads = gathered[:, padding : padding + blocks_dev]
    for distance in range(1, reach + 1):
        lower_slab = gathered[
            :, padding - distance * blocks_dev : padding - (distance - 1) * blocks_dev
        ]
        own_grads = own_grads + passed_along(
            lower_slab.astype(jnp.bfloat16), "seq", -distance
        ).astype(lower_slab.dtype)
        upper_start = padding + blocks_dev + (distance - 1) * blocks_dev
        upper_slab = gathered[:, upper_start : upper_start + blocks_dev]
        own_grads = own_grads + passed_along(
            upper_slab.astype(jnp.bfloat16), "seq", distance
        ).astype(upper_slab.dtype)
    for record, probs_pair, dscore_pair in zip(records, far_probs_list, far_dscores):
        picker = record[1]
        key_part = (
            jnp.einsum(
                "jiqk,jqid->jkid", dscore_pair[0], record[3], preferred_element_type=jnp.float32
            )
            * score_scale
        )
        value_part = jnp.einsum(
            "jiqk,jqid->jkid", probs_pair[0], record[4], preferred_element_type=jnp.float32
        )
        returned = partner_back(jnp.stack([key_part, value_part]), record[0], low_bits)
        own_grads = own_grads + jnp.stack(
            [rows_slots_to_heads(returned[0], picker), rows_slots_to_heads(returned[1], picker)]
        )
    key_grad = own_grads[0].astype(jnp.bfloat16).reshape(tokens_dev, head_count, head_width)
    value_grad = own_grads[1].astype(jnp.bfloat16).reshape(tokens_dev, head_count, head_width)
    return (attended.reshape(tokens_dev, head_count, head_width), query_grad, key_grad, value_grad)


def in_plane(pieces):
    peers = lax.axis_size("seq")
    return [pieces[0]] + [
        lax.ppermute(pieces[m], "seq", [(i, i ^ m) for i in range(peers)])
        for m in range(1, PLANE)
    ]


def with_next_plane(value):
    return partner(value, "seq", PLANE.bit_length() - 1)


def with_other_plane(value):
    return partner(value, "seq", PLANE.bit_length())


def with_last_plane(value):
    peers = lax.axis_size("seq")
    pairs = []
    for i in range(peers):
        other = i + PLANE if i // PLANE % 2 else i - PLANE
        if 0 <= other < peers:
            pairs.append((i, other))
    return lax.ppermute(value, "seq", pairs)


def sharded_by_plane(query_rows, key_rows, value_rows, out_grad, widths, sections):
    position = lax.axis_index("seq").astype(jnp.int32)
    place = jnp.stack([position % PLANE, position // PLANE])
    blocks = lax.axis_size("seq")
    local = PLANE.bit_length() - 1
    total = sections.shape[0]
    groups = [tuple(range(local, total)), tuple(range(local))]
    order = tuple(s for group in groups for s in group)
    sent_far, sent_near = pack(place, sections, [key_rows, value_rows], groups)
    pairs_far = in_plane(sent_far)
    next_sent, other_sent = collect_far(place, pairs_far)
    (next_sent, other_sent), sent_near = lax.optimization_barrier(
        ((next_sent, other_sent), sent_near)
    )
    other_far = with_other_plane(other_sent)
    next_far = with_next_plane(next_sent)
    pairs_near = in_plane(sent_near)
    next_sent, last_sent = collect_near(place, pairs_far, pairs_near)
    (sent,) = pack(place, sections, [query_rows, out_grad], [order])
    (next_sent, last_sent), sent = lax.optimization_barrier(((next_sent, last_sent), sent))
    last = with_last_plane(last_sent)
    next_near = with_next_plane(next_sent)
    graded = in_plane(sent)
    rows, part_far, owed = attend(
        place, widths, sections, pairs_far, graded, [next_far, last, other_far], local, 0, blocks
    )
    other_back = with_other_plane(owed[2])
    owed_far = [with_next_plane(owed[0]), with_last_plane(owed[1]), other_back]
    rows, part_near, owed = attend(
        place, widths, sections, pairs_near, graded, [next_near, last], 0, total - local, blocks, rows
    )
    owed_near = [with_next_plane(owed[0]), with_last_plane(owed[1])]
    rows = in_plane(rows)
    columns = [
        in_plane(combine(place, part_far, owed_far)),
        in_plane(combine(place, part_near, owed_near)),
    ]
    attended, query_grad = unpack(place, sections, [rows], [order])
    key_grad, value_grad = unpack(place, sections, columns, groups)
    return attended, query_grad, key_grad, value_grad


def solution(mesh):
    spec = P(("grp", "seq"), None, None)
    peers = mesh.shape["seq"]

    def per_device_any(*args):
        tokens, heads, width = args[0].shape
        sections, listed = args[5].shape
        once = sections * listed == heads
        if tokens == BLK and once and listed == PLANE and 1 << sections == peers == PLANE**2:
            return sharded_by_plane(*args)
        return per_device(*args)

    return jax.shard_map(
        per_device_any,
        mesh=mesh,
        in_specs=(spec, spec, spec, spec, P(), P()),
        out_specs=(spec,) * 4,
        check_vma=False,
    )
```

```python
import functools
import math

import jax
import jax.numpy as jnp
from jax import lax
from jax.experimental import pallas as pl
from jax.experimental.pallas import tpu as pltpu
from jax.sharding import PartitionSpec as P

BLK = 128
WB = 3
HALO = WB - 1
SPAN = (2 * HALO + 1) * BLK
LINKED = SPAN + BLK
PLANE = 2 * HALO
PADDED = PLANE + 2 * HALO
NT = (((1,), (1,)), ((), ()))
NN = (((1,), (0,)), ((), ()))
blocked_score = -1e30


def mm(a, b, dims=NN):
    return lax.dot_general(a, b, dims, preferred_element_type=jnp.float32)


def moved_cost(arrays):
    return pl.CostEstimate(
        flops=0, transcendentals=0, bytes_accessed=4 * sum(a.size for a in arrays)
    )


def softmax_pair(score, far_score, biases, far_bias, scale2):
    near_parts, far_parts = [], []
    gap = jnp.zeros((BLK, BLK), jnp.bfloat16)
    for r in range(2):
        rows = slice(r * BLK, (r + 1) * BLK)
        sw = score[rows, r * BLK : r * BLK + SPAN] * scale2 + biases[r]
        sf = far_score[r] * scale2 + far_bias
        top = jnp.maximum(jnp.max(sw, axis=1, keepdims=True), jnp.max(sf, axis=1, keepdims=True))
        ew, ef = jnp.exp2(sw - top), jnp.exp2(sf - top)
        total = jnp.sum(ew, axis=1, keepdims=True) + jnp.sum(ef, axis=1, keepdims=True)
        inverse = 1.0 / total
        near = (ew * inverse).astype(jnp.bfloat16)
        near_parts.append(jnp.concatenate([near, gap] if r == 0 else [gap, near], axis=1))
        far_parts.append((ef * inverse).astype(jnp.bfloat16))
    return jnp.concatenate(near_parts, axis=0), far_parts


def attend_pair(q, g, kw, vw, kf, vf, biases, far_bias):
    scale = 1.0 / math.sqrt(q.shape[-1])
    scale2 = scale * math.log2(math.e)
    half = [slice(0, BLK), slice(BLK, 2 * BLK)]
    far_score = [mm(q[half[r]], kf[r], NT) for r in range(2)]
    near, far = softmax_pair(mm(q, kw, NT), far_score, biases, far_bias, scale2)
    far_out = jnp.concatenate([mm(far[r], vf[r]) for r in range(2)], axis=0)
    attended = (mm(near, vw) + far_out).astype(jnp.bfloat16)
    delta = jnp.sum(g.astype(jnp.float32) * attended.astype(jnp.float32), axis=1, keepdims=True)
    d_near = (near.astype(jnp.float32) * (mm(g, vw, NT) - delta)).astype(jnp.bfloat16)
    d_far = [
        (far[r].astype(jnp.float32) * (mm(g[half[r]], vf[r], NT) - delta[half[r]])).astype(
            jnp.bfloat16
        )
        for r in range(2)
    ]
    far_dq = jnp.concatenate([mm(d_far[r], kf[r]) for r in range(2)], axis=0)
    query_grad = ((mm(d_near, kw) + far_dq) * scale).astype(jnp.bfloat16)
    qt, gt = jnp.transpose(q), jnp.transpose(g)
    key_near, value_near = mm(qt, d_near), mm(gt, near)
    key_far = [mm(qt[:, half[r]], d_far[r]) for r in range(2)]
    value_far = [mm(gt[:, half[r]], far[r]) for r in range(2)]
    return attended, query_grad, key_near, value_near, key_far, value_far


def near_biases(b, width, low, high):
    offset = lax.broadcasted_iota(jnp.int32, (1, SPAN), 1) // BLK - HALO
    inside = jnp.abs(offset) < width
    out = []
    for r in range(2):
        there = offset + b + r
        out.append(jnp.where(inside & (there >= low) & (there < high), 0.0, blocked_score))
    return out


def rows_of(block):
    return pl.ds(pl.multiple_of(block * BLK, BLK), BLK)


def whole(shape):
    return pl.BlockSpec(shape, lambda *_: (0,) * len(shape))


SMEM = pl.BlockSpec(memory_space=pltpu.SMEM)
VMEM = pl.BlockSpec(memory_space=pltpu.VMEM)
LIMIT = pltpu.CompilerParams(vmem_limit_bytes=20 << 20)


def pack_kernel(place, sections, *refs, order, count, crossed):
    ins, outs, held = refs[:count], refs[count:-1], refs[-1]
    for i in range(count):
        held[i] = jnp.transpose(ins[i][...], (1, 0, 2))
    for m in range(PLANE):
        owner = place[0] ^ m if crossed else m
        for k, s in enumerate(order):
            head = sections[s, owner]
            for i in range(count):
                if crossed:
                    outs[m][k, i] = held[i, head]
                else:
                    outs[0][m, k, i] = held[i, head]


def pack(place, sections, arrays, order, crossed):
    tokens, heads, width = arrays[0].shape
    chunk = tokens // 2
    count = len(arrays)
    shape = (len(order), count, tokens, width)
    if crossed:
        shapes = [shape] * PLANE
        specs = [pl.BlockSpec((*shape[:2], chunk, width), lambda i: (0, 0, i, 0))] * PLANE
    else:
        shapes = [(PLANE, *shape)]
        specs = [pl.BlockSpec((PLANE, *shape[:2], chunk, width), lambda i: (0, 0, 0, i, 0))]
    return pl.pallas_call(
        functools.partial(pack_kernel, order=order, count=count, crossed=crossed),
        grid=(tokens // chunk,),
        in_specs=[SMEM, SMEM]
        + [pl.BlockSpec((chunk, heads, width), lambda i: (i, 0, 0))] * count,
        out_specs=specs,
        out_shape=[jax.ShapeDtypeStruct(shape, jnp.bfloat16) for shape in shapes],
        scratch_shapes=[pltpu.VMEM((count, heads, chunk, width), jnp.bfloat16)],
        cost_estimate=moved_cost(arrays),
    )(place, sections, *arrays)


def unpack_crossed_kernel(place, sections, *refs, groups, count):
    pieces, outs, held = refs[: len(groups) * PLANE], refs[len(groups) * PLANE : -1], refs[-1]
    for number, group in enumerate(groups):
        for m in range(PLANE):
            for k, s in enumerate(group):
                head = sections[s, place[0] ^ m]
                for i in range(count):
                    held[i, head] = pieces[number * PLANE + m][k, i]
    for i in range(count):
        outs[i][...] = jnp.transpose(held[i], (1, 0, 2))


def unpack_kernel(place, sections, src, *refs, order, count):
    outs, held = refs[:-1], refs[-1]
    for m in range(PLANE):
        for k, s in enumerate(order):
            head = sections[s, m]
            for i in range(count):
                held[i, head] = src[m, k, i]
    for i in range(count):
        outs[i][...] = jnp.transpose(held[i], (1, 0, 2))


def unpack(place, sections, kernel, pieces):
    *lead, count, tokens, width = pieces[0].shape
    heads = sections.size
    chunk = tokens // 2
    return pl.pallas_call(
        functools.partial(kernel, count=count),
        grid=(tokens // chunk,),
        in_specs=[SMEM, SMEM]
        + [
            pl.BlockSpec(
                (*piece.shape[:-2], chunk, width),
                lambda i, zeros=(0,) * (piece.ndim - 2): (*zeros, i, 0),
            )
            for piece in pieces
        ],
        out_specs=[pl.BlockSpec((chunk, heads, width), lambda i: (i, 0, 0))] * count,
        out_shape=[jax.ShapeDtypeStruct((tokens, heads, width), jnp.bfloat16)] * count,
        scratch_shapes=[pltpu.VMEM((count, heads, chunk, width), jnp.bfloat16)],
        compiler_params=LIMIT,
        cost_estimate=moved_cost(pieces),
    )(place, sections, *pieces)


def facing(place):
    return place[0] // HALO == 1 - place[1] % 2


def far_kernel(*refs):
    pieces, outs = refs[:PLANE], refs[PLANE:]
    for k, out in enumerate(outs):
        for m, piece in enumerate(pieces):
            out[m] = piece[k]


def far_parts(pieces, count):
    rest = pieces[0].shape[1:]
    return pl.pallas_call(
        far_kernel,
        in_specs=[VMEM] * PLANE,
        out_specs=[VMEM] * count,
        out_shape=[jax.ShapeDtypeStruct((PLANE, *rest), jnp.bfloat16)] * count,
        compiler_params=LIMIT,
        cost_estimate=moved_cost(pieces),
    )(*pieces)


def halo_kernel(place, *refs):
    pieces, (with_next, with_last) = refs[:PLANE], refs[PLANE:]
    slots = pieces[0].shape[0]

    def fill(base, other):
        for m in range(HALO):
            with_next[m * slots : (m + 1) * slots] = pieces[base + m][...]
            with_last[m * slots : (m + 1) * slots] = pieces[other + m][...]

    @pl.when(facing(place))
    def _():
        fill(0, HALO)

    @pl.when(jnp.logical_not(facing(place)))
    def _():
        fill(HALO, 0)


def halo_parts(place, pieces):
    slots, *rest = pieces[0].shape
    return pl.pallas_call(
        halo_kernel,
        in_specs=[SMEM] + [VMEM] * PLANE,
        out_specs=[VMEM] * 2,
        out_shape=[jax.ShapeDtypeStruct((HALO * slots, *rest), jnp.bfloat16)] * 2,
        compiler_params=LIMIT,
        cost_estimate=moved_cost(pieces),
    )(place, *pieces)


def attend_kernel(place, widths, sections, *refs, first, slot, remote, blocks, aliased):
    pairs, (graded, with_next, with_last) = refs[:PLANE], refs[PLANE : PLANE + 3]
    rest = refs[PLANE + 3 :]
    if remote:
        far_in, rest = rest[:2], rest[2:]
    rest = rest[aliased:]
    (rows, part, to_next, to_last), rest = rest[:4], rest[4:]
    if remote:
        to_other, rest = rest[0], rest[1:]
    keys, values, far_keys, far_values, queries, grads, attended, dq = rest[:8]
    accs, far_accs = rest[8:10], rest[10:12]
    k = pl.program_id(0)
    group = pl.num_programs(0)
    section = first + k
    me = place[0]
    width = widths[sections[section, me]]
    bit = jnp.left_shift(jnp.int32(1), section)
    far_bias = jnp.where(bit >= width, 0.0, blocked_score).astype(jnp.float32)
    scales = (1.0 / math.sqrt(keys.shape[-1]), 1.0)
    lead = PLANE if remote else 0
    pairs_slots = with_next.shape[0] // HALO
    next_at = jnp.where(place[1] % 2 == 0, HALO + PLANE, 0)
    last_at = HALO + PLANE - next_at
    for m in range(PLANE):
        b = me ^ m
        keys[rows_of(HALO + b)] = pairs[m][0, 0]
        values[rows_of(HALO + b)] = pairs[m][0, 1]
        queries[m * BLK : (m + 1) * BLK] = graded[m, 0, 0]
        grads[m * BLK : (m + 1) * BLK] = graded[m, 0, 1]
    for m in range(HALO):
        b = (me % HALO) ^ m
        at = m * pairs_slots + slot + k
        keys[rows_of(next_at + b)] = with_next[at, 0]
        values[rows_of(next_at + b)] = with_next[at, 1]
        keys[rows_of(last_at + b)] = with_last[at, 0]
        values[rows_of(last_at + b)] = with_last[at, 1]
    if remote:
        for n, source in enumerate(far_in):

            @pl.when(k == n)
            def _(source=source):
                for m in range(PLANE):
                    far_keys[rows_of(me ^ m)] = source[m, 0]
                    far_values[rows_of(me ^ m)] = source[m, 1]
    else:
        for b in range(PLANE):
            far_keys[rows_of(b)] = keys[rows_of(HALO + (b ^ bit))]
            far_values[rows_of(b)] = values[rows_of(HALO + (b ^ bit))]
    for acc in accs:
        acc[...] = jnp.zeros_like(acc)
    for b in range(0, PLANE, 2):
        own = slice(b * BLK, (b + 2) * BLK)
        seen = slice(b * BLK, (b + 2 * HALO + 2) * BLK)
        one = [slice((b + r) * BLK, (b + r + 1) * BLK) for r in range(2)]
        o, d, key_near, value_near, key_far, value_far = attend_pair(
            queries[own],
            grads[own],
            keys[seen],
            values[seen],
            [far_keys[one[r]] for r in range(2)],
            [far_values[one[r]] for r in range(2)],
            near_biases(place[1] * PLANE + b, width, 0, blocks),
            far_bias,
        )
        attended[own] = o
        dq[own] = d
        for acc, near in zip(accs, (key_near, value_near)):
            acc[:, seen] += near
        for acc, far in zip(far_accs, (key_far, value_far)):
            for r in range(2):
                acc[:, one[r]] = far[r]
    for i, (acc, far_acc) in enumerate(zip(accs, far_accs)):
        if remote:
            for n, target in enumerate((to_next, to_other)):

                @pl.when(k == n)
                def _(target=target, i=i, far_acc=far_acc):
                    for m in range(PLANE):
                        target[m, i] = (far_acc[:, rows_of(me ^ m)] * scales[i]).astype(
                            jnp.bfloat16
                        )
        else:
            for b in range(PLANE):
                acc[:, rows_of(HALO + (b ^ bit))] += far_acc[:, b * BLK : (b + 1) * BLK]
        for m in range(PLANE):
            part[0, m, i] = acc[:, rows_of(HALO + (me ^ m))] * scales[i]
        for m in range(HALO):
            b = (me % HALO) ^ m
            at = m * group + k
            to_next[lead + at, i] = (acc[:, rows_of(next_at + b)] * scales[i]).astype(jnp.bfloat16)
            to_last[at, i] = (acc[:, rows_of(last_at + b)] * scales[i]).astype(jnp.bfloat16)
    for b in range(PLANE):
        rows[b, 0, 0] = attended[b * BLK : (b + 1) * BLK]
        rows[b, 0, 1] = dq[b * BLK : (b + 1) * BLK]


def attend(place, widths, sections, pairs, graded, halos, far, group, first, slot, blocks, rows=()):
    count, _, width = pairs[0].shape[1:]
    tile = (BLK, width)
    remote = len(far)
    piece = pl.BlockSpec((1, count, *tile), lambda k: (slot + k, 0, 0, 0))
    row_piece = pl.BlockSpec((PLANE, 1, count, *tile), lambda k: (0, slot + k, 0, 0, 0))
    bf16 = jnp.bfloat16
    owed = [(HALO * group + (PLANE if remote else 0), count, *tile), (HALO * group, count, *tile)]
    if remote:
        owed.append((PLANE, count, *tile))
    outs = pl.pallas_call(
        functools.partial(
            attend_kernel,
            first=first,
            slot=slot,
            remote=remote,
            blocks=blocks,
            aliased=len(rows),
        ),
        grid=(group,),
        in_specs=[SMEM] * 3
        + [piece] * PLANE
        + [row_piece]
        + [whole(halo.shape) for halo in (*halos, *far)]
        + [pl.BlockSpec(memory_space=pl.ANY)] * len(rows),
        out_specs=[row_piece, pl.BlockSpec((1, PLANE, count, *tile), lambda k: (k, 0, 0, 0, 0))]
        + [whole(shape) for shape in owed],
        out_shape=[
            jax.ShapeDtypeStruct(graded.shape, bf16),
            jax.ShapeDtypeStruct((group, PLANE, count, *tile), jnp.float32),
        ]
        + [jax.ShapeDtypeStruct(shape, bf16) for shape in owed],
        scratch_shapes=[pltpu.VMEM((PADDED * BLK, width), bf16)] * 2
        + [pltpu.VMEM((PLANE * BLK, width), bf16)] * 6
        + [pltpu.VMEM((width, PADDED * BLK), jnp.float32)] * 2
        + [pltpu.VMEM((width, PLANE * BLK), jnp.float32)] * 2,
        input_output_aliases={4 + PLANE + len(halos) + len(far): 0} if rows else {},
        cost_estimate=pl.CostEstimate(
            flops=group * PLANE * 12 * BLK * LINKED * width,
            transcendentals=group * PLANE * BLK * LINKED,
            bytes_accessed=40 * group * PLANE * BLK * width,
        ),
    )(place, widths, sections, *pairs, graded, *halos, *far, *rows)
    return outs[0], outs[1], outs[2:]


def combine_kernel(place, part, with_next, with_last, *refs, remote):
    outs = refs[remote:]
    group = part.shape[0]
    lead = PLANE if remote else 0
    for m in range(PLANE):
        own_chip = m < HALO
        next_side = facing(place) if own_chip else jnp.logical_not(facing(place))
        for k in range(group):
            slot = (m % HALO) * group + k
            for i in range(part.shape[2]):
                owed = jnp.where(next_side, with_next[lead + slot, i], with_last[slot, i])
                total = part[k, m, i] + owed.astype(jnp.float32)
                if remote:
                    far = (with_next, refs[0])[k]
                    total += far[m, i].astype(jnp.float32)
                outs[m][k, i] = jnp.transpose(total.astype(jnp.bfloat16))


def combine(place, part, owed):
    group, _, *rest = part.shape
    return pl.pallas_call(
        functools.partial(combine_kernel, remote=len(owed) - 2),
        in_specs=[SMEM] + [VMEM] * (1 + len(owed)),
        out_specs=[VMEM] * PLANE,
        out_shape=[jax.ShapeDtypeStruct((group, *rest), jnp.bfloat16)] * PLANE,
        compiler_params=LIMIT,
        cost_estimate=moved_cost([part, *owed]),
    )(place, part, *owed)


def partner(value, axis, apart):
    return lax.ppermute(value, axis, [(i, i ^ 1 << apart) for i in range(lax.axis_size(axis))])


def passed_along(value, axis, by):
    peers = lax.axis_size(axis)
    pairs = [(i, i + by) for i in range(peers) if 0 <= i + by < peers]
    return lax.ppermute(value, axis, pairs)


def to_slots(values, picker):
    return jnp.sum(jnp.where(picker[None, :, :, None], values[:, None, :, :], 0.0), axis=2)


def slots_to_heads(values, picker, filler):
    covered = jnp.any(picker, axis=0)
    summed = jnp.sum(jnp.where(picker[None, :, :, None], values[:, :, None, :], 0.0), axis=1)
    return jnp.where(covered[None, :, None], summed, filler)


def rows_slots_to_heads(values, picker):
    return jnp.einsum(
        "jqid,ih->jqhd", values, picker.astype(jnp.float32), precision=lax.Precision.HIGHEST
    )


def pick_heads(values, picker):
    chooser = picker.astype(jnp.bfloat16)
    return jnp.einsum("ih,jqhd->jqid", chooser, values, preferred_element_type=jnp.float32).astype(
        jnp.bfloat16
    )


def partner_route(values, section_index, low_bits):
    return partner(values, "seq", section_index - low_bits)


def partner_back(values, section_index, low_bits):
    return partner(values, "seq", section_index - low_bits)


def extend_blocks(values, reach, halo_blocks, blocks_dev, mover):
    pieces = [mover(values, distance) for distance in range(reach, 0, -1)]
    pieces = pieces + [values] + [mover(values, -distance) for distance in range(1, reach + 1)]
    start = reach * blocks_dev - halo_blocks
    whole = jnp.concatenate(pieces, axis=1)
    return whole


def move_keys(values, distance):
    return passed_along(values, "seq", distance)


def window_sets(extended, blocks_dev, spread):
    return jnp.stack(
        [extended[:, offset : offset + blocks_dev] for offset in range(spread)], axis=2
    )


def per_device(query_rows, key_rows, value_rows, out_grad, window_blocks, section_heads):
    tokens_dev, head_count, head_width = query_rows.shape
    blocks_dev = tokens_dev // BLK
    low_bits = blocks_dev.bit_length() - 1
    seq_count = lax.axis_size("seq")
    section_total = low_bits + seq_count.bit_length() - 1
    halo_blocks = WB - 1
    reach = (halo_blocks + blocks_dev - 1) // blocks_dev
    padding = reach * blocks_dev
    spread = 2 * WB - 1
    score_scale = 1.0 / math.sqrt(head_width)
    first_block = lax.axis_index("seq") * blocks_dev + jnp.arange(blocks_dev, dtype=jnp.int32)
    all_blocks = blocks_dev * seq_count
    query_blocks = query_rows.reshape(blocks_dev, BLK, head_count, head_width)
    key_blocks = key_rows.reshape(blocks_dev, BLK, head_count, head_width)
    value_blocks = value_rows.reshape(blocks_dev, BLK, head_count, head_width)
    grad_blocks = out_grad.reshape(blocks_dev, BLK, head_count, head_width)
    offsets = jnp.arange(spread, dtype=jnp.int32) - halo_blocks
    near_block = first_block[:, None] + offsets[None, :]
    in_range = (near_block >= 0) & (near_block < all_blocks)
    near_mask = in_range[:, None, :] & (
        jnp.abs(offsets)[None, None, :] < window_blocks[None, :, None]
    )
    wide_mask = near_mask[:, :, None, :, None]
    head_ids = jnp.arange(head_count, dtype=jnp.int32)
    paired = jnp.stack([key_blocks, value_blocks])
    extended = extend_blocks(paired, reach, halo_blocks, blocks_dev, move_keys)
    near_sets = window_sets(extended, blocks_dev, spread)
    near_keys = near_sets[0]
    near_values = near_sets[1]
    near_scores = (
        jnp.einsum("jqhd,jckhd->jhqck", query_blocks, near_keys, preferred_element_type=jnp.float32)
        * score_scale
    )
    near_scores = jnp.where(wide_mask, near_scores, blocked_score)
    top_score = jnp.max(near_scores, axis=(3, 4))
    records = []
    for section_index in range(section_total):
        picker = section_heads[section_index][:, None] == head_ids[None, :]
        slot_width = jnp.sum(jnp.where(picker, window_blocks[None, :], 0), axis=1)
        slot_valid = 2**section_index >= slot_width
        chosen_query = pick_heads(query_blocks, picker)
        chosen_grad = pick_heads(grad_blocks, picker)
        chosen_pair = jnp.stack([pick_heads(key_blocks, picker), pick_heads(value_blocks, picker)])
        partner_pair = partner_route(chosen_pair, section_index, low_bits)
        far_scores = (
            jnp.einsum(
                "jqid,jkid->jiqk", chosen_query, partner_pair[0], preferred_element_type=jnp.float32
            )
            * score_scale
        )
        far_scores = jnp.where(slot_valid[None, :, None, None], far_scores, blocked_score)
        top_score = jnp.maximum(
            top_score, slots_to_heads(jnp.max(far_scores, axis=3), picker, blocked_score)
        )
        records.append(
            (
                section_index,
                picker,
                slot_valid,
                chosen_query,
                chosen_grad,
                chosen_pair,
                partner_pair,
                far_scores,
            )
        )
    row_total = jnp.sum(
        jnp.where(wide_mask, jnp.exp(near_scores - top_score[:, :, :, None, None]), 0.0),
        axis=(3, 4),
    )
    for record in records:
        picker = record[1]
        slot_top = to_slots(top_score, picker)
        far_sum = jnp.sum(
            jnp.where(
                record[2][None, :, None, None], jnp.exp(record[7] - slot_top[:, :, :, None]), 0.0
            ),
            axis=3,
        )
        row_total = row_total + slots_to_heads(far_sum, picker, 0.0)
    log_total = top_score + jnp.log(row_total)
    near_probs = jnp.where(
        wide_mask, jnp.exp(near_scores - log_total[:, :, :, None, None]), 0.0
    ).astype(jnp.bfloat16)
    attended_sum = jnp.einsum(
        "jhqck,jckhd->jqhd", near_probs, near_values, preferred_element_type=jnp.float32
    )
    far_probs_list = []
    for record in records:
        picker = record[1]
        slot_lse = to_slots(log_total, picker)
        far_probs = jnp.where(
            record[2][None, :, None, None], jnp.exp(record[7] - slot_lse[:, :, :, None]), 0.0
        ).astype(jnp.bfloat16)
        far_probs_list.append((far_probs, slot_lse))
        attended_sum = attended_sum + rows_slots_to_heads(
            jnp.einsum(
                "jiqk,jkid->jqid", far_probs, record[6][1], preferred_element_type=jnp.float32
            ),
            picker,
        )
    attended = attended_sum.astype(jnp.bfloat16)
    row_delta = jnp.transpose(
        jnp.sum(grad_blocks.astype(jnp.float32) * attended.astype(jnp.float32), axis=-1), (0, 2, 1)
    )
    near_dprob = jnp.einsum(
        "jqhd,jckhd->jhqck", grad_blocks, near_values, preferred_element_type=jnp.float32
    )
    near_dscore = (
        near_probs.astype(jnp.float32) * (near_dprob - row_delta[:, :, :, None, None])
    ).astype(jnp.bfloat16)
    query_sum = jnp.einsum(
        "jhqck,jckhd->jqhd", near_dscore, near_keys, preferred_element_type=jnp.float32
    )
    far_dscores = []
    for record, probs_pair in zip(records, far_probs_list):
        picker = record[1]
        slot_delta = to_slots(row_delta, picker)
        far_dprob = jnp.einsum(
            "jqid,jkid->jiqk", record[4], record[6][1], preferred_element_type=jnp.float32
        )
        far_dscore = (
            probs_pair[0].astype(jnp.float32) * (far_dprob - slot_delta[:, :, :, None])
        ).astype(jnp.bfloat16)
        far_dscores.append((far_dscore, slot_delta))
        query_sum = query_sum + rows_slots_to_heads(
            jnp.einsum(
                "jiqk,jkid->jqid", far_dscore, record[6][0], preferred_element_type=jnp.float32
            ),
            picker,
        )
    query_grad = (
        (query_sum * score_scale).astype(jnp.bfloat16).reshape(tokens_dev, head_count, head_width)
    )
    near_key_part = (
        jnp.einsum(
            "jhqck,jqhd->jckhd", near_dscore, query_blocks, preferred_element_type=jnp.float32
        )
        * score_scale
    )
    near_value_part = jnp.einsum(
        "jhqck,jqhd->jckhd", near_probs, grad_blocks, preferred_element_type=jnp.float32
    )
    stacked_parts = jnp.stack([near_key_part, near_value_part])
    extended_count = blocks_dev + 2 * padding
    base = padding - halo_blocks
    extended_ids = jnp.arange(extended_count, dtype=jnp.int32)
    own_ids = jnp.arange(blocks_dev, dtype=jnp.int32)
    spread_ids = jnp.arange(spread, dtype=jnp.int32)
    placer = (
        extended_ids[:, None, None] == base + own_ids[None, :, None] + spread_ids[None, None, :]
    ).astype(jnp.float32)
    gathered = jnp.einsum(
        "ejc,xjckhd->xekhd", placer, stacked_parts, precision=lax.Precision.HIGHEST
    )
    own_grads = gathered[:, padding : padding + blocks_dev]
    for distance in range(1, reach + 1):
        lower_slab = gathered[
            :, padding - distance * blocks_dev : padding - (distance - 1) * blocks_dev
        ]
        own_grads = own_grads + passed_along(
            lower_slab.astype(jnp.bfloat16), "seq", -distance
        ).astype(lower_slab.dtype)
        upper_start = padding + blocks_dev + (distance - 1) * blocks_dev
        upper_slab = gathered[:, upper_start : upper_start + blocks_dev]
        own_grads = own_grads + passed_along(
            upper_slab.astype(jnp.bfloat16), "seq", distance
        ).astype(upper_slab.dtype)
    for record, probs_pair, dscore_pair in zip(records, far_probs_list, far_dscores):
        picker = record[1]
        key_part = (
            jnp.einsum(
                "jiqk,jqid->jkid", dscore_pair[0], record[3], preferred_element_type=jnp.float32
            )
            * score_scale
        )
        value_part = jnp.einsum(
            "jiqk,jqid->jkid", probs_pair[0], record[4], preferred_element_type=jnp.float32
        )
        returned = partner_back(jnp.stack([key_part, value_part]), record[0], low_bits)
        own_grads = own_grads + jnp.stack(
            [rows_slots_to_heads(returned[0], picker), rows_slots_to_heads(returned[1], picker)]
        )
    key_grad = own_grads[0].astype(jnp.bfloat16).reshape(tokens_dev, head_count, head_width)
    value_grad = own_grads[1].astype(jnp.bfloat16).reshape(tokens_dev, head_count, head_width)
    return (attended.reshape(tokens_dev, head_count, head_width), query_grad, key_grad, value_grad)


def in_plane(pieces):
    peers = lax.axis_size("seq")
    return [pieces[0]] + [
        lax.ppermute(pieces[m], "seq", [(i, i ^ m) for i in range(peers)])
        for m in range(1, PLANE)
    ]


def with_next_plane(value):
    return partner(value, "seq", PLANE.bit_length() - 1)


def with_other_plane(value):
    return partner(value, "seq", PLANE.bit_length())


def with_last_plane(value):
    peers = lax.axis_size("seq")
    pairs = []
    for i in range(peers):
        other = i + PLANE if i // PLANE % 2 else i - PLANE
        if 0 <= other < peers:
            pairs.append((i, other))
    return lax.ppermute(value, "seq", pairs)


def plane_all_to_all(value):
    peers = lax.axis_size("seq")
    planes = [list(range(i, i + PLANE)) for i in range(0, peers, PLANE)]
    return lax.all_to_all(value, "seq", 0, 0, axis_index_groups=planes, tiled=True)


def sharded_by_plane(query_rows, key_rows, value_rows, out_grad, widths, sections):
    position = lax.axis_index("seq").astype(jnp.int32)
    place = jnp.stack([position % PLANE, position // PLANE])
    blocks = lax.axis_size("seq")
    local = PLANE.bit_length() - 1
    total = sections.shape[0]
    groups = [tuple(range(local, total)), tuple(range(local))]
    order = tuple(s for group in groups for s in group)
    tables = (place, widths, sections)
    sent = pack(place, sections, [key_rows, value_rows], order, True)
    (graded_sent,) = pack(place, sections, [query_rows, out_grad], order, False)
    graded = plane_all_to_all(graded_sent)
    pairs = in_plane(sent)
    next_sent, last_sent = halo_parts(place, pairs)
    far_sent = far_parts(pairs, total - local)
    halos = (with_next_plane(next_sent), with_last_plane(last_sent))
    far = (with_next_plane(far_sent[0]), with_other_plane(far_sent[1]))
    rows, part_near, owed = attend(
        *tables, pairs, graded, halos, (), local, 0, total - local, blocks
    )
    owed_near = [with_next_plane(owed[0]), with_last_plane(owed[1])]
    rows, part_far, owed = attend(
        *tables, pairs, graded, halos, far, total - local, local, 0, blocks, (rows,)
    )
    near = combine(place, part_near, owed_near)
    owed, near, rows = lax.optimization_barrier((owed, near, rows))
    other_back = with_other_plane(owed[2])
    owed_far = [with_next_plane(owed[0]), with_last_plane(owed[1]), other_back]
    near = in_plane(near)
    rows = plane_all_to_all(rows)
    columns = in_plane(combine(place, part_far, owed_far)) + near
    attended, query_grad = unpack(
        place, sections, functools.partial(unpack_kernel, order=order), [rows]
    )
    key_grad, value_grad = unpack(
        place, sections, functools.partial(unpack_crossed_kernel, groups=groups), columns
    )
    return attended, query_grad, key_grad, value_grad


def solution(mesh):
    spec = P(("grp", "seq"), None, None)
    peers = mesh.shape["seq"]

    def per_device_any(*args):
        tokens, heads, width = args[0].shape
        sections, listed = args[5].shape
        once = sections * listed == heads
        if tokens == BLK and once and listed == PLANE and 1 << sections == peers == PLANE**2:
            return sharded_by_plane(*args)
        return per_device(*args)

    return jax.shard_map(
        per_device_any,
        mesh=mesh,
        in_specs=(spec, spec, spec, spec, P(), P()),
        out_specs=(spec,) * 4,
        check_vma=False,
    )
```

```python
import functools
import math

import jax
import jax.numpy as jnp
from jax import lax
from jax.experimental import pallas as pl
from jax.experimental.pallas import tpu as pltpu
from jax.sharding import PartitionSpec as P

BLK = 128
WB = 3
HALO = WB - 1
SPAN = (2 * HALO + 1) * BLK
LINKED = SPAN + BLK
PLANE = 2 * HALO
PADDED = PLANE + 2 * HALO
NT = (((1,), (1,)), ((), ()))
NN = (((1,), (0,)), ((), ()))
blocked_score = -1e30


def mm(a, b, dims=NN):
    return lax.dot_general(a, b, dims, preferred_element_type=jnp.float32)


def moved_cost(arrays):
    return pl.CostEstimate(
        flops=0, transcendentals=0, bytes_accessed=4 * sum(a.size for a in arrays)
    )


def softmax_pair(score, far_score, biases, far_bias, scale2):
    near_parts, far_parts = [], []
    gap = jnp.zeros((BLK, BLK), jnp.bfloat16)
    for r in range(2):
        rows = slice(r * BLK, (r + 1) * BLK)
        sw = score[rows, r * BLK : r * BLK + SPAN] * scale2 + biases[r]
        sf = far_score[r] * scale2 + far_bias
        top = jnp.maximum(jnp.max(sw, axis=1, keepdims=True), jnp.max(sf, axis=1, keepdims=True))
        ew, ef = jnp.exp2(sw - top), jnp.exp2(sf - top)
        total = jnp.sum(ew, axis=1, keepdims=True) + jnp.sum(ef, axis=1, keepdims=True)
        inverse = 1.0 / total
        near = (ew * inverse).astype(jnp.bfloat16)
        near_parts.append(jnp.concatenate([near, gap] if r == 0 else [gap, near], axis=1))
        far_parts.append((ef * inverse).astype(jnp.bfloat16))
    return jnp.concatenate(near_parts, axis=0), far_parts


def attend_pair(q, g, kw, vw, kf, vf, biases, far_bias):
    scale = 1.0 / math.sqrt(q.shape[-1])
    scale2 = scale * math.log2(math.e)
    half = [slice(0, BLK), slice(BLK, 2 * BLK)]
    far_score = [mm(q[half[r]], kf[r], NT) for r in range(2)]
    near, far = softmax_pair(mm(q, kw, NT), far_score, biases, far_bias, scale2)
    far_out = jnp.concatenate([mm(far[r], vf[r]) for r in range(2)], axis=0)
    attended = (mm(near, vw) + far_out).astype(jnp.bfloat16)
    delta = jnp.sum(g.astype(jnp.float32) * attended.astype(jnp.float32), axis=1, keepdims=True)
    d_near = (near.astype(jnp.float32) * (mm(g, vw, NT) - delta)).astype(jnp.bfloat16)
    d_far = [
        (far[r].astype(jnp.float32) * (mm(g[half[r]], vf[r], NT) - delta[half[r]])).astype(
            jnp.bfloat16
        )
        for r in range(2)
    ]
    far_dq = jnp.concatenate([mm(d_far[r], kf[r]) for r in range(2)], axis=0)
    query_grad = ((mm(d_near, kw) + far_dq) * scale).astype(jnp.bfloat16)
    qt, gt = jnp.transpose(q), jnp.transpose(g)
    key_near, value_near = mm(qt, d_near), mm(gt, near)
    key_far = [mm(qt[:, half[r]], d_far[r]) for r in range(2)]
    value_far = [mm(gt[:, half[r]], far[r]) for r in range(2)]
    return attended, query_grad, key_near, value_near, key_far, value_far


def near_biases(b, width, low, high):
    offset = lax.broadcasted_iota(jnp.int32, (1, SPAN), 1) // BLK - HALO
    inside = jnp.abs(offset) < width
    out = []
    for r in range(2):
        there = offset + b + r
        out.append(jnp.where(inside & (there >= low) & (there < high), 0.0, blocked_score))
    return out


def rows_of(block):
    return pl.ds(pl.multiple_of(block * BLK, BLK), BLK)


def whole(shape):
    return pl.BlockSpec(shape, lambda *_: (0,) * len(shape))


SMEM = pl.BlockSpec(memory_space=pltpu.SMEM)
VMEM = pl.BlockSpec(memory_space=pltpu.VMEM)
LIMIT = pltpu.CompilerParams(vmem_limit_bytes=20 << 20)


def pack_kernel(place, sections, *refs, order, count, crossed):
    ins, outs, held = refs[:count], refs[count:-1], refs[-1]
    for i in range(count):
        held[i] = jnp.transpose(ins[i][...], (1, 0, 2))
    for m in range(PLANE):
        owner = place[0] ^ m if crossed else m
        for k, s in enumerate(order):
            head = sections[s, owner]
            for i in range(count):
                if crossed:
                    outs[m][k, i] = held[i, head]
                else:
                    outs[0][m, k, i] = held[i, head]


def pack(place, sections, arrays, order, crossed):
    tokens, heads, width = arrays[0].shape
    chunk = tokens // 2
    count = len(arrays)
    shape = (len(order), count, tokens, width)
    if crossed:
        shapes = [shape] * PLANE
        specs = [pl.BlockSpec((*shape[:2], chunk, width), lambda i: (0, 0, i, 0))] * PLANE
    else:
        shapes = [(PLANE, *shape)]
        specs = [pl.BlockSpec((PLANE, *shape[:2], chunk, width), lambda i: (0, 0, 0, i, 0))]
    return pl.pallas_call(
        functools.partial(pack_kernel, order=order, count=count, crossed=crossed),
        grid=(tokens // chunk,),
        in_specs=[SMEM, SMEM]
        + [pl.BlockSpec((chunk, heads, width), lambda i: (i, 0, 0))] * count,
        out_specs=specs,
        out_shape=[jax.ShapeDtypeStruct(shape, jnp.bfloat16) for shape in shapes],
        scratch_shapes=[pltpu.VMEM((count, heads, chunk, width), jnp.bfloat16)],
        cost_estimate=moved_cost(arrays),
    )(place, sections, *arrays)


def unpack_crossed_kernel(place, sections, *refs, groups, count):
    pieces, outs, held = refs[: len(groups) * PLANE], refs[len(groups) * PLANE : -1], refs[-1]
    for number, group in enumerate(groups):
        for m in range(PLANE):
            for k, s in enumerate(group):
                head = sections[s, place[0] ^ m]
                for i in range(count):
                    held[i, head] = pieces[number * PLANE + m][k, i]
    for i in range(count):
        outs[i][...] = jnp.transpose(held[i], (1, 0, 2))


def unpack_kernel(place, sections, src, *refs, order, count):
    outs, held = refs[:-1], refs[-1]
    for m in range(PLANE):
        for k, s in enumerate(order):
            head = sections[s, m]
            for i in range(count):
                held[i, head] = src[m, k, i]
    for i in range(count):
        outs[i][...] = jnp.transpose(held[i], (1, 0, 2))


def unpack(place, sections, kernel, pieces):
    *lead, count, tokens, width = pieces[0].shape
    heads = sections.size
    chunk = tokens // 2
    return pl.pallas_call(
        functools.partial(kernel, count=count),
        grid=(tokens // chunk,),
        in_specs=[SMEM, SMEM]
        + [
            pl.BlockSpec(
                (*piece.shape[:-2], chunk, width),
                lambda i, zeros=(0,) * (piece.ndim - 2): (*zeros, i, 0),
            )
            for piece in pieces
        ],
        out_specs=[pl.BlockSpec((chunk, heads, width), lambda i: (i, 0, 0))] * count,
        out_shape=[jax.ShapeDtypeStruct((tokens, heads, width), jnp.bfloat16)] * count,
        scratch_shapes=[pltpu.VMEM((count, heads, chunk, width), jnp.bfloat16)],
        compiler_params=LIMIT,
        cost_estimate=moved_cost(pieces),
    )(place, sections, *pieces)


def facing(place):
    return place[0] // HALO == 1 - place[1] % 2


def far_kernel(*refs):
    pieces, outs = refs[:PLANE], refs[PLANE:]
    for k, out in enumerate(outs):
        for m, piece in enumerate(pieces):
            out[m] = piece[k]


def far_parts(pieces, count):
    rest = pieces[0].shape[1:]
    return pl.pallas_call(
        far_kernel,
        in_specs=[VMEM] * PLANE,
        out_specs=[VMEM] * count,
        out_shape=[jax.ShapeDtypeStruct((PLANE, *rest), jnp.bfloat16)] * count,
        compiler_params=LIMIT,
        cost_estimate=moved_cost(pieces),
    )(*pieces)


def halo_kernel(place, *refs):
    pieces, (with_next, with_last) = refs[:PLANE], refs[PLANE:]
    slots = pieces[0].shape[0]

    def fill(base, other):
        for m in range(HALO):
            with_next[m * slots : (m + 1) * slots] = pieces[base + m][...]
            with_last[m * slots : (m + 1) * slots] = pieces[other + m][...]

    @pl.when(facing(place))
    def _():
        fill(0, HALO)

    @pl.when(jnp.logical_not(facing(place)))
    def _():
        fill(HALO, 0)


def halo_parts(place, pieces):
    slots, *rest = pieces[0].shape
    return pl.pallas_call(
        halo_kernel,
        in_specs=[SMEM] + [VMEM] * PLANE,
        out_specs=[VMEM] * 2,
        out_shape=[jax.ShapeDtypeStruct((HALO * slots, *rest), jnp.bfloat16)] * 2,
        compiler_params=LIMIT,
        cost_estimate=moved_cost(pieces),
    )(place, *pieces)


def attend_kernel(place, widths, sections, *refs, first, slot, group, remote, blocks, aliased):
    pairs, (graded, with_next, with_last) = refs[:PLANE], refs[PLANE : PLANE + 3]
    rest = refs[PLANE + 3 :]
    if remote:
        far_in, rest = rest[:2], rest[2:]
    rest = rest[aliased:]
    rows, rest = rest[:PLANE], rest[PLANE:]
    (part, to_next, to_last), rest = rest[:3], rest[3:]
    if remote:
        to_other, rest = rest[0], rest[1:]
    keys, values, far_keys, far_values, attended, dq = rest[:6]
    accs, far_accs = rest[6:8], rest[8:10]
    me = place[0]
    scales = (1.0 / math.sqrt(keys.shape[-1]), 1.0)
    lead = PLANE if remote else 0
    slots = with_next.shape[0] // HALO
    next_at = jnp.where(place[1] % 2 == 0, HALO + PLANE, 0)
    last_at = HALO + PLANE - next_at
    for k in range(group):
        width = widths[sections[first + k, me]]
        bit = 1 << first + k
        far_bias = jnp.where(bit >= width, 0.0, blocked_score).astype(jnp.float32)
        for m in range(PLANE):
            keys[rows_of(HALO + (me ^ m))] = pairs[m][slot + k, 0]
            values[rows_of(HALO + (me ^ m))] = pairs[m][slot + k, 1]
        for m in range(HALO):
            b = (me % HALO) ^ m
            at = m * slots + slot + k
            keys[rows_of(next_at + b)] = with_next[at, 0]
            values[rows_of(next_at + b)] = with_next[at, 1]
            keys[rows_of(last_at + b)] = with_last[at, 0]
            values[rows_of(last_at + b)] = with_last[at, 1]
        if remote:
            for m in range(PLANE):
                far_keys[rows_of(me ^ m)] = far_in[k][m, 0]
                far_values[rows_of(me ^ m)] = far_in[k][m, 1]
        for acc in accs:
            acc[...] = jnp.zeros_like(acc)
        for b in range(0, PLANE, 2):
            own = slice(b * BLK, (b + 2) * BLK)
            seen = slice(b * BLK, (b + 2 * HALO + 2) * BLK)
            one = [slice((b + r) * BLK, (b + r + 1) * BLK) for r in range(2)]
            if remote:
                kf, vf = [[ref[at] for at in one] for ref in (far_keys, far_values)]
            else:
                there = [HALO + ((b + r) ^ bit) for r in range(2)]
                kf, vf = [
                    [ref[at * BLK : (at + 1) * BLK] for at in there] for ref in (keys, values)
                ]
            o, d, key_near, value_near, key_far, value_far = attend_pair(
                jnp.concatenate([graded[b, slot + k, 0], graded[b + 1, slot + k, 0]], axis=0),
                jnp.concatenate([graded[b, slot + k, 1], graded[b + 1, slot + k, 1]], axis=0),
                keys[seen],
                values[seen],
                kf,
                vf,
                near_biases(place[1] * PLANE + b, width, 0, blocks),
                far_bias,
            )
            attended[own] = o
            dq[own] = d
            for acc, near in zip(accs, (key_near, value_near)):
                acc[:, seen] += near
            for acc, far_acc, far in zip(accs, far_accs, (key_far, value_far)):
                for r in range(2):
                    if remote:
                        far_acc[:, one[r]] = far[r]
                    else:
                        acc[:, there[r] * BLK : (there[r] + 1) * BLK] += far[r]
        for i, (acc, far_acc) in enumerate(zip(accs, far_accs)):
            if remote:
                target = (to_next, to_other)[k]
                for m in range(PLANE):
                    owed = far_acc[:, rows_of(me ^ m)] * scales[i]
                    target[m, i] = owed.astype(jnp.bfloat16)
            for m in range(PLANE):
                part[k, m, i] = acc[:, rows_of(HALO + (me ^ m))] * scales[i]
            for m in range(HALO):
                b = (me % HALO) ^ m
                at = m * group + k
                to_next[lead + at, i] = (acc[:, rows_of(next_at + b)] * scales[i]).astype(
                    jnp.bfloat16
                )
                to_last[at, i] = (acc[:, rows_of(last_at + b)] * scales[i]).astype(jnp.bfloat16)
        for m in range(PLANE):
            rows[m][slot + k, 0] = attended[rows_of(me ^ m)]
            rows[m][slot + k, 1] = dq[rows_of(me ^ m)]


def attend(place, widths, sections, pairs, graded, halos, far, group, first, slot, blocks, rows=()):
    count, _, width = pairs[0].shape[1:]
    tile = (BLK, width)
    remote = len(far)
    bf16 = jnp.bfloat16
    owed = [(HALO * group + (PLANE if remote else 0), count, *tile), (HALO * group, count, *tile)]
    if remote:
        owed.append((PLANE, count, *tile))
    inputs = (*pairs, graded, *halos, *far, *rows)
    outs = pl.pallas_call(
        functools.partial(
            attend_kernel,
            first=first,
            slot=slot,
            group=group,
            remote=remote,
            blocks=blocks,
            aliased=len(rows),
        ),
        in_specs=[SMEM] * 3 + [VMEM] * len(inputs),
        out_specs=[VMEM] * (PLANE + 1 + len(owed)),
        out_shape=[jax.ShapeDtypeStruct(pairs[0].shape, bf16)] * PLANE
        + [jax.ShapeDtypeStruct((group, PLANE, count, *tile), jnp.float32)]
        + [jax.ShapeDtypeStruct(shape, bf16) for shape in owed],
        scratch_shapes=[pltpu.VMEM((PADDED * BLK, width), bf16)] * 2
        + [pltpu.VMEM((PLANE * BLK, width), bf16)] * 4
        + [pltpu.VMEM((width, PADDED * BLK), jnp.float32)] * 2
        + [pltpu.VMEM((width, PLANE * BLK), jnp.float32)] * 2,
        input_output_aliases={3 + len(inputs) - len(rows) + m: m for m in range(len(rows))},
        compiler_params=LIMIT,
        cost_estimate=pl.CostEstimate(
            flops=group * PLANE * 12 * BLK * LINKED * width,
            transcendentals=group * PLANE * BLK * LINKED,
            bytes_accessed=40 * group * PLANE * BLK * width,
        ),
    )(place, widths, sections, *inputs)
    return outs[:PLANE], outs[PLANE], outs[PLANE + 1 :]


def combine_kernel(place, part, with_next, with_last, *refs, remote):
    outs = refs[remote:]
    group = part.shape[0]
    lead = PLANE if remote else 0
    for m in range(PLANE):
        own_chip = m < HALO
        next_side = facing(place) if own_chip else jnp.logical_not(facing(place))
        for k in range(group):
            slot = (m % HALO) * group + k
            for i in range(part.shape[2]):
                owed = jnp.where(next_side, with_next[lead + slot, i], with_last[slot, i])
                total = part[k, m, i] + owed.astype(jnp.float32)
                if remote:
                    far = (with_next, refs[0])[k]
                    total += far[m, i].astype(jnp.float32)
                outs[m][k, i] = jnp.transpose(total.astype(jnp.bfloat16))


def combine(place, part, owed):
    group, _, *rest = part.shape
    return pl.pallas_call(
        functools.partial(combine_kernel, remote=len(owed) - 2),
        in_specs=[SMEM] + [VMEM] * (1 + len(owed)),
        out_specs=[VMEM] * PLANE,
        out_shape=[jax.ShapeDtypeStruct((group, *rest), jnp.bfloat16)] * PLANE,
        compiler_params=LIMIT,
        cost_estimate=moved_cost([part, *owed]),
    )(place, part, *owed)


def partner(value, axis, apart):
    return lax.ppermute(value, axis, [(i, i ^ 1 << apart) for i in range(lax.axis_size(axis))])


def passed_along(value, axis, by):
    peers = lax.axis_size(axis)
    pairs = [(i, i + by) for i in range(peers) if 0 <= i + by < peers]
    return lax.ppermute(value, axis, pairs)


def to_slots(values, picker):
    return jnp.sum(jnp.where(picker[None, :, :, None], values[:, None, :, :], 0.0), axis=2)


def slots_to_heads(values, picker, filler):
    covered = jnp.any(picker, axis=0)
    summed = jnp.sum(jnp.where(picker[None, :, :, None], values[:, :, None, :], 0.0), axis=1)
    return jnp.where(covered[None, :, None], summed, filler)


def rows_slots_to_heads(values, picker):
    return jnp.einsum(
        "jqid,ih->jqhd", values, picker.astype(jnp.float32), precision=lax.Precision.HIGHEST
    )


def pick_heads(values, picker):
    chooser = picker.astype(jnp.bfloat16)
    return jnp.einsum("ih,jqhd->jqid", chooser, values, preferred_element_type=jnp.float32).astype(
        jnp.bfloat16
    )


def partner_route(values, section_index, low_bits):
    return partner(values, "seq", section_index - low_bits)


def partner_back(values, section_index, low_bits):
    return partner(values, "seq", section_index - low_bits)


def extend_blocks(values, reach, halo_blocks, blocks_dev, mover):
    pieces = [mover(values, distance) for distance in range(reach, 0, -1)]
    pieces = pieces + [values] + [mover(values, -distance) for distance in range(1, reach + 1)]
    start = reach * blocks_dev - halo_blocks
    whole = jnp.concatenate(pieces, axis=1)
    return whole


def move_keys(values, distance):
    return passed_along(values, "seq", distance)


def window_sets(extended, blocks_dev, spread):
    return jnp.stack(
        [extended[:, offset : offset + blocks_dev] for offset in range(spread)], axis=2
    )


def per_device(query_rows, key_rows, value_rows, out_grad, window_blocks, section_heads):
    tokens_dev, head_count, head_width = query_rows.shape
    blocks_dev = tokens_dev // BLK
    low_bits = blocks_dev.bit_length() - 1
    seq_count = lax.axis_size("seq")
    section_total = low_bits + seq_count.bit_length() - 1
    halo_blocks = WB - 1
    reach = (halo_blocks + blocks_dev - 1) // blocks_dev
    padding = reach * blocks_dev
    spread = 2 * WB - 1
    score_scale = 1.0 / math.sqrt(head_width)
    first_block = lax.axis_index("seq") * blocks_dev + jnp.arange(blocks_dev, dtype=jnp.int32)
    all_blocks = blocks_dev * seq_count
    query_blocks = query_rows.reshape(blocks_dev, BLK, head_count, head_width)
    key_blocks = key_rows.reshape(blocks_dev, BLK, head_count, head_width)
    value_blocks = value_rows.reshape(blocks_dev, BLK, head_count, head_width)
    grad_blocks = out_grad.reshape(blocks_dev, BLK, head_count, head_width)
    offsets = jnp.arange(spread, dtype=jnp.int32) - halo_blocks
    near_block = first_block[:, None] + offsets[None, :]
    in_range = (near_block >= 0) & (near_block < all_blocks)
    near_mask = in_range[:, None, :] & (
        jnp.abs(offsets)[None, None, :] < window_blocks[None, :, None]
    )
    wide_mask = near_mask[:, :, None, :, None]
    head_ids = jnp.arange(head_count, dtype=jnp.int32)
    paired = jnp.stack([key_blocks, value_blocks])
    extended = extend_blocks(paired, reach, halo_blocks, blocks_dev, move_keys)
    near_sets = window_sets(extended, blocks_dev, spread)
    near_keys = near_sets[0]
    near_values = near_sets[1]
    near_scores = (
        jnp.einsum("jqhd,jckhd->jhqck", query_blocks, near_keys, preferred_element_type=jnp.float32)
        * score_scale
    )
    near_scores = jnp.where(wide_mask, near_scores, blocked_score)
    top_score = jnp.max(near_scores, axis=(3, 4))
    records = []
    for section_index in range(section_total):
        picker = section_heads[section_index][:, None] == head_ids[None, :]
        slot_width = jnp.sum(jnp.where(picker, window_blocks[None, :], 0), axis=1)
        slot_valid = 2**section_index >= slot_width
        chosen_query = pick_heads(query_blocks, picker)
        chosen_grad = pick_heads(grad_blocks, picker)
        chosen_pair = jnp.stack([pick_heads(key_blocks, picker), pick_heads(value_blocks, picker)])
        partner_pair = partner_route(chosen_pair, section_index, low_bits)
        far_scores = (
            jnp.einsum(
                "jqid,jkid->jiqk", chosen_query, partner_pair[0], preferred_element_type=jnp.float32
            )
            * score_scale
        )
        far_scores = jnp.where(slot_valid[None, :, None, None], far_scores, blocked_score)
        top_score = jnp.maximum(
            top_score, slots_to_heads(jnp.max(far_scores, axis=3), picker, blocked_score)
        )
        records.append(
            (
                section_index,
                picker,
                slot_valid,
                chosen_query,
                chosen_grad,
                chosen_pair,
                partner_pair,
                far_scores,
            )
        )
    row_total = jnp.sum(
        jnp.where(wide_mask, jnp.exp(near_scores - top_score[:, :, :, None, None]), 0.0),
        axis=(3, 4),
    )
    for record in records:
        picker = record[1]
        slot_top = to_slots(top_score, picker)
        far_sum = jnp.sum(
            jnp.where(
                record[2][None, :, None, None], jnp.exp(record[7] - slot_top[:, :, :, None]), 0.0
            ),
            axis=3,
        )
        row_total = row_total + slots_to_heads(far_sum, picker, 0.0)
    log_total = top_score + jnp.log(row_total)
    near_probs = jnp.where(
        wide_mask, jnp.exp(near_scores - log_total[:, :, :, None, None]), 0.0
    ).astype(jnp.bfloat16)
    attended_sum = jnp.einsum(
        "jhqck,jckhd->jqhd", near_probs, near_values, preferred_element_type=jnp.float32
    )
    far_probs_list = []
    for record in records:
        picker = record[1]
        slot_lse = to_slots(log_total, picker)
        far_probs = jnp.where(
            record[2][None, :, None, None], jnp.exp(record[7] - slot_lse[:, :, :, None]), 0.0
        ).astype(jnp.bfloat16)
        far_probs_list.append((far_probs, slot_lse))
        attended_sum = attended_sum + rows_slots_to_heads(
            jnp.einsum(
                "jiqk,jkid->jqid", far_probs, record[6][1], preferred_element_type=jnp.float32
            ),
            picker,
        )
    attended = attended_sum.astype(jnp.bfloat16)
    row_delta = jnp.transpose(
        jnp.sum(grad_blocks.astype(jnp.float32) * attended.astype(jnp.float32), axis=-1), (0, 2, 1)
    )
    near_dprob = jnp.einsum(
        "jqhd,jckhd->jhqck", grad_blocks, near_values, preferred_element_type=jnp.float32
    )
    near_dscore = (
        near_probs.astype(jnp.float32) * (near_dprob - row_delta[:, :, :, None, None])
    ).astype(jnp.bfloat16)
    query_sum = jnp.einsum(
        "jhqck,jckhd->jqhd", near_dscore, near_keys, preferred_element_type=jnp.float32
    )
    far_dscores = []
    for record, probs_pair in zip(records, far_probs_list):
        picker = record[1]
        slot_delta = to_slots(row_delta, picker)
        far_dprob = jnp.einsum(
            "jqid,jkid->jiqk", record[4], record[6][1], preferred_element_type=jnp.float32
        )
        far_dscore = (
            probs_pair[0].astype(jnp.float32) * (far_dprob - slot_delta[:, :, :, None])
        ).astype(jnp.bfloat16)
        far_dscores.append((far_dscore, slot_delta))
        query_sum = query_sum + rows_slots_to_heads(
            jnp.einsum(
                "jiqk,jkid->jqid", far_dscore, record[6][0], preferred_element_type=jnp.float32
            ),
            picker,
        )
    query_grad = (
        (query_sum * score_scale).astype(jnp.bfloat16).reshape(tokens_dev, head_count, head_width)
    )
    near_key_part = (
        jnp.einsum(
            "jhqck,jqhd->jckhd", near_dscore, query_blocks, preferred_element_type=jnp.float32
        )
        * score_scale
    )
    near_value_part = jnp.einsum(
        "jhqck,jqhd->jckhd", near_probs, grad_blocks, preferred_element_type=jnp.float32
    )
    stacked_parts = jnp.stack([near_key_part, near_value_part])
    extended_count = blocks_dev + 2 * padding
    base = padding - halo_blocks
    extended_ids = jnp.arange(extended_count, dtype=jnp.int32)
    own_ids = jnp.arange(blocks_dev, dtype=jnp.int32)
    spread_ids = jnp.arange(spread, dtype=jnp.int32)
    placer = (
        extended_ids[:, None, None] == base + own_ids[None, :, None] + spread_ids[None, None, :]
    ).astype(jnp.float32)
    gathered = jnp.einsum(
        "ejc,xjckhd->xekhd", placer, stacked_parts, precision=lax.Precision.HIGHEST
    )
    own_grads = gathered[:, padding : padding + blocks_dev]
    for distance in range(1, reach + 1):
        lower_slab = gathered[
            :, padding - distance * blocks_dev : padding - (distance - 1) * blocks_dev
        ]
        own_grads = own_grads + passed_along(
            lower_slab.astype(jnp.bfloat16), "seq", -distance
        ).astype(lower_slab.dtype)
        upper_start = padding + blocks_dev + (distance - 1) * blocks_dev
        upper_slab = gathered[:, upper_start : upper_start + blocks_dev]
        own_grads = own_grads + passed_along(
            upper_slab.astype(jnp.bfloat16), "seq", distance
        ).astype(upper_slab.dtype)
    for record, probs_pair, dscore_pair in zip(records, far_probs_list, far_dscores):
        picker = record[1]
        key_part = (
            jnp.einsum(
                "jiqk,jqid->jkid", dscore_pair[0], record[3], preferred_element_type=jnp.float32
            )
            * score_scale
        )
        value_part = jnp.einsum(
            "jiqk,jqid->jkid", probs_pair[0], record[4], preferred_element_type=jnp.float32
        )
        returned = partner_back(jnp.stack([key_part, value_part]), record[0], low_bits)
        own_grads = own_grads + jnp.stack(
            [rows_slots_to_heads(returned[0], picker), rows_slots_to_heads(returned[1], picker)]
        )
    key_grad = own_grads[0].astype(jnp.bfloat16).reshape(tokens_dev, head_count, head_width)
    value_grad = own_grads[1].astype(jnp.bfloat16).reshape(tokens_dev, head_count, head_width)
    return (attended.reshape(tokens_dev, head_count, head_width), query_grad, key_grad, value_grad)


def in_plane(pieces):
    peers = lax.axis_size("seq")
    return [pieces[0]] + [
        lax.ppermute(pieces[m], "seq", [(i, i ^ m) for i in range(peers)])
        for m in range(1, PLANE)
    ]


def with_next_plane(value):
    return partner(value, "seq", PLANE.bit_length() - 1)


def with_other_plane(value):
    return partner(value, "seq", PLANE.bit_length())


def with_last_plane(value):
    peers = lax.axis_size("seq")
    pairs = []
    for i in range(peers):
        other = i + PLANE if i // PLANE % 2 else i - PLANE
        if 0 <= other < peers:
            pairs.append((i, other))
    return lax.ppermute(value, "seq", pairs)


def plane_all_to_all(value):
    peers = lax.axis_size("seq")
    planes = [list(range(i, i + PLANE)) for i in range(0, peers, PLANE)]
    return lax.all_to_all(value, "seq", 0, 0, axis_index_groups=planes, tiled=True)


def sharded_by_plane(query_rows, key_rows, value_rows, out_grad, widths, sections):
    position = lax.axis_index("seq").astype(jnp.int32)
    place = jnp.stack([position % PLANE, position // PLANE])
    blocks = lax.axis_size("seq")
    local = PLANE.bit_length() - 1
    total = sections.shape[0]
    groups = [tuple(range(local, total)), tuple(range(local))]
    order = tuple(s for group in groups for s in group)
    tables = (place, widths, sections)
    sent = pack(place, sections, [key_rows, value_rows], order, True)
    (graded_sent,) = pack(place, sections, [query_rows, out_grad], order, False)
    graded = plane_all_to_all(graded_sent)
    pairs = in_plane(sent)
    next_sent, last_sent = halo_parts(place, pairs)
    far_sent = far_parts(pairs, total - local)
    halos = (with_next_plane(next_sent), with_last_plane(last_sent))
    far = (with_next_plane(far_sent[0]), with_other_plane(far_sent[1]))
    rows, part_near, owed = attend(
        *tables, pairs, graded, halos, (), local, 0, total - local, blocks
    )
    owed_near = [with_next_plane(owed[0]), with_last_plane(owed[1])]
    rows, part_far, owed = attend(
        *tables, pairs, graded, halos, far, total - local, local, 0, blocks, rows
    )
    near = combine(place, part_near, owed_near)
    owed, near, rows = lax.optimization_barrier((owed, near, rows))
    other_back = with_other_plane(owed[2])
    owed_far = [with_next_plane(owed[0]), with_last_plane(owed[1]), other_back]
    near = in_plane(near)
    attended, query_grad = unpack(
        place,
        sections,
        functools.partial(unpack_crossed_kernel, groups=[order]),
        in_plane(rows),
    )
    owed_far, attended, query_grad = lax.optimization_barrier((owed_far, attended, query_grad))
    columns = in_plane(combine(place, part_far, owed_far)) + near
    key_grad, value_grad = unpack(
        place, sections, functools.partial(unpack_crossed_kernel, groups=groups), columns
    )
    return attended, query_grad, key_grad, value_grad


def solution(mesh):
    spec = P(("grp", "seq"), None, None)
    peers = mesh.shape["seq"]

    def per_device_any(*args):
        tokens, heads, width = args[0].shape
        sections, listed = args[5].shape
        once = sections * listed == heads
        if tokens == BLK and once and listed == PLANE and 1 << sections == peers == PLANE**2:
            return sharded_by_plane(*args)
        return per_device(*args)

    return jax.shard_map(
        per_device_any,
        mesh=mesh,
        in_specs=(spec, spec, spec, spec, P(), P()),
        out_specs=(spec,) * 4,
        check_vma=False,
    )
```

```python
import functools
import math

import jax
import jax.numpy as jnp
from jax import lax
from jax.experimental import pallas as pl
from jax.experimental.pallas import tpu as pltpu
from jax.sharding import PartitionSpec as P

BLK = 128
WB = 3
HALO = WB - 1
SPAN = (2 * HALO + 1) * BLK
LINKED = SPAN + BLK
PLANE = 2 * HALO
PADDED = PLANE + 2 * HALO
NT = (((1,), (1,)), ((), ()))
NN = (((1,), (0,)), ((), ()))
blocked_score = -1e30


def mm(a, b, dims=NN):
    return lax.dot_general(a, b, dims, preferred_element_type=jnp.float32)


def moved_cost(arrays):
    return pl.CostEstimate(
        flops=0, transcendentals=0, bytes_accessed=4 * sum(a.size for a in arrays)
    )


def softmax_pair(score, far_score, biases, far_bias, scale2):
    near_parts, far_parts = [], []
    gap = jnp.zeros((BLK, BLK), jnp.bfloat16)
    for r in range(2):
        rows = slice(r * BLK, (r + 1) * BLK)
        sw = score[rows, r * BLK : r * BLK + SPAN] * scale2 + biases[r]
        sf = far_score[r] * scale2 + far_bias
        top = jnp.maximum(jnp.max(sw, axis=1, keepdims=True), jnp.max(sf, axis=1, keepdims=True))
        ew, ef = jnp.exp2(sw - top), jnp.exp2(sf - top)
        total = jnp.sum(ew, axis=1, keepdims=True) + jnp.sum(ef, axis=1, keepdims=True)
        inverse = 1.0 / total
        near = (ew * inverse).astype(jnp.bfloat16)
        near_parts.append(jnp.concatenate([near, gap] if r == 0 else [gap, near], axis=1))
        far_parts.append((ef * inverse).astype(jnp.bfloat16))
    return jnp.concatenate(near_parts, axis=0), far_parts


def attend_pair(q, g, kw, vw, kf, vf, biases, far_bias):
    scale = 1.0 / math.sqrt(q.shape[-1])
    scale2 = scale * math.log2(math.e)
    half = [slice(0, BLK), slice(BLK, 2 * BLK)]
    far_score = [mm(q[half[r]], kf[r], NT) for r in range(2)]
    near, far = softmax_pair(mm(q, kw, NT), far_score, biases, far_bias, scale2)
    far_out = jnp.concatenate([mm(far[r], vf[r]) for r in range(2)], axis=0)
    attended = (mm(near, vw) + far_out).astype(jnp.bfloat16)
    delta = jnp.sum(g.astype(jnp.float32) * attended.astype(jnp.float32), axis=1, keepdims=True)
    d_near = (near.astype(jnp.float32) * (mm(g, vw, NT) - delta)).astype(jnp.bfloat16)
    d_far = [
        (far[r].astype(jnp.float32) * (mm(g[half[r]], vf[r], NT) - delta[half[r]])).astype(
            jnp.bfloat16
        )
        for r in range(2)
    ]
    far_dq = jnp.concatenate([mm(d_far[r], kf[r]) for r in range(2)], axis=0)
    query_grad = ((mm(d_near, kw) + far_dq) * scale).astype(jnp.bfloat16)
    qt, gt = jnp.transpose(q), jnp.transpose(g)
    key_near, value_near = mm(qt, d_near), mm(gt, near)
    key_far = [mm(qt[:, half[r]], d_far[r]) for r in range(2)]
    value_far = [mm(gt[:, half[r]], far[r]) for r in range(2)]
    return attended, query_grad, key_near, value_near, key_far, value_far


def near_biases(b, width, low, high):
    offset = lax.broadcasted_iota(jnp.int32, (1, SPAN), 1) // BLK - HALO
    inside = jnp.abs(offset) < width
    out = []
    for r in range(2):
        there = offset + b + r
        out.append(jnp.where(inside & (there >= low) & (there < high), 0.0, blocked_score))
    return out


def rows_of(block):
    return pl.ds(pl.multiple_of(block * BLK, BLK), BLK)


def whole(shape):
    return pl.BlockSpec(shape, lambda *_: (0,) * len(shape))


SMEM = pl.BlockSpec(memory_space=pltpu.SMEM)
VMEM = pl.BlockSpec(memory_space=pltpu.VMEM)
LIMIT = pltpu.CompilerParams(vmem_limit_bytes=20 << 20)


def pack_kernel(place, sections, *refs, order, count, crossed):
    ins, outs, held = refs[:count], refs[count:-1], refs[-1]
    for i in range(count):
        held[i] = jnp.transpose(ins[i][...], (1, 0, 2))
    for m in range(PLANE):
        owner = seat(place) ^ m if crossed else m
        for k, s in enumerate(order):
            head = sections[s, owner]
            for i in range(count):
                if crossed:
                    outs[m][k, i] = held[i, head]
                else:
                    outs[0][m, k, i] = held[i, head]


def pack(place, sections, arrays, order, crossed):
    tokens, heads, width = arrays[0].shape
    chunk = tokens // 2
    count = len(arrays)
    shape = (len(order), count, tokens, width)
    if crossed:
        shapes = [shape] * PLANE
        specs = [pl.BlockSpec((*shape[:2], chunk, width), lambda i: (0, 0, i, 0))] * PLANE
    else:
        shapes = [(PLANE, *shape)]
        specs = [pl.BlockSpec((PLANE, *shape[:2], chunk, width), lambda i: (0, 0, 0, i, 0))]
    return pl.pallas_call(
        functools.partial(pack_kernel, order=order, count=count, crossed=crossed),
        grid=(tokens // chunk,),
        in_specs=[SMEM, SMEM]
        + [pl.BlockSpec((chunk, heads, width), lambda i: (i, 0, 0))] * count,
        out_specs=specs,
        out_shape=[jax.ShapeDtypeStruct(shape, jnp.bfloat16) for shape in shapes],
        scratch_shapes=[pltpu.VMEM((count, heads, chunk, width), jnp.bfloat16)],
        cost_estimate=moved_cost(arrays),
    )(place, sections, *arrays)


def unpack_kernel(place, sections, *refs, groups, count):
    pieces, outs, held = refs[: len(groups) * PLANE], refs[len(groups) * PLANE : -1], refs[-1]
    for number, group in enumerate(groups):
        for m in range(PLANE):
            for k, s in enumerate(group):
                head = sections[s, seat(place) ^ m]
                for i in range(count):
                    held[i, head] = pieces[number * PLANE + m][k, i]
    for i in range(count):
        outs[i][...] = jnp.transpose(held[i], (1, 0, 2))


def unpack(place, sections, parts):
    flat = [piece for _, pieces, _ in parts for piece in pieces]
    count, tokens, width = flat[0].shape[1:]
    heads = sections.size
    chunk = tokens // 2
    specs = [
        pl.BlockSpec((len(group), count, chunk, width), lambda i, run=run: (run, 0, i, 0))
        for group, _, run in parts
        for _ in range(PLANE)
    ]
    return pl.pallas_call(
        functools.partial(unpack_kernel, groups=[group for group, _, _ in parts], count=count),
        grid=(tokens // chunk,),
        in_specs=[SMEM, SMEM] + specs,
        out_specs=[pl.BlockSpec((chunk, heads, width), lambda i: (i, 0, 0))] * count,
        out_shape=[jax.ShapeDtypeStruct((tokens, heads, width), jnp.bfloat16)] * count,
        scratch_shapes=[pltpu.VMEM((count, heads, chunk, width), jnp.bfloat16)],
        compiler_params=LIMIT,
        cost_estimate=moved_cost(flat),
    )(place, sections, *flat)


def seat(place):
    return place[0] % PLANE


def plane(place):
    return place[0] // PLANE


def facing(place):
    return seat(place) // HALO == 1 - plane(place) % 2


def far_kernel(*refs):
    pieces, outs = refs[:PLANE], refs[PLANE:]
    for k, out in enumerate(outs):
        for m, piece in enumerate(pieces):
            out[m] = piece[k]


def far_parts(pieces, count):
    rest = pieces[0].shape[1:]
    return pl.pallas_call(
        far_kernel,
        in_specs=[VMEM] * PLANE,
        out_specs=[VMEM] * count,
        out_shape=[jax.ShapeDtypeStruct((PLANE, *rest), jnp.bfloat16)] * count,
        compiler_params=LIMIT,
        cost_estimate=moved_cost(pieces),
    )(*pieces)


def halo_kernel(place, *refs):
    pieces, (with_next, with_last) = refs[:PLANE], refs[PLANE:]
    slots = pieces[0].shape[0]

    def fill(base, other):
        for m in range(HALO):
            with_next[m * slots : (m + 1) * slots] = pieces[base + m][...]
            with_last[m * slots : (m + 1) * slots] = pieces[other + m][...]

    @pl.when(facing(place))
    def _():
        fill(0, HALO)

    @pl.when(jnp.logical_not(facing(place)))
    def _():
        fill(HALO, 0)


def halo_parts(place, pieces):
    slots, *rest = pieces[0].shape
    return pl.pallas_call(
        halo_kernel,
        in_specs=[SMEM] + [VMEM] * PLANE,
        out_specs=[VMEM] * 2,
        out_shape=[jax.ShapeDtypeStruct((HALO * slots, *rest), jnp.bfloat16)] * 2,
        compiler_params=LIMIT,
        cost_estimate=moved_cost(pieces),
    )(place, *pieces)


def attend_kernel(place, widths, sections, *refs, first, slot, group, remote, blocks, aliased):
    pairs, (graded, with_next, with_last) = refs[:PLANE], refs[PLANE : PLANE + 3]
    rest = refs[PLANE + 3 :]
    if remote:
        far_in, rest = rest[:2], rest[2:]
    rest = rest[aliased:]
    rows, rest = rest[:PLANE], rest[PLANE:]
    (part, to_next, to_last), rest = rest[:3], rest[3:]
    if remote:
        to_other, rest = rest[0], rest[1:]
    keys, values, far_keys, far_values, attended, dq = rest[:6]
    accs, far_accs = rest[6:8], rest[8:10]
    me = seat(place)
    scales = (1.0 / math.sqrt(keys.shape[-1]), 1.0)
    lead = PLANE if remote else 0
    slots = with_next.shape[0] // HALO
    next_at = jnp.where(plane(place) % 2 == 0, HALO + PLANE, 0)
    last_at = HALO + PLANE - next_at
    for k in range(group):
        width = widths[sections[first + k, me]]
        bit = 1 << first + k
        far_bias = jnp.where(bit >= width, 0.0, blocked_score).astype(jnp.float32)
        for m in range(PLANE):
            keys[rows_of(HALO + (me ^ m))] = pairs[m][slot + k, 0]
            values[rows_of(HALO + (me ^ m))] = pairs[m][slot + k, 1]
        for m in range(HALO):
            b = (me % HALO) ^ m
            at = m * slots + slot + k
            keys[rows_of(next_at + b)] = with_next[at, 0]
            values[rows_of(next_at + b)] = with_next[at, 1]
            keys[rows_of(last_at + b)] = with_last[at, 0]
            values[rows_of(last_at + b)] = with_last[at, 1]
        if remote:
            for m in range(PLANE):
                far_keys[rows_of(me ^ m)] = far_in[1 - k][m, 0]
                far_values[rows_of(me ^ m)] = far_in[1 - k][m, 1]
        for acc in accs:
            acc[...] = jnp.zeros_like(acc)
        for b in range(0, PLANE, 2):
            own = slice(b * BLK, (b + 2) * BLK)
            seen = slice(b * BLK, (b + 2 * HALO + 2) * BLK)
            one = [slice((b + r) * BLK, (b + r + 1) * BLK) for r in range(2)]
            if remote:
                kf, vf = [[ref[at] for at in one] for ref in (far_keys, far_values)]
            else:
                there = [HALO + ((b + r) ^ bit) for r in range(2)]
                kf, vf = [
                    [ref[at * BLK : (at + 1) * BLK] for at in there] for ref in (keys, values)
                ]
            o, d, key_near, value_near, key_far, value_far = attend_pair(
                jnp.concatenate([graded[b, slot + k, 0], graded[b + 1, slot + k, 0]], axis=0),
                jnp.concatenate([graded[b, slot + k, 1], graded[b + 1, slot + k, 1]], axis=0),
                keys[seen],
                values[seen],
                kf,
                vf,
                near_biases(plane(place) * PLANE + b, width, 0, blocks),
                far_bias,
            )
            attended[own] = o
            dq[own] = d
            for acc, near in zip(accs, (key_near, value_near)):
                acc[:, seen] += near
            for acc, far_acc, far in zip(accs, far_accs, (key_far, value_far)):
                for r in range(2):
                    if remote:
                        far_acc[:, one[r]] = far[r]
                    else:
                        acc[:, there[r] * BLK : (there[r] + 1) * BLK] += far[r]
        for i, (acc, far_acc) in enumerate(zip(accs, far_accs)):
            if remote:
                target = (to_next, to_other)[k]
                for m in range(PLANE):
                    owed = far_acc[:, rows_of(me ^ m)] * scales[i]
                    target[m, i] = owed.astype(jnp.bfloat16)
            for m in range(PLANE):
                part[k, m, i] = acc[:, rows_of(HALO + (me ^ m))] * scales[i]
            for m in range(HALO):
                b = (me % HALO) ^ m
                at = m * group + k
                to_next[lead + at, i] = (acc[:, rows_of(next_at + b)] * scales[i]).astype(
                    jnp.bfloat16
                )
                to_last[at, i] = (acc[:, rows_of(last_at + b)] * scales[i]).astype(jnp.bfloat16)
        for m in range(PLANE):
            rows[m][slot + k, 0] = attended[rows_of(me ^ m)]
            rows[m][slot + k, 1] = dq[rows_of(me ^ m)]


def attend(place, widths, sections, pairs, graded, halos, far, group, first, slot, blocks, rows=()):
    count, _, width = pairs[0].shape[1:]
    tile = (BLK, width)
    remote = len(far)
    room = pairs[0].shape[0] + group
    bf16 = jnp.bfloat16
    owed = [(HALO * group + (PLANE if remote else 0), count, *tile), (HALO * group, count, *tile)]
    if remote:
        owed.append((PLANE, count, *tile))
    inputs = (*pairs, graded, *halos, *far, *rows)
    outs = pl.pallas_call(
        functools.partial(
            attend_kernel,
            first=first,
            slot=slot,
            group=group,
            remote=remote,
            blocks=blocks,
            aliased=len(rows),
        ),
        in_specs=[SMEM] * 3 + [VMEM] * len(inputs),
        out_specs=[VMEM] * (PLANE + 1 + len(owed)),
        out_shape=[jax.ShapeDtypeStruct((room, count, *tile), bf16)] * PLANE
        + [jax.ShapeDtypeStruct((group, PLANE, count, *tile), jnp.float32)]
        + [jax.ShapeDtypeStruct(shape, bf16) for shape in owed],
        scratch_shapes=[pltpu.VMEM((PADDED * BLK, width), bf16)] * 2
        + [pltpu.VMEM((PLANE * BLK, width), bf16)] * 4
        + [pltpu.VMEM((width, PADDED * BLK), jnp.float32)] * 2
        + [pltpu.VMEM((width, PLANE * BLK), jnp.float32)] * 2,
        input_output_aliases={3 + len(inputs) - len(rows) + m: m for m in range(len(rows))},
        compiler_params=LIMIT,
        cost_estimate=pl.CostEstimate(
            flops=group * PLANE * 12 * BLK * LINKED * width,
            transcendentals=group * PLANE * BLK * LINKED,
            bytes_accessed=40 * group * PLANE * BLK * width,
        ),
    )(place, widths, sections, *inputs)
    return outs[:PLANE], outs[PLANE], outs[PLANE + 1 :]


def combine_kernel(place, part, *refs, remote, base, aliased):
    with_other, (with_next, with_last) = refs[0], refs[remote : remote + 2]
    outs = refs[remote + 2 + aliased :]
    group = part.shape[0]
    lead = PLANE if remote else 0
    for m in range(PLANE):
        own_chip = m < HALO
        next_side = facing(place) if own_chip else jnp.logical_not(facing(place))
        for k in range(group):
            slot = (m % HALO) * group + k
            for i in range(part.shape[2]):
                owed = jnp.where(next_side, with_next[lead + slot, i], with_last[slot, i])
                total = part[k, m, i] + owed.astype(jnp.float32)
                if remote:
                    far = (with_next, with_other)[k]
                    total += far[m, i].astype(jnp.float32)
                outs[m][base + k, i] = jnp.transpose(total.astype(jnp.bfloat16))


def combine(place, part, owed, rows=(), base=0):
    group, _, *rest = part.shape
    inputs = (part, *owed, *rows)
    shape = rows[0].shape if rows else (group, *rest)
    return pl.pallas_call(
        functools.partial(
            combine_kernel, remote=len(owed) - 2, base=base, aliased=len(rows)
        ),
        in_specs=[SMEM] + [VMEM] * len(inputs),
        out_specs=[VMEM] * PLANE,
        out_shape=[jax.ShapeDtypeStruct(shape, jnp.bfloat16)] * PLANE,
        input_output_aliases={1 + len(inputs) - len(rows) + m: m for m in range(len(rows))},
        compiler_params=LIMIT,
        cost_estimate=moved_cost([part, *owed]),
    )(place, *inputs)


def partner(value, axis, apart):
    return lax.ppermute(value, axis, [(i, i ^ 1 << apart) for i in range(lax.axis_size(axis))])


def passed_along(value, axis, by):
    peers = lax.axis_size(axis)
    pairs = [(i, i + by) for i in range(peers) if 0 <= i + by < peers]
    return lax.ppermute(value, axis, pairs)


def to_slots(values, picker):
    return jnp.sum(jnp.where(picker[None, :, :, None], values[:, None, :, :], 0.0), axis=2)


def slots_to_heads(values, picker, filler):
    covered = jnp.any(picker, axis=0)
    summed = jnp.sum(jnp.where(picker[None, :, :, None], values[:, :, None, :], 0.0), axis=1)
    return jnp.where(covered[None, :, None], summed, filler)


def rows_slots_to_heads(values, picker):
    return jnp.einsum(
        "jqid,ih->jqhd", values, picker.astype(jnp.float32), precision=lax.Precision.HIGHEST
    )


def pick_heads(values, picker):
    chooser = picker.astype(jnp.bfloat16)
    return jnp.einsum("ih,jqhd->jqid", chooser, values, preferred_element_type=jnp.float32).astype(
        jnp.bfloat16
    )


def partner_route(values, section_index, low_bits):
    return partner(values, "seq", section_index - low_bits)


def partner_back(values, section_index, low_bits):
    return partner(values, "seq", section_index - low_bits)


def extend_blocks(values, reach, halo_blocks, blocks_dev, mover):
    pieces = [mover(values, distance) for distance in range(reach, 0, -1)]
    pieces = pieces + [values] + [mover(values, -distance) for distance in range(1, reach + 1)]
    start = reach * blocks_dev - halo_blocks
    whole = jnp.concatenate(pieces, axis=1)
    return whole


def move_keys(values, distance):
    return passed_along(values, "seq", distance)


def window_sets(extended, blocks_dev, spread):
    return jnp.stack(
        [extended[:, offset : offset + blocks_dev] for offset in range(spread)], axis=2
    )


def per_device(query_rows, key_rows, value_rows, out_grad, window_blocks, section_heads):
    tokens_dev, head_count, head_width = query_rows.shape
    blocks_dev = tokens_dev // BLK
    low_bits = blocks_dev.bit_length() - 1
    seq_count = lax.axis_size("seq")
    section_total = low_bits + seq_count.bit_length() - 1
    halo_blocks = WB - 1
    reach = (halo_blocks + blocks_dev - 1) // blocks_dev
    padding = reach * blocks_dev
    spread = 2 * WB - 1
    score_scale = 1.0 / math.sqrt(head_width)
    first_block = lax.axis_index("seq") * blocks_dev + jnp.arange(blocks_dev, dtype=jnp.int32)
    all_blocks = blocks_dev * seq_count
    query_blocks = query_rows.reshape(blocks_dev, BLK, head_count, head_width)
    key_blocks = key_rows.reshape(blocks_dev, BLK, head_count, head_width)
    value_blocks = value_rows.reshape(blocks_dev, BLK, head_count, head_width)
    grad_blocks = out_grad.reshape(blocks_dev, BLK, head_count, head_width)
    offsets = jnp.arange(spread, dtype=jnp.int32) - halo_blocks
    near_block = first_block[:, None] + offsets[None, :]
    in_range = (near_block >= 0) & (near_block < all_blocks)
    near_mask = in_range[:, None, :] & (
        jnp.abs(offsets)[None, None, :] < window_blocks[None, :, None]
    )
    wide_mask = near_mask[:, :, None, :, None]
    head_ids = jnp.arange(head_count, dtype=jnp.int32)
    paired = jnp.stack([key_blocks, value_blocks])
    extended = extend_blocks(paired, reach, halo_blocks, blocks_dev, move_keys)
    near_sets = window_sets(extended, blocks_dev, spread)
    near_keys = near_sets[0]
    near_values = near_sets[1]
    near_scores = (
        jnp.einsum("jqhd,jckhd->jhqck", query_blocks, near_keys, preferred_element_type=jnp.float32)
        * score_scale
    )
    near_scores = jnp.where(wide_mask, near_scores, blocked_score)
    top_score = jnp.max(near_scores, axis=(3, 4))
    records = []
    for section_index in range(section_total):
        picker = section_heads[section_index][:, None] == head_ids[None, :]
        slot_width = jnp.sum(jnp.where(picker, window_blocks[None, :], 0), axis=1)
        slot_valid = 2**section_index >= slot_width
        chosen_query = pick_heads(query_blocks, picker)
        chosen_grad = pick_heads(grad_blocks, picker)
        chosen_pair = jnp.stack([pick_heads(key_blocks, picker), pick_heads(value_blocks, picker)])
        partner_pair = partner_route(chosen_pair, section_index, low_bits)
        far_scores = (
            jnp.einsum(
                "jqid,jkid->jiqk", chosen_query, partner_pair[0], preferred_element_type=jnp.float32
            )
            * score_scale
        )
        far_scores = jnp.where(slot_valid[None, :, None, None], far_scores, blocked_score)
        top_score = jnp.maximum(
            top_score, slots_to_heads(jnp.max(far_scores, axis=3), picker, blocked_score)
        )
        records.append(
            (
                section_index,
                picker,
                slot_valid,
                chosen_query,
                chosen_grad,
                chosen_pair,
                partner_pair,
                far_scores,
            )
        )
    row_total = jnp.sum(
        jnp.where(wide_mask, jnp.exp(near_scores - top_score[:, :, :, None, None]), 0.0),
        axis=(3, 4),
    )
    for record in records:
        picker = record[1]
        slot_top = to_slots(top_score, picker)
        far_sum = jnp.sum(
            jnp.where(
                record[2][None, :, None, None], jnp.exp(record[7] - slot_top[:, :, :, None]), 0.0
            ),
            axis=3,
        )
        row_total = row_total + slots_to_heads(far_sum, picker, 0.0)
    log_total = top_score + jnp.log(row_total)
    near_probs = jnp.where(
        wide_mask, jnp.exp(near_scores - log_total[:, :, :, None, None]), 0.0
    ).astype(jnp.bfloat16)
    attended_sum = jnp.einsum(
        "jhqck,jckhd->jqhd", near_probs, near_values, preferred_element_type=jnp.float32
    )
    far_probs_list = []
    for record in records:
        picker = record[1]
        slot_lse = to_slots(log_total, picker)
        far_probs = jnp.where(
            record[2][None, :, None, None], jnp.exp(record[7] - slot_lse[:, :, :, None]), 0.0
        ).astype(jnp.bfloat16)
        far_probs_list.append((far_probs, slot_lse))
        attended_sum = attended_sum + rows_slots_to_heads(
            jnp.einsum(
                "jiqk,jkid->jqid", far_probs, record[6][1], preferred_element_type=jnp.float32
            ),
            picker,
        )
    attended = attended_sum.astype(jnp.bfloat16)
    row_delta = jnp.transpose(
        jnp.sum(grad_blocks.astype(jnp.float32) * attended.astype(jnp.float32), axis=-1), (0, 2, 1)
    )
    near_dprob = jnp.einsum(
        "jqhd,jckhd->jhqck", grad_blocks, near_values, preferred_element_type=jnp.float32
    )
    near_dscore = (
        near_probs.astype(jnp.float32) * (near_dprob - row_delta[:, :, :, None, None])
    ).astype(jnp.bfloat16)
    query_sum = jnp.einsum(
        "jhqck,jckhd->jqhd", near_dscore, near_keys, preferred_element_type=jnp.float32
    )
    far_dscores = []
    for record, probs_pair in zip(records, far_probs_list):
        picker = record[1]
        slot_delta = to_slots(row_delta, picker)
        far_dprob = jnp.einsum(
            "jqid,jkid->jiqk", record[4], record[6][1], preferred_element_type=jnp.float32
        )
        far_dscore = (
            probs_pair[0].astype(jnp.float32) * (far_dprob - slot_delta[:, :, :, None])
        ).astype(jnp.bfloat16)
        far_dscores.append((far_dscore, slot_delta))
        query_sum = query_sum + rows_slots_to_heads(
            jnp.einsum(
                "jiqk,jkid->jqid", far_dscore, record[6][0], preferred_element_type=jnp.float32
            ),
            picker,
        )
    query_grad = (
        (query_sum * score_scale).astype(jnp.bfloat16).reshape(tokens_dev, head_count, head_width)
    )
    near_key_part = (
        jnp.einsum(
            "jhqck,jqhd->jckhd", near_dscore, query_blocks, preferred_element_type=jnp.float32
        )
        * score_scale
    )
    near_value_part = jnp.einsum(
        "jhqck,jqhd->jckhd", near_probs, grad_blocks, preferred_element_type=jnp.float32
    )
    stacked_parts = jnp.stack([near_key_part, near_value_part])
    extended_count = blocks_dev + 2 * padding
    base = padding - halo_blocks
    extended_ids = jnp.arange(extended_count, dtype=jnp.int32)
    own_ids = jnp.arange(blocks_dev, dtype=jnp.int32)
    spread_ids = jnp.arange(spread, dtype=jnp.int32)
    placer = (
        extended_ids[:, None, None] == base + own_ids[None, :, None] + spread_ids[None, None, :]
    ).astype(jnp.float32)
    gathered = jnp.einsum(
        "ejc,xjckhd->xekhd", placer, stacked_parts, precision=lax.Precision.HIGHEST
    )
    own_grads = gathered[:, padding : padding + blocks_dev]
    for distance in range(1, reach + 1):
        lower_slab = gathered[
            :, padding - distance * blocks_dev : padding - (distance - 1) * blocks_dev
        ]
        own_grads = own_grads + passed_along(
            lower_slab.astype(jnp.bfloat16), "seq", -distance
        ).astype(lower_slab.dtype)
        upper_start = padding + blocks_dev + (distance - 1) * blocks_dev
        upper_slab = gathered[:, upper_start : upper_start + blocks_dev]
        own_grads = own_grads + passed_along(
            upper_slab.astype(jnp.bfloat16), "seq", distance
        ).astype(upper_slab.dtype)
    for record, probs_pair, dscore_pair in zip(records, far_probs_list, far_dscores):
        picker = record[1]
        key_part = (
            jnp.einsum(
                "jiqk,jqid->jkid", dscore_pair[0], record[3], preferred_element_type=jnp.float32
            )
            * score_scale
        )
        value_part = jnp.einsum(
            "jiqk,jqid->jkid", probs_pair[0], record[4], preferred_element_type=jnp.float32
        )
        returned = partner_back(jnp.stack([key_part, value_part]), record[0], low_bits)
        own_grads = own_grads + jnp.stack(
            [rows_slots_to_heads(returned[0], picker), rows_slots_to_heads(returned[1], picker)]
        )
    key_grad = own_grads[0].astype(jnp.bfloat16).reshape(tokens_dev, head_count, head_width)
    value_grad = own_grads[1].astype(jnp.bfloat16).reshape(tokens_dev, head_count, head_width)
    return (attended.reshape(tokens_dev, head_count, head_width), query_grad, key_grad, value_grad)


def in_plane(pieces, chip_first=False):
    peers = lax.axis_size("seq")
    pieces = list(pieces)
    for m in range(1, PLANE):
        pieces[m] = lax.ppermute(pieces[m], "seq", [(i, i ^ m) for i in range(peers)])
        if chip_first and m == 1:
            pieces = lax.optimization_barrier(pieces)
    return pieces


def with_next_plane(value):
    return partner(value, "seq", PLANE.bit_length() - 1)


def with_other_plane(value):
    return partner(value, "seq", PLANE.bit_length())


def with_last_plane(value):
    peers = lax.axis_size("seq")
    pairs = []
    for i in range(peers):
        other = i + PLANE if i // PLANE % 2 else i - PLANE
        if 0 <= other < peers:
            pairs.append((i, other))
    return lax.ppermute(value, "seq", pairs)


def plane_all_to_all(value):
    peers = lax.axis_size("seq")
    planes = [list(range(i, i + PLANE)) for i in range(0, peers, PLANE)]
    return lax.all_to_all(value, "seq", 0, 0, axis_index_groups=planes, tiled=True)


def sharded_by_plane(query_rows, key_rows, value_rows, out_grad, widths, sections):
    place = lax.axis_index("seq").astype(jnp.int32).reshape(1)
    blocks = lax.axis_size("seq")
    local = PLANE.bit_length() - 1
    total = sections.shape[0]
    groups = [tuple(range(local, total)), tuple(range(local))]
    order = tuple(s for group in groups for s in group)
    tables = (place, widths, sections)
    sent = pack(place, sections, [key_rows, value_rows], order, True)
    (graded_sent,) = pack(place, sections, [query_rows, out_grad], order, False)
    graded = plane_all_to_all(graded_sent)
    pairs = in_plane(sent)
    next_sent, last_sent = halo_parts(place, pairs)
    far_sent = far_parts(pairs, total - local)
    halos = (with_next_plane(next_sent), with_last_plane(last_sent))
    far = (with_other_plane(far_sent[1]), with_next_plane(far_sent[0]))
    rows, part_near, owed = attend(
        *tables, pairs, graded, halos, (), local, 0, total - local, blocks
    )
    owed_near = [with_next_plane(owed[0]), with_last_plane(owed[1])]
    rows, part_far, owed = attend(
        *tables, pairs, graded, halos, far, total - local, local, 0, blocks, rows
    )
    other_back = with_other_plane(owed[2])
    owed_far = [other_back, with_next_plane(owed[0]), with_last_plane(owed[1])]
    rows = in_plane(combine(place, part_near, owed_near, rows, total), True)
    attended, query_grad = unpack(place, sections, [(groups[0], rows, 0), (groups[1], rows, 1)])
    columns = in_plane(combine(place, part_far, owed_far))
    columns, attended, query_grad = lax.optimization_barrier((columns, attended, query_grad))
    key_grad, value_grad = unpack(place, sections, [(groups[0], columns, 0), (groups[1], rows, 2)])
    return attended, query_grad, key_grad, value_grad


def solution(mesh):
    spec = P(("grp", "seq"), None, None)
    peers = mesh.shape["seq"]

    def per_device_any(*args):
        tokens, heads, width = args[0].shape
        sections, listed = args[5].shape
        once = sections * listed == heads
        if tokens == BLK and once and listed == PLANE and 1 << sections == peers == PLANE**2:
            return sharded_by_plane(*args)
        return per_device(*args)

    return jax.shard_map(
        per_device_any,
        mesh=mesh,
        in_specs=(spec, spec, spec, spec, P(), P()),
        out_specs=(spec,) * 4,
        check_vma=False,
    )
```

```python
import functools
import math

import jax
import jax.numpy as jnp
from jax import lax
from jax.experimental import pallas as pl
from jax.experimental.pallas import tpu as pltpu
from jax.sharding import PartitionSpec as P

BLK = 128
WB = 3
HALO = WB - 1
SPAN = (2 * HALO + 1) * BLK
LINKED = SPAN + BLK
PLANE = 2 * HALO
PADDED = PLANE + 2 * HALO
NT = (((1,), (1,)), ((), ()))
NN = (((1,), (0,)), ((), ()))
blocked_score = -1e30


def mm(a, b, dims=NN):
    return lax.dot_general(a, b, dims, preferred_element_type=jnp.float32)


def moved_cost(arrays):
    return pl.CostEstimate(
        flops=0, transcendentals=0, bytes_accessed=4 * sum(a.size for a in arrays)
    )


def softmax_pair(score, far_score, biases, far_bias, scale2):
    near_parts, far_parts = [], []
    gap = jnp.zeros((BLK, BLK), jnp.bfloat16)
    for r in range(2):
        rows = slice(r * BLK, (r + 1) * BLK)
        sw = score[rows, r * BLK : r * BLK + SPAN] * scale2 + biases[r]
        sf = far_score[r] * scale2 + far_bias
        top = jnp.maximum(jnp.max(sw, axis=1, keepdims=True), jnp.max(sf, axis=1, keepdims=True))
        ew, ef = jnp.exp2(sw - top), jnp.exp2(sf - top)
        total = jnp.sum(ew, axis=1, keepdims=True) + jnp.sum(ef, axis=1, keepdims=True)
        inverse = 1.0 / total
        near = (ew * inverse).astype(jnp.bfloat16)
        near_parts.append(jnp.concatenate([near, gap] if r == 0 else [gap, near], axis=1))
        far_parts.append((ef * inverse).astype(jnp.bfloat16))
    return jnp.concatenate(near_parts, axis=0), far_parts


def attend_pair(q, g, kw, vw, kf, vf, biases, far_bias):
    scale = 1.0 / math.sqrt(q.shape[-1])
    scale2 = scale * math.log2(math.e)
    half = [slice(0, BLK), slice(BLK, 2 * BLK)]
    far_score = [mm(q[half[r]], kf[r], NT) for r in range(2)]
    near, far = softmax_pair(mm(q, kw, NT), far_score, biases, far_bias, scale2)
    far_out = jnp.concatenate([mm(far[r], vf[r]) for r in range(2)], axis=0)
    attended = (mm(near, vw) + far_out).astype(jnp.bfloat16)
    delta = jnp.sum(g.astype(jnp.float32) * attended.astype(jnp.float32), axis=1, keepdims=True)
    d_near = (near.astype(jnp.float32) * (mm(g, vw, NT) - delta)).astype(jnp.bfloat16)
    d_far = [
        (far[r].astype(jnp.float32) * (mm(g[half[r]], vf[r], NT) - delta[half[r]])).astype(
            jnp.bfloat16
        )
        for r in range(2)
    ]
    far_dq = jnp.concatenate([mm(d_far[r], kf[r]) for r in range(2)], axis=0)
    query_grad = ((mm(d_near, kw) + far_dq) * scale).astype(jnp.bfloat16)
    qt, gt = jnp.transpose(q), jnp.transpose(g)
    key_near, value_near = mm(qt, d_near), mm(gt, near)
    key_far = [mm(qt[:, half[r]], d_far[r]) for r in range(2)]
    value_far = [mm(gt[:, half[r]], far[r]) for r in range(2)]
    return attended, query_grad, key_near, value_near, key_far, value_far


def near_biases(b, width, low, high):
    offset = lax.broadcasted_iota(jnp.int32, (1, SPAN), 1) // BLK - HALO
    inside = jnp.abs(offset) < width
    out = []
    for r in range(2):
        there = offset + b + r
        out.append(jnp.where(inside & (there >= low) & (there < high), 0.0, blocked_score))
    return out


def rows_of(block):
    return pl.ds(pl.multiple_of(block * BLK, BLK), BLK)


def whole(shape):
    return pl.BlockSpec(shape, lambda *_: (0,) * len(shape))


SMEM = pl.BlockSpec(memory_space=pltpu.SMEM)
VMEM = pl.BlockSpec(memory_space=pltpu.VMEM)
LIMIT = pltpu.CompilerParams(vmem_limit_bytes=20 << 20)


def pack_kernel(place, sections, *refs, order, count, crossed):
    ins, outs, held = refs[:count], refs[count:-1], refs[-1]
    for i in range(count):
        held[i] = jnp.transpose(ins[i][...], (1, 0, 2))
    for m in range(PLANE):
        owner = seat(place) ^ m if crossed else m
        for k, s in enumerate(order):
            head = sections[s, owner]
            for i in range(count):
                if crossed:
                    outs[m][k, i] = held[i, head]
                else:
                    outs[0][m, k, i] = held[i, head]


def pack(place, sections, arrays, order, crossed):
    tokens, heads, width = arrays[0].shape
    chunk = tokens // 2
    count = len(arrays)
    shape = (len(order), count, tokens, width)
    if crossed:
        shapes = [shape] * PLANE
        specs = [pl.BlockSpec((*shape[:2], chunk, width), lambda i: (0, 0, i, 0))] * PLANE
    else:
        shapes = [(PLANE, *shape)]
        specs = [pl.BlockSpec((PLANE, *shape[:2], chunk, width), lambda i: (0, 0, 0, i, 0))]
    return pl.pallas_call(
        functools.partial(pack_kernel, order=order, count=count, crossed=crossed),
        grid=(tokens // chunk,),
        in_specs=[SMEM, SMEM]
        + [pl.BlockSpec((chunk, heads, width), lambda i: (i, 0, 0))] * count,
        out_specs=specs,
        out_shape=[jax.ShapeDtypeStruct(shape, jnp.bfloat16) for shape in shapes],
        scratch_shapes=[pltpu.VMEM((count, heads, chunk, width), jnp.bfloat16)],
        cost_estimate=moved_cost(arrays),
    )(place, sections, *arrays)


def unpack_kernel(place, sections, *refs, groups, count):
    pieces, outs, held = refs[: len(groups) * PLANE], refs[len(groups) * PLANE : -1], refs[-1]
    for number, group in enumerate(groups):
        for m in range(PLANE):
            for k, s in enumerate(group):
                head = sections[s, seat(place) ^ m]
                for i in range(count):
                    held[i, head] = pieces[number * PLANE + m][k, i]
    for i in range(count):
        outs[i][...] = jnp.transpose(held[i], (1, 0, 2))


def unpack(place, sections, parts):
    flat = [piece for _, pieces, _ in parts for piece in pieces]
    count, tokens, width = flat[0].shape[1:]
    heads = sections.size
    chunk = tokens // 2
    specs = [
        pl.BlockSpec((len(group), count, chunk, width), lambda i, run=run: (run, 0, i, 0))
        for group, _, run in parts
        for _ in range(PLANE)
    ]
    return pl.pallas_call(
        functools.partial(unpack_kernel, groups=[group for group, _, _ in parts], count=count),
        grid=(tokens // chunk,),
        in_specs=[SMEM, SMEM] + specs,
        out_specs=[pl.BlockSpec((chunk, heads, width), lambda i: (i, 0, 0))] * count,
        out_shape=[jax.ShapeDtypeStruct((tokens, heads, width), jnp.bfloat16)] * count,
        scratch_shapes=[pltpu.VMEM((count, heads, chunk, width), jnp.bfloat16)],
        compiler_params=LIMIT,
        cost_estimate=moved_cost(flat),
    )(place, sections, *flat)


def seat(place):
    return place[0] % PLANE


def plane(place):
    return place[0] // PLANE


def facing(place):
    return seat(place) // HALO == 1 - plane(place) % 2


def far_kernel(*refs):
    pieces, outs = refs[:PLANE], refs[PLANE:]
    for k, out in enumerate(outs):
        for m, piece in enumerate(pieces):
            out[m] = piece[k]


def far_parts(pieces, count):
    rest = pieces[0].shape[1:]
    return pl.pallas_call(
        far_kernel,
        in_specs=[VMEM] * PLANE,
        out_specs=[VMEM] * count,
        out_shape=[jax.ShapeDtypeStruct((PLANE, *rest), jnp.bfloat16)] * count,
        compiler_params=LIMIT,
        cost_estimate=moved_cost(pieces),
    )(*pieces)


def halo_kernel(place, *refs):
    pieces, (with_next, with_last) = refs[:PLANE], refs[PLANE:]
    slots = pieces[0].shape[0]

    def fill(base, other):
        for m in range(HALO):
            with_next[m * slots : (m + 1) * slots] = pieces[base + m][...]
            with_last[m * slots : (m + 1) * slots] = pieces[other + m][...]

    @pl.when(facing(place))
    def _():
        fill(0, HALO)

    @pl.when(jnp.logical_not(facing(place)))
    def _():
        fill(HALO, 0)


def halo_parts(place, pieces):
    slots, *rest = pieces[0].shape
    return pl.pallas_call(
        halo_kernel,
        in_specs=[SMEM] + [VMEM] * PLANE,
        out_specs=[VMEM] * 2,
        out_shape=[jax.ShapeDtypeStruct((HALO * slots, *rest), jnp.bfloat16)] * 2,
        compiler_params=LIMIT,
        cost_estimate=moved_cost(pieces),
    )(place, *pieces)


def attend_kernel(place, widths, sections, *refs, first, slot, group, remote, blocks, aliased):
    pairs, (graded, with_next, with_last) = refs[:PLANE], refs[PLANE : PLANE + 3]
    rest = refs[PLANE + 3 :]
    if remote:
        far_in, rest = rest[:2], rest[2:]
    rest = rest[aliased:]
    rows, rest = rest[:PLANE], rest[PLANE:]
    (part, to_next, to_last), rest = rest[:3], rest[3:]
    if remote:
        to_other, rest = rest[0], rest[1:]
    keys, values, far_keys, far_values, attended, dq = rest[:6]
    accs, far_accs = rest[6:8], rest[8:10]
    me = seat(place)
    scales = (1.0 / math.sqrt(keys.shape[-1]), 1.0)
    lead = PLANE if remote else 0
    slots = with_next.shape[0] // HALO
    next_at = jnp.where(plane(place) % 2 == 0, HALO + PLANE, 0)
    last_at = HALO + PLANE - next_at
    for k in range(group):
        width = widths[sections[first + k, me]]
        bit = 1 << first + k
        far_bias = jnp.where(bit >= width, 0.0, blocked_score).astype(jnp.float32)
        for m in range(PLANE):
            keys[rows_of(HALO + (me ^ m))] = pairs[m][slot + k, 0]
            values[rows_of(HALO + (me ^ m))] = pairs[m][slot + k, 1]
        for m in range(HALO):
            b = (me % HALO) ^ m
            at = m * slots + slot + k
            keys[rows_of(next_at + b)] = with_next[at, 0]
            values[rows_of(next_at + b)] = with_next[at, 1]
            keys[rows_of(last_at + b)] = with_last[at, 0]
            values[rows_of(last_at + b)] = with_last[at, 1]
        if remote:
            for m in range(PLANE):
                far_keys[rows_of(me ^ m)] = far_in[1 - k][m, 0]
                far_values[rows_of(me ^ m)] = far_in[1 - k][m, 1]
        for acc in accs:
            acc[...] = jnp.zeros_like(acc)
        for b in range(0, PLANE, 2):
            own = slice(b * BLK, (b + 2) * BLK)
            seen = slice(b * BLK, (b + 2 * HALO + 2) * BLK)
            one = [slice((b + r) * BLK, (b + r + 1) * BLK) for r in range(2)]
            if remote:
                kf, vf = [[ref[at] for at in one] for ref in (far_keys, far_values)]
            else:
                there = [HALO + ((b + r) ^ bit) for r in range(2)]
                kf, vf = [
                    [ref[at * BLK : (at + 1) * BLK] for at in there] for ref in (keys, values)
                ]
            o, d, key_near, value_near, key_far, value_far = attend_pair(
                jnp.concatenate([graded[b, slot + k, 0], graded[b + 1, slot + k, 0]], axis=0),
                jnp.concatenate([graded[b, slot + k, 1], graded[b + 1, slot + k, 1]], axis=0),
                keys[seen],
                values[seen],
                kf,
                vf,
                near_biases(plane(place) * PLANE + b, width, 0, blocks),
                far_bias,
            )
            attended[own] = o
            dq[own] = d
            for acc, near in zip(accs, (key_near, value_near)):
                acc[:, seen] += near
            for acc, far_acc, far in zip(accs, far_accs, (key_far, value_far)):
                for r in range(2):
                    if remote:
                        far_acc[:, one[r]] = far[r]
                    else:
                        acc[:, there[r] * BLK : (there[r] + 1) * BLK] += far[r]
        for i, (acc, far_acc) in enumerate(zip(accs, far_accs)):
            if remote:
                target = (to_next, to_other)[k]
                for m in range(PLANE):
                    owed = far_acc[:, rows_of(me ^ m)] * scales[i]
                    target[m, i] = owed.astype(jnp.bfloat16)
            for m in range(PLANE):
                part[k, m, i] = acc[:, rows_of(HALO + (me ^ m))] * scales[i]
            for m in range(HALO):
                b = (me % HALO) ^ m
                at = m * group + k
                to_next[lead + at, i] = (acc[:, rows_of(next_at + b)] * scales[i]).astype(
                    jnp.bfloat16
                )
                to_last[at, i] = (acc[:, rows_of(last_at + b)] * scales[i]).astype(jnp.bfloat16)
        for m in range(PLANE):
            rows[m][slot + k, 0] = attended[rows_of(me ^ m)]
            rows[m][slot + k, 1] = dq[rows_of(me ^ m)]


def attend(place, widths, sections, pairs, graded, halos, far, group, first, slot, blocks, rows=()):
    count, _, width = pairs[0].shape[1:]
    tile = (BLK, width)
    remote = len(far)
    room = pairs[0].shape[0] + group
    bf16 = jnp.bfloat16
    owed = [(HALO * group + (PLANE if remote else 0), count, *tile), (HALO * group, count, *tile)]
    if remote:
        owed.append((PLANE, count, *tile))
    inputs = (*pairs, graded, *halos, *far, *rows)
    outs = pl.pallas_call(
        functools.partial(
            attend_kernel,
            first=first,
            slot=slot,
            group=group,
            remote=remote,
            blocks=blocks,
            aliased=len(rows),
        ),
        in_specs=[SMEM] * 3 + [VMEM] * len(inputs),
        out_specs=[VMEM] * (PLANE + 1 + len(owed)),
        out_shape=[jax.ShapeDtypeStruct((room, count, *tile), bf16)] * PLANE
        + [jax.ShapeDtypeStruct((group, PLANE, count, *tile), jnp.float32)]
        + [jax.ShapeDtypeStruct(shape, bf16) for shape in owed],
        scratch_shapes=[pltpu.VMEM((PADDED * BLK, width), bf16)] * 2
        + [pltpu.VMEM((PLANE * BLK, width), bf16)] * 4
        + [pltpu.VMEM((width, PADDED * BLK), jnp.float32)] * 2
        + [pltpu.VMEM((width, PLANE * BLK), jnp.float32)] * 2,
        input_output_aliases={3 + len(inputs) - len(rows) + m: m for m in range(len(rows))},
        compiler_params=LIMIT,
        cost_estimate=pl.CostEstimate(
            flops=group * PLANE * 12 * BLK * LINKED * width,
            transcendentals=group * PLANE * BLK * LINKED,
            bytes_accessed=40 * group * PLANE * BLK * width,
        ),
    )(place, widths, sections, *inputs)
    return outs[:PLANE], outs[PLANE], outs[PLANE + 1 :]


def combine_kernel(place, part, *refs, remote, base, aliased):
    with_other, (with_next, with_last) = refs[0], refs[remote : remote + 2]
    outs = refs[remote + 2 + aliased :]
    group = part.shape[0]
    lead = PLANE if remote else 0
    for m in range(PLANE):
        own_chip = m < HALO
        next_side = facing(place) if own_chip else jnp.logical_not(facing(place))
        for k in range(group):
            slot = (m % HALO) * group + k
            for i in range(part.shape[2]):
                owed = jnp.where(next_side, with_next[lead + slot, i], with_last[slot, i])
                total = part[k, m, i] + owed.astype(jnp.float32)
                if remote:
                    far = (with_next, with_other)[k]
                    total += far[m, i].astype(jnp.float32)
                outs[m][base + k, i] = jnp.transpose(total.astype(jnp.bfloat16))


def combine(place, part, owed, rows=(), base=0):
    group, _, *rest = part.shape
    inputs = (part, *owed, *rows)
    shape = rows[0].shape if rows else (group, *rest)
    return pl.pallas_call(
        functools.partial(
            combine_kernel, remote=len(owed) - 2, base=base, aliased=len(rows)
        ),
        in_specs=[SMEM] + [VMEM] * len(inputs),
        out_specs=[VMEM] * PLANE,
        out_shape=[jax.ShapeDtypeStruct(shape, jnp.bfloat16)] * PLANE,
        input_output_aliases={1 + len(inputs) - len(rows) + m: m for m in range(len(rows))},
        compiler_params=LIMIT,
        cost_estimate=moved_cost([part, *owed]),
    )(place, *inputs)


def partner(value, axis, apart):
    return lax.ppermute(value, axis, [(i, i ^ 1 << apart) for i in range(lax.axis_size(axis))])


def passed_along(value, axis, by):
    peers = lax.axis_size(axis)
    pairs = [(i, i + by) for i in range(peers) if 0 <= i + by < peers]
    return lax.ppermute(value, axis, pairs)


def to_slots(values, picker):
    return jnp.sum(jnp.where(picker[None, :, :, None], values[:, None, :, :], 0.0), axis=2)


def slots_to_heads(values, picker, filler):
    covered = jnp.any(picker, axis=0)
    summed = jnp.sum(jnp.where(picker[None, :, :, None], values[:, :, None, :], 0.0), axis=1)
    return jnp.where(covered[None, :, None], summed, filler)


def rows_slots_to_heads(values, picker):
    return jnp.einsum(
        "jqid,ih->jqhd", values, picker.astype(jnp.float32), precision=lax.Precision.HIGHEST
    )


def pick_heads(values, picker):
    chooser = picker.astype(jnp.bfloat16)
    return jnp.einsum("ih,jqhd->jqid", chooser, values, preferred_element_type=jnp.float32).astype(
        jnp.bfloat16
    )


def partner_route(values, section_index, low_bits):
    return partner(values, "seq", section_index - low_bits)


def partner_back(values, section_index, low_bits):
    return partner(values, "seq", section_index - low_bits)


def extend_blocks(values, reach, halo_blocks, blocks_dev, mover):
    pieces = [mover(values, distance) for distance in range(reach, 0, -1)]
    pieces = pieces + [values] + [mover(values, -distance) for distance in range(1, reach + 1)]
    start = reach * blocks_dev - halo_blocks
    whole = jnp.concatenate(pieces, axis=1)
    return whole


def move_keys(values, distance):
    return passed_along(values, "seq", distance)


def window_sets(extended, blocks_dev, spread):
    return jnp.stack(
        [extended[:, offset : offset + blocks_dev] for offset in range(spread)], axis=2
    )


def per_device(query_rows, key_rows, value_rows, out_grad, window_blocks, section_heads):
    tokens_dev, head_count, head_width = query_rows.shape
    blocks_dev = tokens_dev // BLK
    low_bits = blocks_dev.bit_length() - 1
    seq_count = lax.axis_size("seq")
    section_total = low_bits + seq_count.bit_length() - 1
    halo_blocks = WB - 1
    reach = (halo_blocks + blocks_dev - 1) // blocks_dev
    padding = reach * blocks_dev
    spread = 2 * WB - 1
    score_scale = 1.0 / math.sqrt(head_width)
    first_block = lax.axis_index("seq") * blocks_dev + jnp.arange(blocks_dev, dtype=jnp.int32)
    all_blocks = blocks_dev * seq_count
    query_blocks = query_rows.reshape(blocks_dev, BLK, head_count, head_width)
    key_blocks = key_rows.reshape(blocks_dev, BLK, head_count, head_width)
    value_blocks = value_rows.reshape(blocks_dev, BLK, head_count, head_width)
    grad_blocks = out_grad.reshape(blocks_dev, BLK, head_count, head_width)
    offsets = jnp.arange(spread, dtype=jnp.int32) - halo_blocks
    near_block = first_block[:, None] + offsets[None, :]
    in_range = (near_block >= 0) & (near_block < all_blocks)
    near_mask = in_range[:, None, :] & (
        jnp.abs(offsets)[None, None, :] < window_blocks[None, :, None]
    )
    wide_mask = near_mask[:, :, None, :, None]
    head_ids = jnp.arange(head_count, dtype=jnp.int32)
    paired = jnp.stack([key_blocks, value_blocks])
    extended = extend_blocks(paired, reach, halo_blocks, blocks_dev, move_keys)
    near_sets = window_sets(extended, blocks_dev, spread)
    near_keys = near_sets[0]
    near_values = near_sets[1]
    near_scores = (
        jnp.einsum("jqhd,jckhd->jhqck", query_blocks, near_keys, preferred_element_type=jnp.float32)
        * score_scale
    )
    near_scores = jnp.where(wide_mask, near_scores, blocked_score)
    top_score = jnp.max(near_scores, axis=(3, 4))
    records = []
    for section_index in range(section_total):
        picker = section_heads[section_index][:, None] == head_ids[None, :]
        slot_width = jnp.sum(jnp.where(picker, window_blocks[None, :], 0), axis=1)
        slot_valid = 2**section_index >= slot_width
        chosen_query = pick_heads(query_blocks, picker)
        chosen_grad = pick_heads(grad_blocks, picker)
        chosen_pair = jnp.stack([pick_heads(key_blocks, picker), pick_heads(value_blocks, picker)])
        partner_pair = partner_route(chosen_pair, section_index, low_bits)
        far_scores = (
            jnp.einsum(
                "jqid,jkid->jiqk", chosen_query, partner_pair[0], preferred_element_type=jnp.float32
            )
            * score_scale
        )
        far_scores = jnp.where(slot_valid[None, :, None, None], far_scores, blocked_score)
        top_score = jnp.maximum(
            top_score, slots_to_heads(jnp.max(far_scores, axis=3), picker, blocked_score)
        )
        records.append(
            (
                section_index,
                picker,
                slot_valid,
                chosen_query,
                chosen_grad,
                chosen_pair,
                partner_pair,
                far_scores,
            )
        )
    row_total = jnp.sum(
        jnp.where(wide_mask, jnp.exp(near_scores - top_score[:, :, :, None, None]), 0.0),
        axis=(3, 4),
    )
    for record in records:
        picker = record[1]
        slot_top = to_slots(top_score, picker)
        far_sum = jnp.sum(
            jnp.where(
                record[2][None, :, None, None], jnp.exp(record[7] - slot_top[:, :, :, None]), 0.0
            ),
            axis=3,
        )
        row_total = row_total + slots_to_heads(far_sum, picker, 0.0)
    log_total = top_score + jnp.log(row_total)
    near_probs = jnp.where(
        wide_mask, jnp.exp(near_scores - log_total[:, :, :, None, None]), 0.0
    ).astype(jnp.bfloat16)
    attended_sum = jnp.einsum(
        "jhqck,jckhd->jqhd", near_probs, near_values, preferred_element_type=jnp.float32
    )
    far_probs_list = []
    for record in records:
        picker = record[1]
        slot_lse = to_slots(log_total, picker)
        far_probs = jnp.where(
            record[2][None, :, None, None], jnp.exp(record[7] - slot_lse[:, :, :, None]), 0.0
        ).astype(jnp.bfloat16)
        far_probs_list.append((far_probs, slot_lse))
        attended_sum = attended_sum + rows_slots_to_heads(
            jnp.einsum(
                "jiqk,jkid->jqid", far_probs, record[6][1], preferred_element_type=jnp.float32
            ),
            picker,
        )
    attended = attended_sum.astype(jnp.bfloat16)
    row_delta = jnp.transpose(
        jnp.sum(grad_blocks.astype(jnp.float32) * attended.astype(jnp.float32), axis=-1), (0, 2, 1)
    )
    near_dprob = jnp.einsum(
        "jqhd,jckhd->jhqck", grad_blocks, near_values, preferred_element_type=jnp.float32
    )
    near_dscore = (
        near_probs.astype(jnp.float32) * (near_dprob - row_delta[:, :, :, None, None])
    ).astype(jnp.bfloat16)
    query_sum = jnp.einsum(
        "jhqck,jckhd->jqhd", near_dscore, near_keys, preferred_element_type=jnp.float32
    )
    far_dscores = []
    for record, probs_pair in zip(records, far_probs_list):
        picker = record[1]
        slot_delta = to_slots(row_delta, picker)
        far_dprob = jnp.einsum(
            "jqid,jkid->jiqk", record[4], record[6][1], preferred_element_type=jnp.float32
        )
        far_dscore = (
            probs_pair[0].astype(jnp.float32) * (far_dprob - slot_delta[:, :, :, None])
        ).astype(jnp.bfloat16)
        far_dscores.append((far_dscore, slot_delta))
        query_sum = query_sum + rows_slots_to_heads(
            jnp.einsum(
                "jiqk,jkid->jqid", far_dscore, record[6][0], preferred_element_type=jnp.float32
            ),
            picker,
        )
    query_grad = (
        (query_sum * score_scale).astype(jnp.bfloat16).reshape(tokens_dev, head_count, head_width)
    )
    near_key_part = (
        jnp.einsum(
            "jhqck,jqhd->jckhd", near_dscore, query_blocks, preferred_element_type=jnp.float32
        )
        * score_scale
    )
    near_value_part = jnp.einsum(
        "jhqck,jqhd->jckhd", near_probs, grad_blocks, preferred_element_type=jnp.float32
    )
    stacked_parts = jnp.stack([near_key_part, near_value_part])
    extended_count = blocks_dev + 2 * padding
    base = padding - halo_blocks
    extended_ids = jnp.arange(extended_count, dtype=jnp.int32)
    own_ids = jnp.arange(blocks_dev, dtype=jnp.int32)
    spread_ids = jnp.arange(spread, dtype=jnp.int32)
    placer = (
        extended_ids[:, None, None] == base + own_ids[None, :, None] + spread_ids[None, None, :]
    ).astype(jnp.float32)
    gathered = jnp.einsum(
        "ejc,xjckhd->xekhd", placer, stacked_parts, precision=lax.Precision.HIGHEST
    )
    own_grads = gathered[:, padding : padding + blocks_dev]
    for distance in range(1, reach + 1):
        lower_slab = gathered[
            :, padding - distance * blocks_dev : padding - (distance - 1) * blocks_dev
        ]
        own_grads = own_grads + passed_along(
            lower_slab.astype(jnp.bfloat16), "seq", -distance
        ).astype(lower_slab.dtype)
        upper_start = padding + blocks_dev + (distance - 1) * blocks_dev
        upper_slab = gathered[:, upper_start : upper_start + blocks_dev]
        own_grads = own_grads + passed_along(
            upper_slab.astype(jnp.bfloat16), "seq", distance
        ).astype(upper_slab.dtype)
    for record, probs_pair, dscore_pair in zip(records, far_probs_list, far_dscores):
        picker = record[1]
        key_part = (
            jnp.einsum(
                "jiqk,jqid->jkid", dscore_pair[0], record[3], preferred_element_type=jnp.float32
            )
            * score_scale
        )
        value_part = jnp.einsum(
            "jiqk,jqid->jkid", probs_pair[0], record[4], preferred_element_type=jnp.float32
        )
        returned = partner_back(jnp.stack([key_part, value_part]), record[0], low_bits)
        own_grads = own_grads + jnp.stack(
            [rows_slots_to_heads(returned[0], picker), rows_slots_to_heads(returned[1], picker)]
        )
    key_grad = own_grads[0].astype(jnp.bfloat16).reshape(tokens_dev, head_count, head_width)
    value_grad = own_grads[1].astype(jnp.bfloat16).reshape(tokens_dev, head_count, head_width)
    return (attended.reshape(tokens_dev, head_count, head_width), query_grad, key_grad, value_grad)


def in_plane(pieces, chip_first=False):
    peers = lax.axis_size("seq")
    pieces = list(pieces)
    for m in range(1, PLANE):
        pieces[m] = lax.ppermute(pieces[m], "seq", [(i, i ^ m) for i in range(peers)])
        if chip_first and m == 1:
            pieces = lax.optimization_barrier(pieces)
    return pieces


def with_next_plane(value):
    return partner(value, "seq", PLANE.bit_length() - 1)


def with_other_plane(value):
    return partner(value, "seq", PLANE.bit_length())


def with_last_plane(value):
    peers = lax.axis_size("seq")
    pairs = []
    for i in range(peers):
        other = i + PLANE if i // PLANE % 2 else i - PLANE
        if 0 <= other < peers:
            pairs.append((i, other))
    return lax.ppermute(value, "seq", pairs)


def plane_all_to_all(value):
    peers = lax.axis_size("seq")
    planes = [list(range(i, i + PLANE)) for i in range(0, peers, PLANE)]
    return lax.all_to_all(value, "seq", 0, 0, axis_index_groups=planes, tiled=True)


def sharded_by_plane(query_rows, key_rows, value_rows, out_grad, widths, sections):
    place = lax.axis_index("seq").astype(jnp.int32).reshape(1)
    blocks = lax.axis_size("seq")
    local = PLANE.bit_length() - 1
    total = sections.shape[0]
    groups = [tuple(range(local, total)), tuple(range(local))]
    order = tuple(s for group in groups for s in group)
    tables = (place, widths, sections)
    sent = pack(place, sections, [key_rows, value_rows], order, True)
    (graded_sent,) = pack(place, sections, [query_rows, out_grad], order, False)
    graded = plane_all_to_all(graded_sent)
    pairs = in_plane(sent)
    next_sent, last_sent = halo_parts(place, pairs)
    far_sent = far_parts(pairs, total - local)
    halos = [with_next_plane(next_sent), with_last_plane(last_sent)]
    halos[0], other_sent = lax.optimization_barrier((halos[0], far_sent[1]))
    far = (with_other_plane(other_sent), with_next_plane(far_sent[0]))
    rows, part_near, owed = attend(
        *tables, pairs, graded, halos, (), local, 0, total - local, blocks
    )
    owed_near = [with_next_plane(owed[0]), with_last_plane(owed[1])]
    rows, part_far, owed = attend(
        *tables, pairs, graded, halos, far, total - local, local, 0, blocks, rows
    )
    other_back = with_other_plane(owed[2])
    owed_far = [other_back, with_next_plane(owed[0]), with_last_plane(owed[1])]
    rows = in_plane(combine(place, part_near, owed_near, rows, total), True)
    attended, query_grad = unpack(place, sections, [(groups[0], rows, 0), (groups[1], rows, 1)])
    columns = in_plane(combine(place, part_far, owed_far))
    columns, attended, query_grad = lax.optimization_barrier((columns, attended, query_grad))
    key_grad, value_grad = unpack(place, sections, [(groups[0], columns, 0), (groups[1], rows, 2)])
    return attended, query_grad, key_grad, value_grad


def solution(mesh):
    spec = P(("grp", "seq"), None, None)
    peers = mesh.shape["seq"]

    def per_device_any(*args):
        tokens, heads, width = args[0].shape
        sections, listed = args[5].shape
        once = sections * listed == heads
        if tokens == BLK and once and listed == PLANE and 1 << sections == peers == PLANE**2:
            return sharded_by_plane(*args)
        return per_device(*args)

    return jax.shard_map(
        per_device_any,
        mesh=mesh,
        in_specs=(spec, spec, spec, spec, P(), P()),
        out_specs=(spec,) * 4,
        check_vma=False,
    )
```

```python
import functools
import math

import jax
import jax.numpy as jnp
from jax import lax
from jax.experimental import pallas as pl
from jax.experimental.pallas import tpu as pltpu
from jax.sharding import PartitionSpec as P

BLK = 128
WB = 3
HALO = WB - 1
SPAN = (2 * HALO + 1) * BLK
LINKED = SPAN + BLK
PLANE = 2 * HALO
PADDED = PLANE + 2 * HALO
NT = (((1,), (1,)), ((), ()))
NN = (((1,), (0,)), ((), ()))
blocked_score = -1e30


def mm(a, b, dims=NN):
    return lax.dot_general(a, b, dims, preferred_element_type=jnp.float32)


def moved_cost(arrays):
    return pl.CostEstimate(
        flops=0, transcendentals=0, bytes_accessed=4 * sum(a.size for a in arrays)
    )


def softmax_pair(score, far_score, biases, far_bias, scale2):
    near_parts, far_parts = [], []
    gap = jnp.zeros((BLK, BLK), jnp.bfloat16)
    for r in range(2):
        rows = slice(r * BLK, (r + 1) * BLK)
        sw = score[rows, r * BLK : r * BLK + SPAN] * scale2 + biases[r]
        sf = far_score[r] * scale2 + far_bias
        top = jnp.maximum(jnp.max(sw, axis=1, keepdims=True), jnp.max(sf, axis=1, keepdims=True))
        ew, ef = jnp.exp2(sw - top), jnp.exp2(sf - top)
        total = jnp.sum(ew, axis=1, keepdims=True) + jnp.sum(ef, axis=1, keepdims=True)
        inverse = 1.0 / total
        near = (ew * inverse).astype(jnp.bfloat16)
        near_parts.append(jnp.concatenate([near, gap] if r == 0 else [gap, near], axis=1))
        far_parts.append((ef * inverse).astype(jnp.bfloat16))
    return jnp.concatenate(near_parts, axis=0), far_parts


def attend_pair(q, g, kw, vw, kf, vf, biases, far_bias):
    scale = 1.0 / math.sqrt(q.shape[-1])
    scale2 = scale * math.log2(math.e)
    half = [slice(0, BLK), slice(BLK, 2 * BLK)]
    far_score = [mm(q[half[r]], kf[r], NT) for r in range(2)]
    near, far = softmax_pair(mm(q, kw, NT), far_score, biases, far_bias, scale2)
    far_out = jnp.concatenate([mm(far[r], vf[r]) for r in range(2)], axis=0)
    attended = (mm(near, vw) + far_out).astype(jnp.bfloat16)
    delta = jnp.sum(g.astype(jnp.float32) * attended.astype(jnp.float32), axis=1, keepdims=True)
    d_near = (near.astype(jnp.float32) * (mm(g, vw, NT) - delta)).astype(jnp.bfloat16)
    d_far = [
        (far[r].astype(jnp.float32) * (mm(g[half[r]], vf[r], NT) - delta[half[r]])).astype(
            jnp.bfloat16
        )
        for r in range(2)
    ]
    far_dq = jnp.concatenate([mm(d_far[r], kf[r]) for r in range(2)], axis=0)
    query_grad = ((mm(d_near, kw) + far_dq) * scale).astype(jnp.bfloat16)
    qt, gt = jnp.transpose(q), jnp.transpose(g)
    key_near, value_near = mm(qt, d_near), mm(gt, near)
    key_far = [mm(qt[:, half[r]], d_far[r]) for r in range(2)]
    value_far = [mm(gt[:, half[r]], far[r]) for r in range(2)]
    return attended, query_grad, key_near, value_near, key_far, value_far


def near_biases(b, width, low, high):
    offset = lax.broadcasted_iota(jnp.int32, (1, SPAN), 1) // BLK - HALO
    inside = jnp.abs(offset) < width
    out = []
    for r in range(2):
        there = offset + b + r
        out.append(jnp.where(inside & (there >= low) & (there < high), 0.0, blocked_score))
    return out


def rows_of(block):
    return pl.ds(pl.multiple_of(block * BLK, BLK), BLK)


def whole(shape):
    return pl.BlockSpec(shape, lambda *_: (0,) * len(shape))


SMEM = pl.BlockSpec(memory_space=pltpu.SMEM)
VMEM = pl.BlockSpec(memory_space=pltpu.VMEM)
LIMIT = pltpu.CompilerParams(vmem_limit_bytes=20 << 20)


def pack_kernel(place, sections, *refs, order, count, crossed):
    ins, outs, held = refs[:count], refs[count:-1], refs[-1]
    for i in range(count):
        held[i] = jnp.transpose(ins[i][...], (1, 0, 2))
    for m in range(PLANE):
        owner = seat(place) ^ m if crossed else m
        for k, s in enumerate(order):
            head = sections[s, owner]
            for i in range(count):
                if crossed:
                    outs[m][k, i] = held[i, head]
                else:
                    outs[0][m, k, i] = held[i, head]


def pack(place, sections, arrays, order, crossed):
    tokens, heads, width = arrays[0].shape
    chunk = tokens // 2
    count = len(arrays)
    shape = (len(order), count, tokens, width)
    if crossed:
        shapes = [shape] * PLANE
        specs = [pl.BlockSpec((*shape[:2], chunk, width), lambda i: (0, 0, i, 0))] * PLANE
    else:
        shapes = [(PLANE, *shape)]
        specs = [pl.BlockSpec((PLANE, *shape[:2], chunk, width), lambda i: (0, 0, 0, i, 0))]
    return pl.pallas_call(
        functools.partial(pack_kernel, order=order, count=count, crossed=crossed),
        grid=(tokens // chunk,),
        in_specs=[SMEM, SMEM]
        + [pl.BlockSpec((chunk, heads, width), lambda i: (i, 0, 0))] * count,
        out_specs=specs,
        out_shape=[jax.ShapeDtypeStruct(shape, jnp.bfloat16) for shape in shapes],
        scratch_shapes=[pltpu.VMEM((count, heads, chunk, width), jnp.bfloat16)],
        cost_estimate=moved_cost(arrays),
    )(place, sections, *arrays)


def unpack_kernel(place, sections, *refs, groups, count):
    pieces, outs, held = refs[: len(groups) * PLANE], refs[len(groups) * PLANE : -1], refs[-1]
    for number, group in enumerate(groups):
        for m in range(PLANE):
            for k, s in enumerate(group):
                head = sections[s, seat(place) ^ m]
                for i in range(count):
                    held[i, head] = pieces[number * PLANE + m][k, i]
    for i in range(count):
        outs[i][...] = jnp.transpose(held[i], (1, 0, 2))


def unpack(place, sections, parts):
    flat = [piece for _, pieces, _ in parts for piece in pieces]
    count, tokens, width = flat[0].shape[1:]
    heads = sections.size
    chunk = tokens // 2
    specs = [
        pl.BlockSpec((len(group), count, chunk, width), lambda i, run=run: (run, 0, i, 0))
        for group, _, run in parts
        for _ in range(PLANE)
    ]
    return pl.pallas_call(
        functools.partial(unpack_kernel, groups=[group for group, _, _ in parts], count=count),
        grid=(tokens // chunk,),
        in_specs=[SMEM, SMEM] + specs,
        out_specs=[pl.BlockSpec((chunk, heads, width), lambda i: (i, 0, 0))] * count,
        out_shape=[jax.ShapeDtypeStruct((tokens, heads, width), jnp.bfloat16)] * count,
        scratch_shapes=[pltpu.VMEM((count, heads, chunk, width), jnp.bfloat16)],
        compiler_params=LIMIT,
        cost_estimate=moved_cost(flat),
    )(place, sections, *flat)


def seat(place):
    return place[0] % PLANE


def plane(place):
    return place[0] // PLANE


def facing(place):
    return seat(place) // HALO == 1 - plane(place) % 2


def far_kernel(*refs):
    pieces, outs = refs[:PLANE], refs[PLANE:]
    for k, out in enumerate(outs):
        for m, piece in enumerate(pieces):
            out[m] = piece[k]


def far_parts(pieces, count):
    rest = pieces[0].shape[1:]
    return pl.pallas_call(
        far_kernel,
        in_specs=[VMEM] * PLANE,
        out_specs=[VMEM] * count,
        out_shape=[jax.ShapeDtypeStruct((PLANE, *rest), jnp.bfloat16)] * count,
        compiler_params=LIMIT,
        cost_estimate=moved_cost(pieces),
    )(*pieces)


def halo_kernel(place, *refs):
    pieces, (with_next, with_last) = refs[:PLANE], refs[PLANE:]
    slots = pieces[0].shape[0]

    def fill(base, other):
        for m in range(HALO):
            with_next[m * slots : (m + 1) * slots] = pieces[base + m][...]
            with_last[m * slots : (m + 1) * slots] = pieces[other + m][...]

    @pl.when(facing(place))
    def _():
        fill(0, HALO)

    @pl.when(jnp.logical_not(facing(place)))
    def _():
        fill(HALO, 0)


def halo_parts(place, pieces):
    slots, *rest = pieces[0].shape
    return pl.pallas_call(
        halo_kernel,
        in_specs=[SMEM] + [VMEM] * PLANE,
        out_specs=[VMEM] * 2,
        out_shape=[jax.ShapeDtypeStruct((HALO * slots, *rest), jnp.bfloat16)] * 2,
        compiler_params=LIMIT,
        cost_estimate=moved_cost(pieces),
    )(place, *pieces)


def attend_kernel(place, widths, sections, *refs, first, slot, group, picked, remote, blocks, aliased):
    pairs, (graded, with_next, with_last) = refs[:PLANE], refs[PLANE : PLANE + 3]
    rest = refs[PLANE + 3 :]
    if remote:
        far_in, rest = rest[0], rest[1:]
    rest = rest[aliased:]
    rows, rest = rest[:PLANE], rest[PLANE:]
    (to_next, to_last, part), rest = rest[:3], rest[3:]
    lead = PLANE if remote else 0
    if remote and 1 in picked:
        to_other, rest = rest[0], rest[1:]
    keys, values, far_keys, far_values, attended, dq = rest[:6]
    accs, far_accs = rest[6:8], rest[8:10]
    me = seat(place)
    scales = (1.0 / math.sqrt(keys.shape[-1]), 1.0)
    slots = with_next.shape[0] // HALO
    next_at = jnp.where(plane(place) % 2 == 0, HALO + PLANE, 0)
    last_at = HALO + PLANE - next_at
    for n, k in enumerate(picked):
        width = widths[sections[first + k, me]]
        bit = 1 << first + k
        far_bias = jnp.where(bit >= width, 0.0, blocked_score).astype(jnp.float32)
        for m in range(PLANE):
            keys[rows_of(HALO + (me ^ m))] = pairs[m][slot + k, 0]
            values[rows_of(HALO + (me ^ m))] = pairs[m][slot + k, 1]
        for m in range(HALO):
            b = (me % HALO) ^ m
            at = m * slots + slot + k
            keys[rows_of(next_at + b)] = with_next[at, 0]
            values[rows_of(next_at + b)] = with_next[at, 1]
            keys[rows_of(last_at + b)] = with_last[at, 0]
            values[rows_of(last_at + b)] = with_last[at, 1]
        if remote:
            for m in range(PLANE):
                far_keys[rows_of(me ^ m)] = far_in[m, 0]
                far_values[rows_of(me ^ m)] = far_in[m, 1]
        for acc in accs:
            acc[...] = jnp.zeros_like(acc)
        for b in range(0, PLANE, 2):
            own = slice(b * BLK, (b + 2) * BLK)
            seen = slice(b * BLK, (b + 2 * HALO + 2) * BLK)
            one = [slice((b + r) * BLK, (b + r + 1) * BLK) for r in range(2)]
            if remote:
                kf, vf = [[ref[at] for at in one] for ref in (far_keys, far_values)]
            else:
                there = [HALO + ((b + r) ^ bit) for r in range(2)]
                kf, vf = [
                    [ref[at * BLK : (at + 1) * BLK] for at in there] for ref in (keys, values)
                ]
            o, d, key_near, value_near, key_far, value_far = attend_pair(
                jnp.concatenate([graded[b, slot + k, 0], graded[b + 1, slot + k, 0]], axis=0),
                jnp.concatenate([graded[b, slot + k, 1], graded[b + 1, slot + k, 1]], axis=0),
                keys[seen],
                values[seen],
                kf,
                vf,
                near_biases(plane(place) * PLANE + b, width, 0, blocks),
                far_bias,
            )
            attended[own] = o
            dq[own] = d
            for acc, near in zip(accs, (key_near, value_near)):
                acc[:, seen] += near
            for acc, far_acc, far in zip(accs, far_accs, (key_far, value_far)):
                for r in range(2):
                    if remote:
                        far_acc[:, one[r]] = far[r]
                    else:
                        acc[:, there[r] * BLK : (there[r] + 1) * BLK] += far[r]
        for i, (acc, far_acc) in enumerate(zip(accs, far_accs)):
            if remote:
                target = to_other if k else to_next
                for m in range(PLANE):
                    owed = far_acc[:, rows_of(me ^ m)] * scales[i]
                    target[m, i] = owed.astype(jnp.bfloat16)
            for m in range(PLANE):
                part[n, m, i] = acc[:, rows_of(HALO + (me ^ m))] * scales[i]
            for m in range(HALO):
                b = (me % HALO) ^ m
                at = m * group + k
                to_next[lead + at, i] = (acc[:, rows_of(next_at + b)] * scales[i]).astype(
                    jnp.bfloat16
                )
                to_last[at, i] = (acc[:, rows_of(last_at + b)] * scales[i]).astype(jnp.bfloat16)
        for m in range(PLANE):
            rows[m][slot + k, 0] = attended[rows_of(me ^ m)]
            rows[m][slot + k, 1] = dq[rows_of(me ^ m)]


def attend(place, widths, sections, pairs, graded, halos, far, group, first, slot, blocks, picked, shared=()):
    count, _, width = pairs[0].shape[1:]
    tile = (BLK, width)
    bf16 = jnp.bfloat16
    inputs = (*pairs, graded, *halos, *far, *shared)
    sizes = [HALO * group + (PLANE if far else 0), HALO * group]
    outs = [jax.ShapeDtypeStruct((pairs[0].shape[0] + group, count, *tile), bf16)] * PLANE
    outs += [jax.ShapeDtypeStruct((size, count, *tile), bf16) for size in sizes]
    outs.append(jax.ShapeDtypeStruct((len(picked), PLANE, count, *tile), jnp.float32))
    if far and 1 in picked:
        outs.append(jax.ShapeDtypeStruct((PLANE, count, *tile), bf16))
    outs = pl.pallas_call(
        functools.partial(
            attend_kernel,
            first=first,
            slot=slot,
            group=group,
            picked=picked,
            remote=len(far),
            blocks=blocks,
            aliased=len(shared),
        ),
        in_specs=[SMEM] * 3 + [VMEM] * len(inputs),
        out_specs=[VMEM] * len(outs),
        out_shape=outs,
        scratch_shapes=[pltpu.VMEM((PADDED * BLK, width), bf16)] * 2
        + [pltpu.VMEM((PLANE * BLK, width), bf16)] * 4
        + [pltpu.VMEM((width, PADDED * BLK), jnp.float32)] * 2
        + [pltpu.VMEM((width, PLANE * BLK), jnp.float32)] * 2,
        input_output_aliases={3 + len(inputs) - len(shared) + m: m for m in range(len(shared))},
        compiler_params=LIMIT,
        cost_estimate=pl.CostEstimate(
            flops=len(picked) * PLANE * 12 * BLK * LINKED * width,
            transcendentals=len(picked) * PLANE * BLK * LINKED,
            bytes_accessed=40 * len(picked) * PLANE * BLK * width,
        ),
    )(place, widths, sections, *inputs)
    return outs[:PLANE], outs[PLANE : PLANE + 2], outs[PLANE + 2 :]


def combine_kernel(place, *refs, parts, remote, base, aliased):
    pieces, rest = refs[:parts], refs[parts:]
    if remote:
        with_other, rest = rest[0], rest[1:]
    (with_next, with_last), outs = rest[:2], rest[2 + aliased :]
    each = pieces[0].shape[0]
    group = each * parts
    lead = PLANE if remote else 0
    for m in range(PLANE):
        own_chip = m < HALO
        next_side = facing(place) if own_chip else jnp.logical_not(facing(place))
        for k in range(group):
            slot = (m % HALO) * group + k
            for i in range(pieces[0].shape[2]):
                owed = jnp.where(next_side, with_next[lead + slot, i], with_last[slot, i])
                total = pieces[k // each][k % each, m, i] + owed.astype(jnp.float32)
                if remote:
                    far = (with_next, with_other)[k]
                    total += far[m, i].astype(jnp.float32)
                outs[m][base + k, i] = jnp.transpose(total.astype(jnp.bfloat16))


def combine(place, parts, owed, rows=(), base=0):
    each, _, *rest = parts[0].shape
    inputs = (*parts, *owed, *rows)
    shape = rows[0].shape if rows else (each * len(parts), *rest)
    return pl.pallas_call(
        functools.partial(
            combine_kernel, parts=len(parts), remote=len(owed) > 2, base=base, aliased=len(rows)
        ),
        in_specs=[SMEM] + [VMEM] * len(inputs),
        out_specs=[VMEM] * PLANE,
        out_shape=[jax.ShapeDtypeStruct(shape, jnp.bfloat16)] * PLANE,
        input_output_aliases={1 + len(inputs) - len(rows) + m: m for m in range(len(rows))},
        compiler_params=LIMIT,
        cost_estimate=moved_cost([*parts, *owed]),
    )(place, *inputs)


def partner(value, axis, apart):
    return lax.ppermute(value, axis, [(i, i ^ 1 << apart) for i in range(lax.axis_size(axis))])


def passed_along(value, axis, by):
    peers = lax.axis_size(axis)
    pairs = [(i, i + by) for i in range(peers) if 0 <= i + by < peers]
    return lax.ppermute(value, axis, pairs)


def to_slots(values, picker):
    return jnp.sum(jnp.where(picker[None, :, :, None], values[:, None, :, :], 0.0), axis=2)


def slots_to_heads(values, picker, filler):
    covered = jnp.any(picker, axis=0)
    summed = jnp.sum(jnp.where(picker[None, :, :, None], values[:, :, None, :], 0.0), axis=1)
    return jnp.where(covered[None, :, None], summed, filler)


def rows_slots_to_heads(values, picker):
    return jnp.einsum(
        "jqid,ih->jqhd", values, picker.astype(jnp.float32), precision=lax.Precision.HIGHEST
    )


def pick_heads(values, picker):
    chooser = picker.astype(jnp.bfloat16)
    return jnp.einsum("ih,jqhd->jqid", chooser, values, preferred_element_type=jnp.float32).astype(
        jnp.bfloat16
    )


def partner_route(values, section_index, low_bits):
    return partner(values, "seq", section_index - low_bits)


def partner_back(values, section_index, low_bits):
    return partner(values, "seq", section_index - low_bits)


def extend_blocks(values, reach, halo_blocks, blocks_dev, mover):
    pieces = [mover(values, distance) for distance in range(reach, 0, -1)]
    pieces = pieces + [values] + [mover(values, -distance) for distance in range(1, reach + 1)]
    start = reach * blocks_dev - halo_blocks
    whole = jnp.concatenate(pieces, axis=1)
    return whole


def move_keys(values, distance):
    return passed_along(values, "seq", distance)


def window_sets(extended, blocks_dev, spread):
    return jnp.stack(
        [extended[:, offset : offset + blocks_dev] for offset in range(spread)], axis=2
    )


def per_device(query_rows, key_rows, value_rows, out_grad, window_blocks, section_heads):
    tokens_dev, head_count, head_width = query_rows.shape
    blocks_dev = tokens_dev // BLK
    low_bits = blocks_dev.bit_length() - 1
    seq_count = lax.axis_size("seq")
    section_total = low_bits + seq_count.bit_length() - 1
    halo_blocks = WB - 1
    reach = (halo_blocks + blocks_dev - 1) // blocks_dev
    padding = reach * blocks_dev
    spread = 2 * WB - 1
    score_scale = 1.0 / math.sqrt(head_width)
    first_block = lax.axis_index("seq") * blocks_dev + jnp.arange(blocks_dev, dtype=jnp.int32)
    all_blocks = blocks_dev * seq_count
    query_blocks = query_rows.reshape(blocks_dev, BLK, head_count, head_width)
    key_blocks = key_rows.reshape(blocks_dev, BLK, head_count, head_width)
    value_blocks = value_rows.reshape(blocks_dev, BLK, head_count, head_width)
    grad_blocks = out_grad.reshape(blocks_dev, BLK, head_count, head_width)
    offsets = jnp.arange(spread, dtype=jnp.int32) - halo_blocks
    near_block = first_block[:, None] + offsets[None, :]
    in_range = (near_block >= 0) & (near_block < all_blocks)
    near_mask = in_range[:, None, :] & (
        jnp.abs(offsets)[None, None, :] < window_blocks[None, :, None]
    )
    wide_mask = near_mask[:, :, None, :, None]
    head_ids = jnp.arange(head_count, dtype=jnp.int32)
    paired = jnp.stack([key_blocks, value_blocks])
    extended = extend_blocks(paired, reach, halo_blocks, blocks_dev, move_keys)
    near_sets = window_sets(extended, blocks_dev, spread)
    near_keys = near_sets[0]
    near_values = near_sets[1]
    near_scores = (
        jnp.einsum("jqhd,jckhd->jhqck", query_blocks, near_keys, preferred_element_type=jnp.float32)
        * score_scale
    )
    near_scores = jnp.where(wide_mask, near_scores, blocked_score)
    top_score = jnp.max(near_scores, axis=(3, 4))
    records = []
    for section_index in range(section_total):
        picker = section_heads[section_index][:, None] == head_ids[None, :]
        slot_width = jnp.sum(jnp.where(picker, window_blocks[None, :], 0), axis=1)
        slot_valid = 2**section_index >= slot_width
        chosen_query = pick_heads(query_blocks, picker)
        chosen_grad = pick_heads(grad_blocks, picker)
        chosen_pair = jnp.stack([pick_heads(key_blocks, picker), pick_heads(value_blocks, picker)])
        partner_pair = partner_route(chosen_pair, section_index, low_bits)
        far_scores = (
            jnp.einsum(
                "jqid,jkid->jiqk", chosen_query, partner_pair[0], preferred_element_type=jnp.float32
            )
            * score_scale
        )
        far_scores = jnp.where(slot_valid[None, :, None, None], far_scores, blocked_score)
        top_score = jnp.maximum(
            top_score, slots_to_heads(jnp.max(far_scores, axis=3), picker, blocked_score)
        )
        records.append(
            (
                section_index,
                picker,
                slot_valid,
                chosen_query,
                chosen_grad,
                chosen_pair,
                partner_pair,
                far_scores,
            )
        )
    row_total = jnp.sum(
        jnp.where(wide_mask, jnp.exp(near_scores - top_score[:, :, :, None, None]), 0.0),
        axis=(3, 4),
    )
    for record in records:
        picker = record[1]
        slot_top = to_slots(top_score, picker)
        far_sum = jnp.sum(
            jnp.where(
                record[2][None, :, None, None], jnp.exp(record[7] - slot_top[:, :, :, None]), 0.0
            ),
            axis=3,
        )
        row_total = row_total + slots_to_heads(far_sum, picker, 0.0)
    log_total = top_score + jnp.log(row_total)
    near_probs = jnp.where(
        wide_mask, jnp.exp(near_scores - log_total[:, :, :, None, None]), 0.0
    ).astype(jnp.bfloat16)
    attended_sum = jnp.einsum(
        "jhqck,jckhd->jqhd", near_probs, near_values, preferred_element_type=jnp.float32
    )
    far_probs_list = []
    for record in records:
        picker = record[1]
        slot_lse = to_slots(log_total, picker)
        far_probs = jnp.where(
            record[2][None, :, None, None], jnp.exp(record[7] - slot_lse[:, :, :, None]), 0.0
        ).astype(jnp.bfloat16)
        far_probs_list.append((far_probs, slot_lse))
        attended_sum = attended_sum + rows_slots_to_heads(
            jnp.einsum(
                "jiqk,jkid->jqid", far_probs, record[6][1], preferred_element_type=jnp.float32
            ),
            picker,
        )
    attended = attended_sum.astype(jnp.bfloat16)
    row_delta = jnp.transpose(
        jnp.sum(grad_blocks.astype(jnp.float32) * attended.astype(jnp.float32), axis=-1), (0, 2, 1)
    )
    near_dprob = jnp.einsum(
        "jqhd,jckhd->jhqck", grad_blocks, near_values, preferred_element_type=jnp.float32
    )
    near_dscore = (
        near_probs.astype(jnp.float32) * (near_dprob - row_delta[:, :, :, None, None])
    ).astype(jnp.bfloat16)
    query_sum = jnp.einsum(
        "jhqck,jckhd->jqhd", near_dscore, near_keys, preferred_element_type=jnp.float32
    )
    far_dscores = []
    for record, probs_pair in zip(records, far_probs_list):
        picker = record[1]
        slot_delta = to_slots(row_delta, picker)
        far_dprob = jnp.einsum(
            "jqid,jkid->jiqk", record[4], record[6][1], preferred_element_type=jnp.float32
        )
        far_dscore = (
            probs_pair[0].astype(jnp.float32) * (far_dprob - slot_delta[:, :, :, None])
        ).astype(jnp.bfloat16)
        far_dscores.append((far_dscore, slot_delta))
        query_sum = query_sum + rows_slots_to_heads(
            jnp.einsum(
                "jiqk,jkid->jqid", far_dscore, record[6][0], preferred_element_type=jnp.float32
            ),
            picker,
        )
    query_grad = (
        (query_sum * score_scale).astype(jnp.bfloat16).reshape(tokens_dev, head_count, head_width)
    )
    near_key_part = (
        jnp.einsum(
            "jhqck,jqhd->jckhd", near_dscore, query_blocks, preferred_element_type=jnp.float32
        )
        * score_scale
    )
    near_value_part = jnp.einsum(
        "jhqck,jqhd->jckhd", near_probs, grad_blocks, preferred_element_type=jnp.float32
    )
    stacked_parts = jnp.stack([near_key_part, near_value_part])
    extended_count = blocks_dev + 2 * padding
    base = padding - halo_blocks
    extended_ids = jnp.arange(extended_count, dtype=jnp.int32)
    own_ids = jnp.arange(blocks_dev, dtype=jnp.int32)
    spread_ids = jnp.arange(spread, dtype=jnp.int32)
    placer = (
        extended_ids[:, None, None] == base + own_ids[None, :, None] + spread_ids[None, None, :]
    ).astype(jnp.float32)
    gathered = jnp.einsum(
        "ejc,xjckhd->xekhd", placer, stacked_parts, precision=lax.Precision.HIGHEST
    )
    own_grads = gathered[:, padding : padding + blocks_dev]
    for distance in range(1, reach + 1):
        lower_slab = gathered[
            :, padding - distance * blocks_dev : padding - (distance - 1) * blocks_dev
        ]
        own_grads = own_grads + passed_along(
            lower_slab.astype(jnp.bfloat16), "seq", -distance
        ).astype(lower_slab.dtype)
        upper_start = padding + blocks_dev + (distance - 1) * blocks_dev
        upper_slab = gathered[:, upper_start : upper_start + blocks_dev]
        own_grads = own_grads + passed_along(
            upper_slab.astype(jnp.bfloat16), "seq", distance
        ).astype(upper_slab.dtype)
    for record, probs_pair, dscore_pair in zip(records, far_probs_list, far_dscores):
        picker = record[1]
        key_part = (
            jnp.einsum(
                "jiqk,jqid->jkid", dscore_pair[0], record[3], preferred_element_type=jnp.float32
            )
            * score_scale
        )
        value_part = jnp.einsum(
            "jiqk,jqid->jkid", probs_pair[0], record[4], preferred_element_type=jnp.float32
        )
        returned = partner_back(jnp.stack([key_part, value_part]), record[0], low_bits)
        own_grads = own_grads + jnp.stack(
            [rows_slots_to_heads(returned[0], picker), rows_slots_to_heads(returned[1], picker)]
        )
    key_grad = own_grads[0].astype(jnp.bfloat16).reshape(tokens_dev, head_count, head_width)
    value_grad = own_grads[1].astype(jnp.bfloat16).reshape(tokens_dev, head_count, head_width)
    return (attended.reshape(tokens_dev, head_count, head_width), query_grad, key_grad, value_grad)


def in_plane(pieces, chip_first=False):
    peers = lax.axis_size("seq")
    pieces = list(pieces)
    for m in range(1, PLANE):
        pieces[m] = lax.ppermute(pieces[m], "seq", [(i, i ^ m) for i in range(peers)])
        if chip_first and m == 1:
            pieces = lax.optimization_barrier(pieces)
    return pieces


def with_next_plane(value):
    return partner(value, "seq", PLANE.bit_length() - 1)


def with_other_plane(value):
    return partner(value, "seq", PLANE.bit_length())


def with_last_plane(value):
    peers = lax.axis_size("seq")
    pairs = []
    for i in range(peers):
        other = i + PLANE if i // PLANE % 2 else i - PLANE
        if 0 <= other < peers:
            pairs.append((i, other))
    return lax.ppermute(value, "seq", pairs)


def plane_all_to_all(value):
    peers = lax.axis_size("seq")
    planes = [list(range(i, i + PLANE)) for i in range(0, peers, PLANE)]
    return lax.all_to_all(value, "seq", 0, 0, axis_index_groups=planes, tiled=True)


def sharded_by_plane(query_rows, key_rows, value_rows, out_grad, widths, sections):
    place = lax.axis_index("seq").astype(jnp.int32).reshape(1)
    blocks = lax.axis_size("seq")
    local = PLANE.bit_length() - 1
    total = sections.shape[0]
    groups = [tuple(range(local, total)), tuple(range(local))]
    order = tuple(s for group in groups for s in group)
    tables = (place, widths, sections)
    sent = pack(place, sections, [key_rows, value_rows], order, True)
    (graded_sent,) = pack(place, sections, [query_rows, out_grad], order, False)
    graded = plane_all_to_all(graded_sent)
    pairs = in_plane(sent)
    next_sent, last_sent = halo_parts(place, pairs)
    far_sent = far_parts(pairs, total - local)
    halos = [with_next_plane(next_sent), with_last_plane(last_sent)]
    halos[0], other_sent = lax.optimization_barrier((halos[0], far_sent[1]))
    far = (with_other_plane(other_sent), with_next_plane(far_sent[0]))
    given = (*tables, pairs, graded, halos)
    size = total - local
    rows, owed, (part_near,) = attend(*given, (), local, 0, size, blocks, range(local))
    owed_near = [with_next_plane(owed[0]), with_last_plane(owed[1])]
    rows, owed, (part_next,) = attend(*given, (far[1],), size, local, 0, blocks, (0,), rows)
    rows, owed, (part_other, far_other) = attend(
        *given, (far[0],), size, local, 0, blocks, (1,), (*rows, *owed)
    )
    other_back = with_other_plane(far_other)
    owed_far = [other_back, with_next_plane(owed[0]), with_last_plane(owed[1])]
    rows = in_plane(combine(place, [part_near], owed_near, rows, total), True)
    columns = in_plane(combine(place, [part_next, part_other], owed_far))
    attended, query_grad = unpack(place, sections, [(groups[0], rows, 0), (groups[1], rows, 1)])
    columns, attended, query_grad = lax.optimization_barrier((columns, attended, query_grad))
    key_grad, value_grad = unpack(place, sections, [(groups[0], columns, 0), (groups[1], rows, 2)])
    return attended, query_grad, key_grad, value_grad


def solution(mesh):
    spec = P(("grp", "seq"), None, None)
    peers = mesh.shape["seq"]

    def per_device_any(*args):
        tokens, heads, width = args[0].shape
        sections, listed = args[5].shape
        once = sections * listed == heads
        if tokens == BLK and once and listed == PLANE and 1 << sections == peers == PLANE**2:
            return sharded_by_plane(*args)
        return per_device(*args)

    return jax.shard_map(
        per_device_any,
        mesh=mesh,
        in_specs=(spec, spec, spec, spec, P(), P()),
        out_specs=(spec,) * 4,
        check_vma=False,
    )
```

```python
import functools
import math

import jax
import jax.numpy as jnp
from jax import lax
from jax.experimental import pallas as pl
from jax.experimental.pallas import tpu as pltpu
from jax.sharding import PartitionSpec as P

BLK = 128
WB = 3
HALO = WB - 1
SPAN = (2 * HALO + 1) * BLK
LINKED = SPAN + BLK
PLANE = 2 * HALO
PADDED = PLANE + 2 * HALO
NT = (((1,), (1,)), ((), ()))
NN = (((1,), (0,)), ((), ()))
blocked_score = -1e30


def mm(a, b, dims=NN):
    return lax.dot_general(a, b, dims, preferred_element_type=jnp.float32)


def moved_cost(arrays):
    return pl.CostEstimate(
        flops=0, transcendentals=0, bytes_accessed=4 * sum(a.size for a in arrays)
    )


def softmax_pair(score, far_score, biases, far_bias, scale2):
    near_parts, far_parts = [], []
    gap = jnp.zeros((BLK, BLK), jnp.bfloat16)
    for r in range(2):
        rows = slice(r * BLK, (r + 1) * BLK)
        sw = score[rows, r * BLK : r * BLK + SPAN] * scale2 + biases[r]
        sf = far_score[r] * scale2 + far_bias
        top = jnp.maximum(jnp.max(sw, axis=1, keepdims=True), jnp.max(sf, axis=1, keepdims=True))
        ew, ef = jnp.exp2(sw - top), jnp.exp2(sf - top)
        total = jnp.sum(ew, axis=1, keepdims=True) + jnp.sum(ef, axis=1, keepdims=True)
        inverse = 1.0 / total
        near = (ew * inverse).astype(jnp.bfloat16)
        near_parts.append(jnp.concatenate([near, gap] if r == 0 else [gap, near], axis=1))
        far_parts.append((ef * inverse).astype(jnp.bfloat16))
    return jnp.concatenate(near_parts, axis=0), far_parts


def attend_pair(q, g, kw, vw, kf, vf, biases, far_bias):
    scale = 1.0 / math.sqrt(q.shape[-1])
    scale2 = scale * math.log2(math.e)
    half = [slice(0, BLK), slice(BLK, 2 * BLK)]
    far_score = [mm(q[half[r]], kf[r], NT) for r in range(2)]
    near, far = softmax_pair(mm(q, kw, NT), far_score, biases, far_bias, scale2)
    far_out = jnp.concatenate([mm(far[r], vf[r]) for r in range(2)], axis=0)
    attended = (mm(near, vw) + far_out).astype(jnp.bfloat16)
    delta = jnp.sum(g.astype(jnp.float32) * attended.astype(jnp.float32), axis=1, keepdims=True)
    d_near = (near.astype(jnp.float32) * (mm(g, vw, NT) - delta)).astype(jnp.bfloat16)
    d_far = [
        (far[r].astype(jnp.float32) * (mm(g[half[r]], vf[r], NT) - delta[half[r]])).astype(
            jnp.bfloat16
        )
        for r in range(2)
    ]
    far_dq = jnp.concatenate([mm(d_far[r], kf[r]) for r in range(2)], axis=0)
    query_grad = ((mm(d_near, kw) + far_dq) * scale).astype(jnp.bfloat16)
    qt, gt = jnp.transpose(q), jnp.transpose(g)
    key_near, value_near = mm(qt, d_near), mm(gt, near)
    key_far = [mm(qt[:, half[r]], d_far[r]) for r in range(2)]
    value_far = [mm(gt[:, half[r]], far[r]) for r in range(2)]
    return attended, query_grad, key_near, value_near, key_far, value_far


def near_biases(b, width, low, high):
    offset = lax.broadcasted_iota(jnp.int32, (1, SPAN), 1) // BLK - HALO
    inside = jnp.abs(offset) < width
    out = []
    for r in range(2):
        there = offset + b + r
        out.append(jnp.where(inside & (there >= low) & (there < high), 0.0, blocked_score))
    return out


def rows_of(block):
    return pl.ds(pl.multiple_of(block * BLK, BLK), BLK)


def whole(shape):
    return pl.BlockSpec(shape, lambda *_: (0,) * len(shape))


SMEM = pl.BlockSpec(memory_space=pltpu.SMEM)
VMEM = pl.BlockSpec(memory_space=pltpu.VMEM)
LIMIT = pltpu.CompilerParams(vmem_limit_bytes=20 << 20)


def pack_kernel(place, sections, *refs, order, count, crossed):
    ins, outs, held = refs[:count], refs[count:-1], refs[-1]
    for i in range(count):
        held[i] = jnp.transpose(ins[i][...], (1, 0, 2))
    for m in range(PLANE):
        owner = seat(place) ^ m if crossed else m
        for k, s in enumerate(order):
            head = sections[s, owner]
            for i in range(count):
                if crossed:
                    outs[m][k, i] = held[i, head]
                else:
                    outs[0][m, k, i] = held[i, head]


def pack(place, sections, arrays, order, crossed):
    tokens, heads, width = arrays[0].shape
    chunk = tokens // 2
    count = len(arrays)
    shape = (len(order), count, tokens, width)
    if crossed:
        shapes = [shape] * PLANE
        specs = [pl.BlockSpec((*shape[:2], chunk, width), lambda i: (0, 0, i, 0))] * PLANE
    else:
        shapes = [(PLANE, *shape)]
        specs = [pl.BlockSpec((PLANE, *shape[:2], chunk, width), lambda i: (0, 0, 0, i, 0))]
    return pl.pallas_call(
        functools.partial(pack_kernel, order=order, count=count, crossed=crossed),
        grid=(tokens // chunk,),
        in_specs=[SMEM, SMEM]
        + [pl.BlockSpec((chunk, heads, width), lambda i: (i, 0, 0))] * count,
        out_specs=specs,
        out_shape=[jax.ShapeDtypeStruct(shape, jnp.bfloat16) for shape in shapes],
        scratch_shapes=[pltpu.VMEM((count, heads, chunk, width), jnp.bfloat16)],
        cost_estimate=moved_cost(arrays),
    )(place, sections, *arrays)


def unpack_kernel(place, sections, *refs, groups, count):
    pieces, outs, held = refs[: len(groups) * PLANE], refs[len(groups) * PLANE : -1], refs[-1]
    for number, group in enumerate(groups):
        for m in range(PLANE):
            for k, s in enumerate(group):
                head = sections[s, seat(place) ^ m]
                for i in range(count):
                    held[i, head] = pieces[number * PLANE + m][k, i]
    for i in range(count):
        outs[i][...] = jnp.transpose(held[i], (1, 0, 2))


def unpack(place, sections, parts):
    flat = [piece for _, pieces, _ in parts for piece in pieces]
    count, tokens, width = flat[0].shape[1:]
    heads = sections.size
    chunk = tokens // 2
    specs = [
        pl.BlockSpec((len(group), count, chunk, width), lambda i, run=run: (run, 0, i, 0))
        for group, _, run in parts
        for _ in range(PLANE)
    ]
    return pl.pallas_call(
        functools.partial(unpack_kernel, groups=[group for group, _, _ in parts], count=count),
        grid=(tokens // chunk,),
        in_specs=[SMEM, SMEM] + specs,
        out_specs=[pl.BlockSpec((chunk, heads, width), lambda i: (i, 0, 0))] * count,
        out_shape=[jax.ShapeDtypeStruct((tokens, heads, width), jnp.bfloat16)] * count,
        scratch_shapes=[pltpu.VMEM((count, heads, chunk, width), jnp.bfloat16)],
        compiler_params=LIMIT,
        cost_estimate=moved_cost(flat),
    )(place, sections, *flat)


def seat(place):
    return place[0] % PLANE


def plane(place):
    return place[0] // PLANE


def facing(place):
    return seat(place) // HALO == 1 - plane(place) % 2


def far_kernel(*refs):
    pieces, outs = refs[:PLANE], refs[PLANE:]
    for k, out in enumerate(outs):
        for m, piece in enumerate(pieces):
            out[m] = piece[k]


def far_parts(pieces, count):
    rest = pieces[0].shape[1:]
    return pl.pallas_call(
        far_kernel,
        in_specs=[VMEM] * PLANE,
        out_specs=[VMEM] * count,
        out_shape=[jax.ShapeDtypeStruct((PLANE, *rest), jnp.bfloat16)] * count,
        compiler_params=LIMIT,
        cost_estimate=moved_cost(pieces),
    )(*pieces)


def halo_kernel(place, *refs):
    pieces, (with_next, with_last) = refs[:PLANE], refs[PLANE:]
    slots = pieces[0].shape[0]

    def fill(base, other):
        for m in range(HALO):
            with_next[m * slots : (m + 1) * slots] = pieces[base + m][...]
            with_last[m * slots : (m + 1) * slots] = pieces[other + m][...]

    @pl.when(facing(place))
    def _():
        fill(0, HALO)

    @pl.when(jnp.logical_not(facing(place)))
    def _():
        fill(HALO, 0)


def halo_parts(place, pieces):
    slots, *rest = pieces[0].shape
    return pl.pallas_call(
        halo_kernel,
        in_specs=[SMEM] + [VMEM] * PLANE,
        out_specs=[VMEM] * 2,
        out_shape=[jax.ShapeDtypeStruct((HALO * slots, *rest), jnp.bfloat16)] * 2,
        compiler_params=LIMIT,
        cost_estimate=moved_cost(pieces),
    )(place, *pieces)


def attend_kernel(place, widths, sections, *refs, first, slot, group, picked, remote, blocks, aliased):
    pairs, (graded, with_next, with_last) = refs[:PLANE], refs[PLANE : PLANE + 3]
    rest = refs[PLANE + 3 :]
    if remote:
        far_in, rest = rest[0], rest[1:]
    rest = rest[aliased:]
    rows, rest = rest[:PLANE], rest[PLANE:]
    (to_next, to_last, part), rest = rest[:3], rest[3:]
    lead = PLANE if remote else 0
    if remote and 1 in picked:
        to_other, rest = rest[0], rest[1:]
    keys, values, far_keys, far_values, attended, dq = rest[:6]
    accs, far_accs = rest[6:8], rest[8:10]
    me = seat(place)
    scales = (1.0 / math.sqrt(keys.shape[-1]), 1.0)
    slots = with_next.shape[0] // HALO
    next_at = jnp.where(plane(place) % 2 == 0, HALO + PLANE, 0)
    last_at = HALO + PLANE - next_at
    for n, k in enumerate(picked):
        width = widths[sections[first + k, me]]
        bit = 1 << first + k
        far_bias = jnp.where(bit >= width, 0.0, blocked_score).astype(jnp.float32)
        for m in range(PLANE):
            keys[rows_of(HALO + (me ^ m))] = pairs[m][slot + k, 0]
            values[rows_of(HALO + (me ^ m))] = pairs[m][slot + k, 1]
        for m in range(HALO):
            b = (me % HALO) ^ m
            at = m * slots + slot + k
            keys[rows_of(next_at + b)] = with_next[at, 0]
            values[rows_of(next_at + b)] = with_next[at, 1]
            keys[rows_of(last_at + b)] = with_last[at, 0]
            values[rows_of(last_at + b)] = with_last[at, 1]
        if remote:
            for m in range(PLANE):
                far_keys[rows_of(me ^ m)] = far_in[m, 0]
                far_values[rows_of(me ^ m)] = far_in[m, 1]
        for acc in accs:
            acc[...] = jnp.zeros_like(acc)
        for b in range(0, PLANE, 2):
            own = slice(b * BLK, (b + 2) * BLK)
            seen = slice(b * BLK, (b + 2 * HALO + 2) * BLK)
            one = [slice((b + r) * BLK, (b + r + 1) * BLK) for r in range(2)]
            if remote:
                kf, vf = [[ref[at] for at in one] for ref in (far_keys, far_values)]
            else:
                there = [HALO + ((b + r) ^ bit) for r in range(2)]
                kf, vf = [
                    [ref[at * BLK : (at + 1) * BLK] for at in there] for ref in (keys, values)
                ]
            o, d, key_near, value_near, key_far, value_far = attend_pair(
                jnp.concatenate([graded[b, slot + k, 0], graded[b + 1, slot + k, 0]], axis=0),
                jnp.concatenate([graded[b, slot + k, 1], graded[b + 1, slot + k, 1]], axis=0),
                keys[seen],
                values[seen],
                kf,
                vf,
                near_biases(plane(place) * PLANE + b, width, 0, blocks),
                far_bias,
            )
            attended[own] = o
            dq[own] = d
            for acc, near in zip(accs, (key_near, value_near)):
                acc[:, seen] += near
            for acc, far_acc, far in zip(accs, far_accs, (key_far, value_far)):
                for r in range(2):
                    if remote:
                        far_acc[:, one[r]] = far[r]
                    else:
                        acc[:, there[r] * BLK : (there[r] + 1) * BLK] += far[r]
        for i, (acc, far_acc) in enumerate(zip(accs, far_accs)):
            if remote:
                target = to_other if k else to_next
                for m in range(PLANE):
                    owed = far_acc[:, rows_of(me ^ m)] * scales[i]
                    target[m, i] = owed.astype(jnp.bfloat16)
            for m in range(PLANE):
                part[n, m, i] = acc[:, rows_of(HALO + (me ^ m))] * scales[i]
            for m in range(HALO):
                b = (me % HALO) ^ m
                at = m * group + k
                to_next[lead + at, i] = (acc[:, rows_of(next_at + b)] * scales[i]).astype(
                    jnp.bfloat16
                )
                to_last[at, i] = (acc[:, rows_of(last_at + b)] * scales[i]).astype(jnp.bfloat16)
        for m in range(PLANE):
            rows[m][slot + k, 0] = attended[rows_of(me ^ m)]
            rows[m][slot + k, 1] = dq[rows_of(me ^ m)]


def attend(place, widths, sections, pairs, graded, halos, far, group, first, slot, blocks, picked, shared=()):
    count, _, width = pairs[0].shape[1:]
    tile = (BLK, width)
    bf16 = jnp.bfloat16
    inputs = (*pairs, graded, *halos, *far, *shared)
    sizes = [HALO * group + (PLANE if far else 0), HALO * group]
    outs = [jax.ShapeDtypeStruct((pairs[0].shape[0] + group, count, *tile), bf16)] * PLANE
    outs += [jax.ShapeDtypeStruct((size, count, *tile), bf16) for size in sizes]
    outs.append(jax.ShapeDtypeStruct((len(picked), PLANE, count, *tile), jnp.float32))
    if far and 1 in picked:
        outs.append(jax.ShapeDtypeStruct((PLANE, count, *tile), bf16))
    outs = pl.pallas_call(
        functools.partial(
            attend_kernel,
            first=first,
            slot=slot,
            group=group,
            picked=picked,
            remote=len(far),
            blocks=blocks,
            aliased=len(shared),
        ),
        in_specs=[SMEM] * 3 + [VMEM] * len(inputs),
        out_specs=[VMEM] * len(outs),
        out_shape=outs,
        scratch_shapes=[pltpu.VMEM((PADDED * BLK, width), bf16)] * 2
        + [pltpu.VMEM((PLANE * BLK, width), bf16)] * 4
        + [pltpu.VMEM((width, PADDED * BLK), jnp.float32)] * 2
        + [pltpu.VMEM((width, PLANE * BLK), jnp.float32)] * 2,
        input_output_aliases={3 + len(inputs) - len(shared) + m: m for m in range(len(shared))},
        compiler_params=LIMIT,
        cost_estimate=pl.CostEstimate(
            flops=len(picked) * PLANE * 12 * BLK * LINKED * width,
            transcendentals=len(picked) * PLANE * BLK * LINKED,
            bytes_accessed=40 * len(picked) * PLANE * BLK * width,
        ),
    )(place, widths, sections, *inputs)
    return outs[:PLANE], outs[PLANE : PLANE + 2], outs[PLANE + 2 :]


def combine_kernel(place, *refs, parts, remote, base, aliased):
    pieces, rest = refs[:parts], refs[parts:]
    if remote:
        with_other, rest = rest[0], rest[1:]
    (with_next, with_last), outs = rest[:2], rest[2 + aliased :]
    each = pieces[0].shape[0]
    group = each * parts
    lead = PLANE if remote else 0
    for m in range(PLANE):
        own_chip = m < HALO
        next_side = facing(place) if own_chip else jnp.logical_not(facing(place))
        for k in range(group):
            slot = (m % HALO) * group + k
            for i in range(pieces[0].shape[2]):
                owed = jnp.where(next_side, with_next[lead + slot, i], with_last[slot, i])
                total = pieces[k // each][k % each, m, i] + owed.astype(jnp.float32)
                if remote:
                    far = (with_next, with_other)[k]
                    total += far[m, i].astype(jnp.float32)
                outs[m][base + k, i] = jnp.transpose(total.astype(jnp.bfloat16))


def combine(place, parts, owed, rows=(), base=0):
    each, _, *rest = parts[0].shape
    inputs = (*parts, *owed, *rows)
    shape = rows[0].shape if rows else (each * len(parts), *rest)
    return pl.pallas_call(
        functools.partial(
            combine_kernel, parts=len(parts), remote=len(owed) > 2, base=base, aliased=len(rows)
        ),
        in_specs=[SMEM] + [VMEM] * len(inputs),
        out_specs=[VMEM] * PLANE,
        out_shape=[jax.ShapeDtypeStruct(shape, jnp.bfloat16)] * PLANE,
        input_output_aliases={1 + len(inputs) - len(rows) + m: m for m in range(len(rows))},
        compiler_params=LIMIT,
        cost_estimate=moved_cost([*parts, *owed]),
    )(place, *inputs)


def partner(value, axis, apart):
    return lax.ppermute(value, axis, [(i, i ^ 1 << apart) for i in range(lax.axis_size(axis))])


def passed_along(value, axis, by):
    peers = lax.axis_size(axis)
    pairs = [(i, i + by) for i in range(peers) if 0 <= i + by < peers]
    return lax.ppermute(value, axis, pairs)


def to_slots(values, picker):
    return jnp.sum(jnp.where(picker[None, :, :, None], values[:, None, :, :], 0.0), axis=2)


def slots_to_heads(values, picker, filler):
    covered = jnp.any(picker, axis=0)
    summed = jnp.sum(jnp.where(picker[None, :, :, None], values[:, :, None, :], 0.0), axis=1)
    return jnp.where(covered[None, :, None], summed, filler)


def rows_slots_to_heads(values, picker):
    return jnp.einsum(
        "jqid,ih->jqhd", values, picker.astype(jnp.float32), precision=lax.Precision.HIGHEST
    )


def pick_heads(values, picker):
    chooser = picker.astype(jnp.bfloat16)
    return jnp.einsum("ih,jqhd->jqid", chooser, values, preferred_element_type=jnp.float32).astype(
        jnp.bfloat16
    )


def partner_route(values, section_index, low_bits):
    return partner(values, "seq", section_index - low_bits)


def partner_back(values, section_index, low_bits):
    return partner(values, "seq", section_index - low_bits)


def extend_blocks(values, reach, halo_blocks, blocks_dev, mover):
    pieces = [mover(values, distance) for distance in range(reach, 0, -1)]
    pieces = pieces + [values] + [mover(values, -distance) for distance in range(1, reach + 1)]
    start = reach * blocks_dev - halo_blocks
    whole = jnp.concatenate(pieces, axis=1)
    return whole


def move_keys(values, distance):
    return passed_along(values, "seq", distance)


def window_sets(extended, blocks_dev, spread):
    return jnp.stack(
        [extended[:, offset : offset + blocks_dev] for offset in range(spread)], axis=2
    )


def per_device(query_rows, key_rows, value_rows, out_grad, window_blocks, section_heads):
    tokens_dev, head_count, head_width = query_rows.shape
    blocks_dev = tokens_dev // BLK
    low_bits = blocks_dev.bit_length() - 1
    seq_count = lax.axis_size("seq")
    section_total = low_bits + seq_count.bit_length() - 1
    halo_blocks = WB - 1
    reach = (halo_blocks + blocks_dev - 1) // blocks_dev
    padding = reach * blocks_dev
    spread = 2 * WB - 1
    score_scale = 1.0 / math.sqrt(head_width)
    first_block = lax.axis_index("seq") * blocks_dev + jnp.arange(blocks_dev, dtype=jnp.int32)
    all_blocks = blocks_dev * seq_count
    query_blocks = query_rows.reshape(blocks_dev, BLK, head_count, head_width)
    key_blocks = key_rows.reshape(blocks_dev, BLK, head_count, head_width)
    value_blocks = value_rows.reshape(blocks_dev, BLK, head_count, head_width)
    grad_blocks = out_grad.reshape(blocks_dev, BLK, head_count, head_width)
    offsets = jnp.arange(spread, dtype=jnp.int32) - halo_blocks
    near_block = first_block[:, None] + offsets[None, :]
    in_range = (near_block >= 0) & (near_block < all_blocks)
    near_mask = in_range[:, None, :] & (
        jnp.abs(offsets)[None, None, :] < window_blocks[None, :, None]
    )
    wide_mask = near_mask[:, :, None, :, None]
    head_ids = jnp.arange(head_count, dtype=jnp.int32)
    paired = jnp.stack([key_blocks, value_blocks])
    extended = extend_blocks(paired, reach, halo_blocks, blocks_dev, move_keys)
    near_sets = window_sets(extended, blocks_dev, spread)
    near_keys = near_sets[0]
    near_values = near_sets[1]
    near_scores = (
        jnp.einsum("jqhd,jckhd->jhqck", query_blocks, near_keys, preferred_element_type=jnp.float32)
        * score_scale
    )
    near_scores = jnp.where(wide_mask, near_scores, blocked_score)
    top_score = jnp.max(near_scores, axis=(3, 4))
    records = []
    for section_index in range(section_total):
        picker = section_heads[section_index][:, None] == head_ids[None, :]
        slot_width = jnp.sum(jnp.where(picker, window_blocks[None, :], 0), axis=1)
        slot_valid = 2**section_index >= slot_width
        chosen_query = pick_heads(query_blocks, picker)
        chosen_grad = pick_heads(grad_blocks, picker)
        chosen_pair = jnp.stack([pick_heads(key_blocks, picker), pick_heads(value_blocks, picker)])
        partner_pair = partner_route(chosen_pair, section_index, low_bits)
        far_scores = (
            jnp.einsum(
                "jqid,jkid->jiqk", chosen_query, partner_pair[0], preferred_element_type=jnp.float32
            )
            * score_scale
        )
        far_scores = jnp.where(slot_valid[None, :, None, None], far_scores, blocked_score)
        top_score = jnp.maximum(
            top_score, slots_to_heads(jnp.max(far_scores, axis=3), picker, blocked_score)
        )
        records.append(
            (
                section_index,
                picker,
                slot_valid,
                chosen_query,
                chosen_grad,
                chosen_pair,
                partner_pair,
                far_scores,
            )
        )
    row_total = jnp.sum(
        jnp.where(wide_mask, jnp.exp(near_scores - top_score[:, :, :, None, None]), 0.0),
        axis=(3, 4),
    )
    for record in records:
        picker = record[1]
        slot_top = to_slots(top_score, picker)
        far_sum = jnp.sum(
            jnp.where(
                record[2][None, :, None, None], jnp.exp(record[7] - slot_top[:, :, :, None]), 0.0
            ),
            axis=3,
        )
        row_total = row_total + slots_to_heads(far_sum, picker, 0.0)
    log_total = top_score + jnp.log(row_total)
    near_probs = jnp.where(
        wide_mask, jnp.exp(near_scores - log_total[:, :, :, None, None]), 0.0
    ).astype(jnp.bfloat16)
    attended_sum = jnp.einsum(
        "jhqck,jckhd->jqhd", near_probs, near_values, preferred_element_type=jnp.float32
    )
    far_probs_list = []
    for record in records:
        picker = record[1]
        slot_lse = to_slots(log_total, picker)
        far_probs = jnp.where(
            record[2][None, :, None, None], jnp.exp(record[7] - slot_lse[:, :, :, None]), 0.0
        ).astype(jnp.bfloat16)
        far_probs_list.append((far_probs, slot_lse))
        attended_sum = attended_sum + rows_slots_to_heads(
            jnp.einsum(
                "jiqk,jkid->jqid", far_probs, record[6][1], preferred_element_type=jnp.float32
            ),
            picker,
        )
    attended = attended_sum.astype(jnp.bfloat16)
    row_delta = jnp.transpose(
        jnp.sum(grad_blocks.astype(jnp.float32) * attended.astype(jnp.float32), axis=-1), (0, 2, 1)
    )
    near_dprob = jnp.einsum(
        "jqhd,jckhd->jhqck", grad_blocks, near_values, preferred_element_type=jnp.float32
    )
    near_dscore = (
        near_probs.astype(jnp.float32) * (near_dprob - row_delta[:, :, :, None, None])
    ).astype(jnp.bfloat16)
    query_sum = jnp.einsum(
        "jhqck,jckhd->jqhd", near_dscore, near_keys, preferred_element_type=jnp.float32
    )
    far_dscores = []
    for record, probs_pair in zip(records, far_probs_list):
        picker = record[1]
        slot_delta = to_slots(row_delta, picker)
        far_dprob = jnp.einsum(
            "jqid,jkid->jiqk", record[4], record[6][1], preferred_element_type=jnp.float32
        )
        far_dscore = (
            probs_pair[0].astype(jnp.float32) * (far_dprob - slot_delta[:, :, :, None])
        ).astype(jnp.bfloat16)
        far_dscores.append((far_dscore, slot_delta))
        query_sum = query_sum + rows_slots_to_heads(
            jnp.einsum(
                "jiqk,jkid->jqid", far_dscore, record[6][0], preferred_element_type=jnp.float32
            ),
            picker,
        )
    query_grad = (
        (query_sum * score_scale).astype(jnp.bfloat16).reshape(tokens_dev, head_count, head_width)
    )
    near_key_part = (
        jnp.einsum(
            "jhqck,jqhd->jckhd", near_dscore, query_blocks, preferred_element_type=jnp.float32
        )
        * score_scale
    )
    near_value_part = jnp.einsum(
        "jhqck,jqhd->jckhd", near_probs, grad_blocks, preferred_element_type=jnp.float32
    )
    stacked_parts = jnp.stack([near_key_part, near_value_part])
    extended_count = blocks_dev + 2 * padding
    base = padding - halo_blocks
    extended_ids = jnp.arange(extended_count, dtype=jnp.int32)
    own_ids = jnp.arange(blocks_dev, dtype=jnp.int32)
    spread_ids = jnp.arange(spread, dtype=jnp.int32)
    placer = (
        extended_ids[:, None, None] == base + own_ids[None, :, None] + spread_ids[None, None, :]
    ).astype(jnp.float32)
    gathered = jnp.einsum(
        "ejc,xjckhd->xekhd", placer, stacked_parts, precision=lax.Precision.HIGHEST
    )
    own_grads = gathered[:, padding : padding + blocks_dev]
    for distance in range(1, reach + 1):
        lower_slab = gathered[
            :, padding - distance * blocks_dev : padding - (distance - 1) * blocks_dev
        ]
        own_grads = own_grads + passed_along(
            lower_slab.astype(jnp.bfloat16), "seq", -distance
        ).astype(lower_slab.dtype)
        upper_start = padding + blocks_dev + (distance - 1) * blocks_dev
        upper_slab = gathered[:, upper_start : upper_start + blocks_dev]
        own_grads = own_grads + passed_along(
            upper_slab.astype(jnp.bfloat16), "seq", distance
        ).astype(upper_slab.dtype)
    for record, probs_pair, dscore_pair in zip(records, far_probs_list, far_dscores):
        picker = record[1]
        key_part = (
            jnp.einsum(
                "jiqk,jqid->jkid", dscore_pair[0], record[3], preferred_element_type=jnp.float32
            )
            * score_scale
        )
        value_part = jnp.einsum(
            "jiqk,jqid->jkid", probs_pair[0], record[4], preferred_element_type=jnp.float32
        )
        returned = partner_back(jnp.stack([key_part, value_part]), record[0], low_bits)
        own_grads = own_grads + jnp.stack(
            [rows_slots_to_heads(returned[0], picker), rows_slots_to_heads(returned[1], picker)]
        )
    key_grad = own_grads[0].astype(jnp.bfloat16).reshape(tokens_dev, head_count, head_width)
    value_grad = own_grads[1].astype(jnp.bfloat16).reshape(tokens_dev, head_count, head_width)
    return (attended.reshape(tokens_dev, head_count, head_width), query_grad, key_grad, value_grad)


def in_plane(pieces, chip_first=False):
    peers = lax.axis_size("seq")
    pieces = list(pieces)
    for m in range(1, PLANE):
        pieces[m] = lax.ppermute(pieces[m], "seq", [(i, i ^ m) for i in range(peers)])
        if chip_first and m == 1:
            pieces[1], pieces[3] = lax.optimization_barrier((pieces[1], pieces[3]))
    return pieces


def with_next_plane(value):
    return partner(value, "seq", PLANE.bit_length() - 1)


def with_other_plane(value):
    return partner(value, "seq", PLANE.bit_length())


def with_last_plane(value):
    peers = lax.axis_size("seq")
    pairs = []
    for i in range(peers):
        other = i + PLANE if i // PLANE % 2 else i - PLANE
        if 0 <= other < peers:
            pairs.append((i, other))
    return lax.ppermute(value, "seq", pairs)


def plane_all_to_all(value):
    peers = lax.axis_size("seq")
    planes = [list(range(i, i + PLANE)) for i in range(0, peers, PLANE)]
    return lax.all_to_all(value, "seq", 0, 0, axis_index_groups=planes, tiled=True)


def sharded_by_plane(query_rows, key_rows, value_rows, out_grad, widths, sections):
    place = lax.axis_index("seq").astype(jnp.int32).reshape(1)
    blocks = lax.axis_size("seq")
    local = PLANE.bit_length() - 1
    total = sections.shape[0]
    groups = [tuple(range(local, total)), tuple(range(local))]
    order = tuple(s for group in groups for s in group)
    tables = (place, widths, sections)
    sent = pack(place, sections, [key_rows, value_rows], order, True)
    (graded_sent,) = pack(place, sections, [query_rows, out_grad], order, False)
    graded = plane_all_to_all(graded_sent)
    pairs = in_plane(sent)
    next_sent, last_sent = halo_parts(place, pairs)
    far_sent = far_parts(pairs, total - local)
    halos = [with_next_plane(next_sent), with_last_plane(last_sent)]
    halos[0], other_sent = lax.optimization_barrier((halos[0], far_sent[1]))
    far = (with_other_plane(other_sent), with_next_plane(far_sent[0]))
    given = (*tables, pairs, graded, halos)
    size = total - local
    rows, owed, (part_near,) = attend(*given, (), local, 0, size, blocks, range(local))
    owed_near = [with_next_plane(owed[0]), with_last_plane(owed[1])]
    rows, owed, (part_next,) = attend(*given, (far[1],), size, local, 0, blocks, (0,), rows)
    rows, owed, (part_other, far_other) = attend(
        *given, (far[0],), size, local, 0, blocks, (1,), (*rows, *owed)
    )
    other_back = with_other_plane(far_other)
    owed_far = [other_back, with_next_plane(owed[0]), with_last_plane(owed[1])]
    rows = in_plane(combine(place, [part_near], owed_near, rows, total), True)
    columns = in_plane(combine(place, [part_next, part_other], owed_far))
    attended, query_grad = unpack(place, sections, [(groups[0], rows, 0), (groups[1], rows, 1)])
    columns, attended, query_grad = lax.optimization_barrier((columns, attended, query_grad))
    key_grad, value_grad = unpack(place, sections, [(groups[0], columns, 0), (groups[1], rows, 2)])
    return attended, query_grad, key_grad, value_grad


def solution(mesh):
    spec = P(("grp", "seq"), None, None)
    peers = mesh.shape["seq"]

    def per_device_any(*args):
        tokens, heads, width = args[0].shape
        sections, listed = args[5].shape
        once = sections * listed == heads
        if tokens == BLK and once and listed == PLANE and 1 << sections == peers == PLANE**2:
            return sharded_by_plane(*args)
        return per_device(*args)

    return jax.shard_map(
        per_device_any,
        mesh=mesh,
        in_specs=(spec, spec, spec, spec, P(), P()),
        out_specs=(spec,) * 4,
        check_vma=False,
    )
```

```python
import functools
import math

import jax
import jax.numpy as jnp
from jax import lax
from jax.experimental import pallas as pl
from jax.experimental.pallas import tpu as pltpu
from jax.sharding import PartitionSpec as P

BLK = 128
WB = 3
HALO = WB - 1
SPAN = (2 * HALO + 1) * BLK
LINKED = SPAN + BLK
PLANE = 2 * HALO
PADDED = PLANE + 2 * HALO
NT = (((1,), (1,)), ((), ()))
NN = (((1,), (0,)), ((), ()))
blocked_score = -1e30


def mm(a, b, dims=NN):
    return lax.dot_general(a, b, dims, preferred_element_type=jnp.float32)


def moved_cost(arrays):
    return pl.CostEstimate(
        flops=0, transcendentals=0, bytes_accessed=4 * sum(a.size for a in arrays)
    )


def softmax_pair(score, far_score, biases, far_bias, scale2):
    near_parts, far_parts = [], []
    gap = jnp.zeros((BLK, BLK), jnp.bfloat16)
    for r in range(2):
        rows = slice(r * BLK, (r + 1) * BLK)
        sw = score[rows, r * BLK : r * BLK + SPAN] * scale2 + biases[r]
        sf = far_score[r] * scale2 + far_bias
        top = jnp.maximum(jnp.max(sw, axis=1, keepdims=True), jnp.max(sf, axis=1, keepdims=True))
        ew, ef = jnp.exp2(sw - top), jnp.exp2(sf - top)
        total = jnp.sum(ew, axis=1, keepdims=True) + jnp.sum(ef, axis=1, keepdims=True)
        inverse = 1.0 / total
        near = (ew * inverse).astype(jnp.bfloat16)
        near_parts.append(jnp.concatenate([near, gap] if r == 0 else [gap, near], axis=1))
        far_parts.append((ef * inverse).astype(jnp.bfloat16))
    return jnp.concatenate(near_parts, axis=0), far_parts


def attend_pair(q, g, kw, vw, kf, vf, biases, far_bias):
    scale = 1.0 / math.sqrt(q.shape[-1])
    scale2 = scale * math.log2(math.e)
    half = [slice(0, BLK), slice(BLK, 2 * BLK)]
    far_score = [mm(q[half[r]], kf[r], NT) for r in range(2)]
    near, far = softmax_pair(mm(q, kw, NT), far_score, biases, far_bias, scale2)
    far_out = jnp.concatenate([mm(far[r], vf[r]) for r in range(2)], axis=0)
    attended = (mm(near, vw) + far_out).astype(jnp.bfloat16)
    delta = jnp.sum(g.astype(jnp.float32) * attended.astype(jnp.float32), axis=1, keepdims=True)
    d_near = (near.astype(jnp.float32) * (mm(g, vw, NT) - delta)).astype(jnp.bfloat16)
    d_far = [
        (far[r].astype(jnp.float32) * (mm(g[half[r]], vf[r], NT) - delta[half[r]])).astype(
            jnp.bfloat16
        )
        for r in range(2)
    ]
    far_dq = jnp.concatenate([mm(d_far[r], kf[r]) for r in range(2)], axis=0)
    query_grad = ((mm(d_near, kw) + far_dq) * scale).astype(jnp.bfloat16)
    qt, gt = jnp.transpose(q), jnp.transpose(g)
    key_near, value_near = mm(qt, d_near), mm(gt, near)
    key_far = [mm(qt[:, half[r]], d_far[r]) for r in range(2)]
    value_far = [mm(gt[:, half[r]], far[r]) for r in range(2)]
    return attended, query_grad, key_near, value_near, key_far, value_far


def near_biases(b, width, low, high):
    offset = lax.broadcasted_iota(jnp.int32, (1, SPAN), 1) // BLK - HALO
    inside = jnp.abs(offset) < width
    out = []
    for r in range(2):
        there = offset + b + r
        out.append(jnp.where(inside & (there >= low) & (there < high), 0.0, blocked_score))
    return out


def rows_of(block):
    return pl.ds(pl.multiple_of(block * BLK, BLK), BLK)


def whole(shape):
    return pl.BlockSpec(shape, lambda *_: (0,) * len(shape))


SMEM = pl.BlockSpec(memory_space=pltpu.SMEM)
VMEM = pl.BlockSpec(memory_space=pltpu.VMEM)
LIMIT = pltpu.CompilerParams(vmem_limit_bytes=20 << 20)


def pack_kernel(place, sections, *refs, order, count, crossed):
    ins, outs, held = refs[:count], refs[count:-1], refs[-1]
    for i in range(count):
        held[i] = jnp.transpose(ins[i][...], (1, 0, 2))
    for m in range(PLANE):
        owner = seat(place) ^ m if crossed else m
        for k, s in enumerate(order):
            head = sections[s, owner]
            for i in range(count):
                if crossed:
                    outs[m][k, i] = held[i, head]
                else:
                    outs[0][m, k, i] = held[i, head]


def pack(place, sections, arrays, order, crossed):
    tokens, heads, width = arrays[0].shape
    chunk = tokens // 2
    count = len(arrays)
    shape = (len(order), count, tokens, width)
    if crossed:
        shapes = [shape] * PLANE
        specs = [pl.BlockSpec((*shape[:2], chunk, width), lambda i: (0, 0, i, 0))] * PLANE
    else:
        shapes = [(PLANE, *shape)]
        specs = [pl.BlockSpec((PLANE, *shape[:2], chunk, width), lambda i: (0, 0, 0, i, 0))]
    return pl.pallas_call(
        functools.partial(pack_kernel, order=order, count=count, crossed=crossed),
        grid=(tokens // chunk,),
        in_specs=[SMEM, SMEM]
        + [pl.BlockSpec((chunk, heads, width), lambda i: (i, 0, 0))] * count,
        out_specs=specs,
        out_shape=[jax.ShapeDtypeStruct(shape, jnp.bfloat16) for shape in shapes],
        scratch_shapes=[pltpu.VMEM((count, heads, chunk, width), jnp.bfloat16)],
        cost_estimate=moved_cost(arrays),
    )(place, sections, *arrays)


def unpack_kernel(place, sections, *refs, groups, count):
    pieces, outs, held = refs[: len(groups) * PLANE], refs[len(groups) * PLANE : -1], refs[-1]
    for number, group in enumerate(groups):
        for m in range(PLANE):
            for k, s in enumerate(group):
                head = sections[s, seat(place) ^ m]
                for i in range(count):
                    held[i, head] = pieces[number * PLANE + m][k, i]
    for i in range(count):
        outs[i][...] = jnp.transpose(held[i], (1, 0, 2))


def unpack(place, sections, parts):
    flat = [piece for _, pieces, _ in parts for piece in pieces]
    count, tokens, width = flat[0].shape[1:]
    heads = sections.size
    chunk = tokens // 4
    specs = [
        pl.BlockSpec((len(group), count, chunk, width), lambda i, run=run: (run, 0, i, 0))
        for group, _, run in parts
        for _ in range(PLANE)
    ]
    return pl.pallas_call(
        functools.partial(unpack_kernel, groups=[group for group, _, _ in parts], count=count),
        grid=(tokens // chunk,),
        in_specs=[SMEM, SMEM] + specs,
        out_specs=[pl.BlockSpec((chunk, heads, width), lambda i: (i, 0, 0))] * count,
        out_shape=[jax.ShapeDtypeStruct((tokens, heads, width), jnp.bfloat16)] * count,
        scratch_shapes=[pltpu.VMEM((count, heads, chunk, width), jnp.bfloat16)],
        compiler_params=LIMIT,
        cost_estimate=moved_cost(flat),
    )(place, sections, *flat)


def seat(place):
    return place[0] % PLANE


def plane(place):
    return place[0] // PLANE


def facing(place):
    return seat(place) // HALO == 1 - plane(place) % 2


def far_kernel(*refs):
    pieces, outs = refs[:PLANE], refs[PLANE:]
    for k, out in enumerate(outs):
        for m, piece in enumerate(pieces):
            out[m] = piece[k]


def far_parts(pieces, count):
    rest = pieces[0].shape[1:]
    return pl.pallas_call(
        far_kernel,
        in_specs=[VMEM] * PLANE,
        out_specs=[VMEM] * count,
        out_shape=[jax.ShapeDtypeStruct((PLANE, *rest), jnp.bfloat16)] * count,
        compiler_params=LIMIT,
        cost_estimate=moved_cost(pieces),
    )(*pieces)


def halo_kernel(place, *refs):
    pieces, (with_next, with_last) = refs[:PLANE], refs[PLANE:]
    slots = pieces[0].shape[0]

    def fill(base, other):
        for m in range(HALO):
            with_next[m * slots : (m + 1) * slots] = pieces[base + m][...]
            with_last[m * slots : (m + 1) * slots] = pieces[other + m][...]

    @pl.when(facing(place))
    def _():
        fill(0, HALO)

    @pl.when(jnp.logical_not(facing(place)))
    def _():
        fill(HALO, 0)


def halo_parts(place, pieces):
    slots, *rest = pieces[0].shape
    return pl.pallas_call(
        halo_kernel,
        in_specs=[SMEM] + [VMEM] * PLANE,
        out_specs=[VMEM] * 2,
        out_shape=[jax.ShapeDtypeStruct((HALO * slots, *rest), jnp.bfloat16)] * 2,
        compiler_params=LIMIT,
        cost_estimate=moved_cost(pieces),
    )(place, *pieces)


def attend_kernel(place, widths, sections, *refs, first, slot, group, picked, remote, blocks, aliased):
    pairs, (graded, with_next, with_last) = refs[:PLANE], refs[PLANE : PLANE + 3]
    rest = refs[PLANE + 3 :]
    if remote:
        far_in, rest = rest[0], rest[1:]
    rest = rest[aliased:]
    rows, rest = rest[:PLANE], rest[PLANE:]
    (to_next, to_last, part), rest = rest[:3], rest[3:]
    lead = PLANE if remote else 0
    if remote and 1 in picked:
        to_other, rest = rest[0], rest[1:]
    keys, values, far_keys, far_values, attended, dq = rest[:6]
    accs, far_accs = rest[6:8], rest[8:10]
    me = seat(place)
    scales = (1.0 / math.sqrt(keys.shape[-1]), 1.0)
    slots = with_next.shape[0] // HALO
    next_at = jnp.where(plane(place) % 2 == 0, HALO + PLANE, 0)
    last_at = HALO + PLANE - next_at
    for n, k in enumerate(picked):
        width = widths[sections[first + k, me]]
        bit = 1 << first + k
        far_bias = jnp.where(bit >= width, 0.0, blocked_score).astype(jnp.float32)
        for m in range(PLANE):
            keys[rows_of(HALO + (me ^ m))] = pairs[m][slot + k, 0]
            values[rows_of(HALO + (me ^ m))] = pairs[m][slot + k, 1]
        for m in range(HALO):
            b = (me % HALO) ^ m
            at = m * slots + slot + k
            keys[rows_of(next_at + b)] = with_next[at, 0]
            values[rows_of(next_at + b)] = with_next[at, 1]
            keys[rows_of(last_at + b)] = with_last[at, 0]
            values[rows_of(last_at + b)] = with_last[at, 1]
        if remote:
            for m in range(PLANE):
                far_keys[rows_of(me ^ m)] = far_in[m, 0]
                far_values[rows_of(me ^ m)] = far_in[m, 1]
        for acc in accs:
            acc[...] = jnp.zeros_like(acc)
        for b in range(0, PLANE, 2):
            own = slice(b * BLK, (b + 2) * BLK)
            seen = slice(b * BLK, (b + 2 * HALO + 2) * BLK)
            one = [slice((b + r) * BLK, (b + r + 1) * BLK) for r in range(2)]
            if remote:
                kf, vf = [[ref[at] for at in one] for ref in (far_keys, far_values)]
            else:
                there = [HALO + ((b + r) ^ bit) for r in range(2)]
                kf, vf = [
                    [ref[at * BLK : (at + 1) * BLK] for at in there] for ref in (keys, values)
                ]
            o, d, key_near, value_near, key_far, value_far = attend_pair(
                jnp.concatenate([graded[b, slot + k, 0], graded[b + 1, slot + k, 0]], axis=0),
                jnp.concatenate([graded[b, slot + k, 1], graded[b + 1, slot + k, 1]], axis=0),
                keys[seen],
                values[seen],
                kf,
                vf,
                near_biases(plane(place) * PLANE + b, width, 0, blocks),
                far_bias,
            )
            attended[own] = o
            dq[own] = d
            for acc, near in zip(accs, (key_near, value_near)):
                acc[:, seen] += near
            for acc, far_acc, far in zip(accs, far_accs, (key_far, value_far)):
                for r in range(2):
                    if remote:
                        far_acc[:, one[r]] = far[r]
                    else:
                        acc[:, there[r] * BLK : (there[r] + 1) * BLK] += far[r]
        for i, (acc, far_acc) in enumerate(zip(accs, far_accs)):
            if remote:
                target = to_other if k else to_next
                for m in range(PLANE):
                    owed = far_acc[:, rows_of(me ^ m)] * scales[i]
                    target[m, i] = owed.astype(jnp.bfloat16)
            for m in range(PLANE):
                part[n, m, i] = acc[:, rows_of(HALO + (me ^ m))] * scales[i]
            for m in range(HALO):
                b = (me % HALO) ^ m
                at = m * group + k
                to_next[lead + at, i] = (acc[:, rows_of(next_at + b)] * scales[i]).astype(
                    jnp.bfloat16
                )
                to_last[at, i] = (acc[:, rows_of(last_at + b)] * scales[i]).astype(jnp.bfloat16)
        for m in range(PLANE):
            rows[m][slot + k, 0] = attended[rows_of(me ^ m)]
            rows[m][slot + k, 1] = dq[rows_of(me ^ m)]


def attend(place, widths, sections, pairs, graded, halos, far, group, first, slot, blocks, picked, shared=()):
    count, _, width = pairs[0].shape[1:]
    tile = (BLK, width)
    bf16 = jnp.bfloat16
    inputs = (*pairs, graded, *halos, *far, *shared)
    sizes = [HALO * group + (PLANE if far else 0), HALO * group]
    outs = [jax.ShapeDtypeStruct((pairs[0].shape[0] + group, count, *tile), bf16)] * PLANE
    outs += [jax.ShapeDtypeStruct((size, count, *tile), bf16) for size in sizes]
    outs.append(jax.ShapeDtypeStruct((len(picked), PLANE, count, *tile), jnp.float32))
    if far and 1 in picked:
        outs.append(jax.ShapeDtypeStruct((PLANE, count, *tile), bf16))
    outs = pl.pallas_call(
        functools.partial(
            attend_kernel,
            first=first,
            slot=slot,
            group=group,
            picked=picked,
            remote=len(far),
            blocks=blocks,
            aliased=len(shared),
        ),
        in_specs=[SMEM] * 3 + [VMEM] * len(inputs),
        out_specs=[VMEM] * len(outs),
        out_shape=outs,
        scratch_shapes=[pltpu.VMEM((PADDED * BLK, width), bf16)] * 2
        + [pltpu.VMEM((PLANE * BLK, width), bf16)] * 4
        + [pltpu.VMEM((width, PADDED * BLK), jnp.float32)] * 2
        + [pltpu.VMEM((width, PLANE * BLK), jnp.float32)] * 2,
        input_output_aliases={3 + len(inputs) - len(shared) + m: m for m in range(len(shared))},
        compiler_params=LIMIT,
        cost_estimate=pl.CostEstimate(
            flops=len(picked) * PLANE * 12 * BLK * LINKED * width,
            transcendentals=len(picked) * PLANE * BLK * LINKED,
            bytes_accessed=40 * len(picked) * PLANE * BLK * width,
        ),
    )(place, widths, sections, *inputs)
    return outs[:PLANE], outs[PLANE : PLANE + 2], outs[PLANE + 2 :]


def combine_kernel(place, *refs, parts, remote, base, aliased):
    pieces, rest = refs[:parts], refs[parts:]
    if remote:
        with_other, rest = rest[0], rest[1:]
    (with_next, with_last), outs = rest[:2], rest[2 + aliased :]
    each = pieces[0].shape[0]
    group = each * parts
    lead = PLANE if remote else 0
    for m in range(PLANE):
        own_chip = m < HALO
        next_side = facing(place) if own_chip else jnp.logical_not(facing(place))
        for k in range(group):
            slot = (m % HALO) * group + k
            for i in range(pieces[0].shape[2]):
                owed = jnp.where(next_side, with_next[lead + slot, i], with_last[slot, i])
                total = pieces[k // each][k % each, m, i] + owed.astype(jnp.float32)
                if remote:
                    far = (with_next, with_other)[k]
                    total += far[m, i].astype(jnp.float32)
                outs[m][base + k, i] = jnp.transpose(total.astype(jnp.bfloat16))


def combine(place, parts, owed, rows=(), base=0):
    each, _, *rest = parts[0].shape
    inputs = (*parts, *owed, *rows)
    shape = rows[0].shape if rows else (each * len(parts), *rest)
    return pl.pallas_call(
        functools.partial(
            combine_kernel, parts=len(parts), remote=len(owed) > 2, base=base, aliased=len(rows)
        ),
        in_specs=[SMEM] + [VMEM] * len(inputs),
        out_specs=[VMEM] * PLANE,
        out_shape=[jax.ShapeDtypeStruct(shape, jnp.bfloat16)] * PLANE,
        input_output_aliases={1 + len(inputs) - len(rows) + m: m for m in range(len(rows))},
        compiler_params=LIMIT,
        cost_estimate=moved_cost([*parts, *owed]),
    )(place, *inputs)


def partner(value, axis, apart):
    return lax.ppermute(value, axis, [(i, i ^ 1 << apart) for i in range(lax.axis_size(axis))])


def passed_along(value, axis, by):
    peers = lax.axis_size(axis)
    pairs = [(i, i + by) for i in range(peers) if 0 <= i + by < peers]
    return lax.ppermute(value, axis, pairs)


def to_slots(values, picker):
    return jnp.sum(jnp.where(picker[None, :, :, None], values[:, None, :, :], 0.0), axis=2)


def slots_to_heads(values, picker, filler):
    covered = jnp.any(picker, axis=0)
    summed = jnp.sum(jnp.where(picker[None, :, :, None], values[:, :, None, :], 0.0), axis=1)
    return jnp.where(covered[None, :, None], summed, filler)


def rows_slots_to_heads(values, picker):
    return jnp.einsum(
        "jqid,ih->jqhd", values, picker.astype(jnp.float32), precision=lax.Precision.HIGHEST
    )


def pick_heads(values, picker):
    chooser = picker.astype(jnp.bfloat16)
    return jnp.einsum("ih,jqhd->jqid", chooser, values, preferred_element_type=jnp.float32).astype(
        jnp.bfloat16
    )


def partner_route(values, section_index, low_bits):
    return partner(values, "seq", section_index - low_bits)


def partner_back(values, section_index, low_bits):
    return partner(values, "seq", section_index - low_bits)


def extend_blocks(values, reach, halo_blocks, blocks_dev, mover):
    pieces = [mover(values, distance) for distance in range(reach, 0, -1)]
    pieces = pieces + [values] + [mover(values, -distance) for distance in range(1, reach + 1)]
    start = reach * blocks_dev - halo_blocks
    whole = jnp.concatenate(pieces, axis=1)
    return whole


def move_keys(values, distance):
    return passed_along(values, "seq", distance)


def window_sets(extended, blocks_dev, spread):
    return jnp.stack(
        [extended[:, offset : offset + blocks_dev] for offset in range(spread)], axis=2
    )


def per_device(query_rows, key_rows, value_rows, out_grad, window_blocks, section_heads):
    tokens_dev, head_count, head_width = query_rows.shape
    blocks_dev = tokens_dev // BLK
    low_bits = blocks_dev.bit_length() - 1
    seq_count = lax.axis_size("seq")
    section_total = low_bits + seq_count.bit_length() - 1
    halo_blocks = WB - 1
    reach = (halo_blocks + blocks_dev - 1) // blocks_dev
    padding = reach * blocks_dev
    spread = 2 * WB - 1
    score_scale = 1.0 / math.sqrt(head_width)
    first_block = lax.axis_index("seq") * blocks_dev + jnp.arange(blocks_dev, dtype=jnp.int32)
    all_blocks = blocks_dev * seq_count
    query_blocks = query_rows.reshape(blocks_dev, BLK, head_count, head_width)
    key_blocks = key_rows.reshape(blocks_dev, BLK, head_count, head_width)
    value_blocks = value_rows.reshape(blocks_dev, BLK, head_count, head_width)
    grad_blocks = out_grad.reshape(blocks_dev, BLK, head_count, head_width)
    offsets = jnp.arange(spread, dtype=jnp.int32) - halo_blocks
    near_block = first_block[:, None] + offsets[None, :]
    in_range = (near_block >= 0) & (near_block < all_blocks)
    near_mask = in_range[:, None, :] & (
        jnp.abs(offsets)[None, None, :] < window_blocks[None, :, None]
    )
    wide_mask = near_mask[:, :, None, :, None]
    head_ids = jnp.arange(head_count, dtype=jnp.int32)
    paired = jnp.stack([key_blocks, value_blocks])
    extended = extend_blocks(paired, reach, halo_blocks, blocks_dev, move_keys)
    near_sets = window_sets(extended, blocks_dev, spread)
    near_keys = near_sets[0]
    near_values = near_sets[1]
    near_scores = (
        jnp.einsum("jqhd,jckhd->jhqck", query_blocks, near_keys, preferred_element_type=jnp.float32)
        * score_scale
    )
    near_scores = jnp.where(wide_mask, near_scores, blocked_score)
    top_score = jnp.max(near_scores, axis=(3, 4))
    records = []
    for section_index in range(section_total):
        picker = section_heads[section_index][:, None] == head_ids[None, :]
        slot_width = jnp.sum(jnp.where(picker, window_blocks[None, :], 0), axis=1)
        slot_valid = 2**section_index >= slot_width
        chosen_query = pick_heads(query_blocks, picker)
        chosen_grad = pick_heads(grad_blocks, picker)
        chosen_pair = jnp.stack([pick_heads(key_blocks, picker), pick_heads(value_blocks, picker)])
        partner_pair = partner_route(chosen_pair, section_index, low_bits)
        far_scores = (
            jnp.einsum(
                "jqid,jkid->jiqk", chosen_query, partner_pair[0], preferred_element_type=jnp.float32
            )
            * score_scale
        )
        far_scores = jnp.where(slot_valid[None, :, None, None], far_scores, blocked_score)
        top_score = jnp.maximum(
            top_score, slots_to_heads(jnp.max(far_scores, axis=3), picker, blocked_score)
        )
        records.append(
            (
                section_index,
                picker,
                slot_valid,
                chosen_query,
                chosen_grad,
                chosen_pair,
                partner_pair,
                far_scores,
            )
        )
    row_total = jnp.sum(
        jnp.where(wide_mask, jnp.exp(near_scores - top_score[:, :, :, None, None]), 0.0),
        axis=(3, 4),
    )
    for record in records:
        picker = record[1]
        slot_top = to_slots(top_score, picker)
        far_sum = jnp.sum(
            jnp.where(
                record[2][None, :, None, None], jnp.exp(record[7] - slot_top[:, :, :, None]), 0.0
            ),
            axis=3,
        )
        row_total = row_total + slots_to_heads(far_sum, picker, 0.0)
    log_total = top_score + jnp.log(row_total)
    near_probs = jnp.where(
        wide_mask, jnp.exp(near_scores - log_total[:, :, :, None, None]), 0.0
    ).astype(jnp.bfloat16)
    attended_sum = jnp.einsum(
        "jhqck,jckhd->jqhd", near_probs, near_values, preferred_element_type=jnp.float32
    )
    far_probs_list = []
    for record in records:
        picker = record[1]
        slot_lse = to_slots(log_total, picker)
        far_probs = jnp.where(
            record[2][None, :, None, None], jnp.exp(record[7] - slot_lse[:, :, :, None]), 0.0
        ).astype(jnp.bfloat16)
        far_probs_list.append((far_probs, slot_lse))
        attended_sum = attended_sum + rows_slots_to_heads(
            jnp.einsum(
                "jiqk,jkid->jqid", far_probs, record[6][1], preferred_element_type=jnp.float32
            ),
            picker,
        )
    attended = attended_sum.astype(jnp.bfloat16)
    row_delta = jnp.transpose(
        jnp.sum(grad_blocks.astype(jnp.float32) * attended.astype(jnp.float32), axis=-1), (0, 2, 1)
    )
    near_dprob = jnp.einsum(
        "jqhd,jckhd->jhqck", grad_blocks, near_values, preferred_element_type=jnp.float32
    )
    near_dscore = (
        near_probs.astype(jnp.float32) * (near_dprob - row_delta[:, :, :, None, None])
    ).astype(jnp.bfloat16)
    query_sum = jnp.einsum(
        "jhqck,jckhd->jqhd", near_dscore, near_keys, preferred_element_type=jnp.float32
    )
    far_dscores = []
    for record, probs_pair in zip(records, far_probs_list):
        picker = record[1]
        slot_delta = to_slots(row_delta, picker)
        far_dprob = jnp.einsum(
            "jqid,jkid->jiqk", record[4], record[6][1], preferred_element_type=jnp.float32
        )
        far_dscore = (
            probs_pair[0].astype(jnp.float32) * (far_dprob - slot_delta[:, :, :, None])
        ).astype(jnp.bfloat16)
        far_dscores.append((far_dscore, slot_delta))
        query_sum = query_sum + rows_slots_to_heads(
            jnp.einsum(
                "jiqk,jkid->jqid", far_dscore, record[6][0], preferred_element_type=jnp.float32
            ),
            picker,
        )
    query_grad = (
        (query_sum * score_scale).astype(jnp.bfloat16).reshape(tokens_dev, head_count, head_width)
    )
    near_key_part = (
        jnp.einsum(
            "jhqck,jqhd->jckhd", near_dscore, query_blocks, preferred_element_type=jnp.float32
        )
        * score_scale
    )
    near_value_part = jnp.einsum(
        "jhqck,jqhd->jckhd", near_probs, grad_blocks, preferred_element_type=jnp.float32
    )
    stacked_parts = jnp.stack([near_key_part, near_value_part])
    extended_count = blocks_dev + 2 * padding
    base = padding - halo_blocks
    extended_ids = jnp.arange(extended_count, dtype=jnp.int32)
    own_ids = jnp.arange(blocks_dev, dtype=jnp.int32)
    spread_ids = jnp.arange(spread, dtype=jnp.int32)
    placer = (
        extended_ids[:, None, None] == base + own_ids[None, :, None] + spread_ids[None, None, :]
    ).astype(jnp.float32)
    gathered = jnp.einsum(
        "ejc,xjckhd->xekhd", placer, stacked_parts, precision=lax.Precision.HIGHEST
    )
    own_grads = gathered[:, padding : padding + blocks_dev]
    for distance in range(1, reach + 1):
        lower_slab = gathered[
            :, padding - distance * blocks_dev : padding - (distance - 1) * blocks_dev
        ]
        own_grads = own_grads + passed_along(
            lower_slab.astype(jnp.bfloat16), "seq", -distance
        ).astype(lower_slab.dtype)
        upper_start = padding + blocks_dev + (distance - 1) * blocks_dev
        upper_slab = gathered[:, upper_start : upper_start + blocks_dev]
        own_grads = own_grads + passed_along(
            upper_slab.astype(jnp.bfloat16), "seq", distance
        ).astype(upper_slab.dtype)
    for record, probs_pair, dscore_pair in zip(records, far_probs_list, far_dscores):
        picker = record[1]
        key_part = (
            jnp.einsum(
                "jiqk,jqid->jkid", dscore_pair[0], record[3], preferred_element_type=jnp.float32
            )
            * score_scale
        )
        value_part = jnp.einsum(
            "jiqk,jqid->jkid", probs_pair[0], record[4], preferred_element_type=jnp.float32
        )
        returned = partner_back(jnp.stack([key_part, value_part]), record[0], low_bits)
        own_grads = own_grads + jnp.stack(
            [rows_slots_to_heads(returned[0], picker), rows_slots_to_heads(returned[1], picker)]
        )
    key_grad = own_grads[0].astype(jnp.bfloat16).reshape(tokens_dev, head_count, head_width)
    value_grad = own_grads[1].astype(jnp.bfloat16).reshape(tokens_dev, head_count, head_width)
    return (attended.reshape(tokens_dev, head_count, head_width), query_grad, key_grad, value_grad)


def in_plane(pieces, chip_first=False):
    peers = lax.axis_size("seq")
    pieces = list(pieces)
    for m in range(1, PLANE):
        pieces[m] = lax.ppermute(pieces[m], "seq", [(i, i ^ m) for i in range(peers)])
        if chip_first and m == 1:
            pieces = lax.optimization_barrier(pieces)
    return pieces


def with_next_plane(value):
    return partner(value, "seq", PLANE.bit_length() - 1)


def with_other_plane(value):
    return partner(value, "seq", PLANE.bit_length())


def with_last_plane(value):
    peers = lax.axis_size("seq")
    pairs = []
    for i in range(peers):
        other = i + PLANE if i // PLANE % 2 else i - PLANE
        if 0 <= other < peers:
            pairs.append((i, other))
    return lax.ppermute(value, "seq", pairs)


def plane_all_to_all(value):
    peers = lax.axis_size("seq")
    planes = [list(range(i, i + PLANE)) for i in range(0, peers, PLANE)]
    return lax.all_to_all(value, "seq", 0, 0, axis_index_groups=planes, tiled=True)


def sharded_by_plane(query_rows, key_rows, value_rows, out_grad, widths, sections):
    place = lax.axis_index("seq").astype(jnp.int32).reshape(1)
    blocks = lax.axis_size("seq")
    local = PLANE.bit_length() - 1
    total = sections.shape[0]
    groups = [tuple(range(local, total)), tuple(range(local))]
    order = tuple(s for group in groups for s in group)
    tables = (place, widths, sections)
    sent = pack(place, sections, [key_rows, value_rows], order, True)
    (graded_sent,) = pack(place, sections, [query_rows, out_grad], order, False)
    graded = plane_all_to_all(graded_sent)
    pairs = in_plane(sent)
    next_sent, last_sent = halo_parts(place, pairs)
    far_sent = far_parts(pairs, total - local)
    halos = [with_next_plane(next_sent), with_last_plane(last_sent)]
    halos[0], other_sent = lax.optimization_barrier((halos[0], far_sent[1]))
    far = (with_other_plane(other_sent), with_next_plane(far_sent[0]))
    given = (*tables, pairs, graded, halos)
    size = total - local
    rows, owed, (part_near,) = attend(*given, (), local, 0, size, blocks, range(local))
    owed_near = [with_next_plane(owed[0]), with_last_plane(owed[1])]
    rows, owed, (part_next,) = attend(*given, (far[1],), size, local, 0, blocks, (0,), rows)
    rows, owed, (part_other, far_other) = attend(
        *given, (far[0],), size, local, 0, blocks, (1,), (*rows, *owed)
    )
    other_back = with_other_plane(far_other)
    owed_far = [other_back, with_next_plane(owed[0]), with_last_plane(owed[1])]
    rows = in_plane(combine(place, [part_near], owed_near, rows, total), True)
    columns = in_plane(combine(place, [part_next, part_other], owed_far))
    attended, query_grad = unpack(place, sections, [(groups[0], rows, 0), (groups[1], rows, 1)])
    columns, attended, query_grad = lax.optimization_barrier((columns, attended, query_grad))
    key_grad, value_grad = unpack(place, sections, [(groups[0], columns, 0), (groups[1], rows, 2)])
    return attended, query_grad, key_grad, value_grad


def solution(mesh):
    spec = P(("grp", "seq"), None, None)
    peers = mesh.shape["seq"]

    def per_device_any(*args):
        tokens, heads, width = args[0].shape
        sections, listed = args[5].shape
        once = sections * listed == heads
        if tokens == BLK and once and listed == PLANE and 1 << sections == peers == PLANE**2:
            return sharded_by_plane(*args)
        return per_device(*args)

    return jax.shard_map(
        per_device_any,
        mesh=mesh,
        in_specs=(spec, spec, spec, spec, P(), P()),
        out_specs=(spec,) * 4,
        check_vma=False,
    )
```

```python
import functools
import math

import jax
import jax.numpy as jnp
from jax import lax
from jax.experimental import pallas as pl
from jax.experimental.pallas import tpu as pltpu
from jax.sharding import PartitionSpec as P

BLK = 128
WB = 3
HALO = WB - 1
SPAN = (2 * HALO + 1) * BLK
LINKED = SPAN + BLK
PLANE = 2 * HALO
PADDED = PLANE + 2 * HALO
NT = (((1,), (1,)), ((), ()))
NN = (((1,), (0,)), ((), ()))
blocked_score = -1e30


def mm(a, b, dims=NN):
    return lax.dot_general(a, b, dims, preferred_element_type=jnp.float32)


def moved_cost(arrays):
    return pl.CostEstimate(
        flops=0, transcendentals=0, bytes_accessed=4 * sum(a.size for a in arrays)
    )


def softmax_pair(score, far_score, biases, far_bias, scale2):
    near_parts, far_parts = [], []
    gap = jnp.zeros((BLK, BLK), jnp.bfloat16)
    for r in range(2):
        rows = slice(r * BLK, (r + 1) * BLK)
        sw = score[rows, r * BLK : r * BLK + SPAN] * scale2 + biases[r]
        sf = far_score[r] * scale2 + far_bias
        top = jnp.maximum(jnp.max(sw, axis=1, keepdims=True), jnp.max(sf, axis=1, keepdims=True))
        ew, ef = jnp.exp2(sw - top), jnp.exp2(sf - top)
        total = jnp.sum(ew, axis=1, keepdims=True) + jnp.sum(ef, axis=1, keepdims=True)
        inverse = 1.0 / total
        near = (ew * inverse).astype(jnp.bfloat16)
        near_parts.append(jnp.concatenate([near, gap] if r == 0 else [gap, near], axis=1))
        far_parts.append((ef * inverse).astype(jnp.bfloat16))
    return jnp.concatenate(near_parts, axis=0), far_parts


def attend_pair(q, g, kw, vw, kf, vf, biases, far_bias):
    scale = 1.0 / math.sqrt(q.shape[-1])
    scale2 = scale * math.log2(math.e)
    half = [slice(0, BLK), slice(BLK, 2 * BLK)]
    far_score = [mm(q[half[r]], kf[r], NT) for r in range(2)]
    near, far = softmax_pair(mm(q, kw, NT), far_score, biases, far_bias, scale2)
    far_out = jnp.concatenate([mm(far[r], vf[r]) for r in range(2)], axis=0)
    attended = (mm(near, vw) + far_out).astype(jnp.bfloat16)
    delta = jnp.sum(g.astype(jnp.float32) * attended.astype(jnp.float32), axis=1, keepdims=True)
    d_near = (near.astype(jnp.float32) * (mm(g, vw, NT) - delta)).astype(jnp.bfloat16)
    d_far = [
        (far[r].astype(jnp.float32) * (mm(g[half[r]], vf[r], NT) - delta[half[r]])).astype(
            jnp.bfloat16
        )
        for r in range(2)
    ]
    far_dq = jnp.concatenate([mm(d_far[r], kf[r]) for r in range(2)], axis=0)
    query_grad = ((mm(d_near, kw) + far_dq) * scale).astype(jnp.bfloat16)
    qt, gt = jnp.transpose(q), jnp.transpose(g)
    key_near, value_near = mm(qt, d_near), mm(gt, near)
    key_far = [mm(qt[:, half[r]], d_far[r]) for r in range(2)]
    value_far = [mm(gt[:, half[r]], far[r]) for r in range(2)]
    return attended, query_grad, key_near, value_near, key_far, value_far


def near_biases(b, width, low, high):
    offset = lax.broadcasted_iota(jnp.int32, (1, SPAN), 1) // BLK - HALO
    inside = jnp.abs(offset) < width
    out = []
    for r in range(2):
        there = offset + b + r
        out.append(jnp.where(inside & (there >= low) & (there < high), 0.0, blocked_score))
    return out


def rows_of(block):
    return pl.ds(pl.multiple_of(block * BLK, BLK), BLK)


def whole(shape):
    return pl.BlockSpec(shape, lambda *_: (0,) * len(shape))


SMEM = pl.BlockSpec(memory_space=pltpu.SMEM)
VMEM = pl.BlockSpec(memory_space=pltpu.VMEM)
LIMIT = pltpu.CompilerParams(vmem_limit_bytes=20 << 20)


def pack_kernel(place, sections, *refs, order, count, crossed):
    ins, outs, held = refs[:count], refs[count:-1], refs[-1]
    for i in range(count):
        held[i] = jnp.transpose(ins[i][...], (1, 0, 2))
    for m in range(PLANE):
        owner = seat(place) ^ m if crossed else m
        for k, s in enumerate(order):
            head = sections[s, owner]
            for i in range(count):
                if crossed:
                    outs[m][k, i] = held[i, head]
                else:
                    outs[0][m, k, i] = held[i, head]


def pack(place, sections, arrays, order, crossed):
    tokens, heads, width = arrays[0].shape
    chunk = tokens // 2
    count = len(arrays)
    shape = (len(order), count, tokens, width)
    if crossed:
        shapes = [shape] * PLANE
        specs = [pl.BlockSpec((*shape[:2], chunk, width), lambda i: (0, 0, i, 0))] * PLANE
    else:
        shapes = [(PLANE, *shape)]
        specs = [pl.BlockSpec((PLANE, *shape[:2], chunk, width), lambda i: (0, 0, 0, i, 0))]
    return pl.pallas_call(
        functools.partial(pack_kernel, order=order, count=count, crossed=crossed),
        grid=(tokens // chunk,),
        in_specs=[SMEM, SMEM]
        + [pl.BlockSpec((chunk, heads, width), lambda i: (i, 0, 0))] * count,
        out_specs=specs,
        out_shape=[jax.ShapeDtypeStruct(shape, jnp.bfloat16) for shape in shapes],
        scratch_shapes=[pltpu.VMEM((count, heads, chunk, width), jnp.bfloat16)],
        cost_estimate=moved_cost(arrays),
    )(place, sections, *arrays)


def unpack_kernel(place, sections, *refs, groups, bases, count):
    pieces, outs, held = refs[: len(groups) * PLANE], refs[len(groups) * PLANE : -1], refs[-1]
    for number, group in enumerate(groups):
        for m in range(PLANE):
            for k, s in enumerate(group):
                head = sections[s, seat(place) ^ m]
                for i in range(count):
                    held[i, head] = pieces[number * PLANE + m][bases[number] + k, i]
    for i in range(count):
        outs[i][...] = jnp.transpose(held[i], (1, 0, 2))


def unpack(place, sections, parts):
    flat = [piece for _, pieces, _ in parts for piece in pieces]
    count, tokens, width = flat[0].shape[1:]
    heads = sections.size
    return pl.pallas_call(
        functools.partial(
            unpack_kernel,
            groups=[group for group, _, _ in parts],
            bases=[run * len(group) for group, _, run in parts],
            count=count,
        ),
        in_specs=[SMEM, SMEM] + [VMEM] * len(flat),
        out_shape=[jax.ShapeDtypeStruct((tokens, heads, width), jnp.bfloat16)] * count,
        scratch_shapes=[pltpu.VMEM((count, heads, tokens, width), jnp.bfloat16)],
        compiler_params=LIMIT,
        cost_estimate=moved_cost(flat),
    )(place, sections, *flat)


def seat(place):
    return place[0] % PLANE


def plane(place):
    return place[0] // PLANE


def facing(place):
    return seat(place) // HALO == 1 - plane(place) % 2


def far_kernel(*refs):
    pieces, outs = refs[:PLANE], refs[PLANE:]
    for k, out in enumerate(outs):
        for m, piece in enumerate(pieces):
            out[m] = piece[k]


def far_parts(pieces, count):
    rest = pieces[0].shape[1:]
    return pl.pallas_call(
        far_kernel,
        in_specs=[VMEM] * PLANE,
        out_specs=[VMEM] * count,
        out_shape=[jax.ShapeDtypeStruct((PLANE, *rest), jnp.bfloat16)] * count,
        compiler_params=LIMIT,
        cost_estimate=moved_cost(pieces),
    )(*pieces)


def halo_kernel(place, *refs):
    pieces, (with_next, with_last) = refs[:PLANE], refs[PLANE:]
    slots = pieces[0].shape[0]

    def fill(base, other):
        for m in range(HALO):
            with_next[m * slots : (m + 1) * slots] = pieces[base + m][...]
            with_last[m * slots : (m + 1) * slots] = pieces[other + m][...]

    @pl.when(facing(place))
    def _():
        fill(0, HALO)

    @pl.when(jnp.logical_not(facing(place)))
    def _():
        fill(HALO, 0)


def halo_parts(place, pieces):
    slots, *rest = pieces[0].shape
    return pl.pallas_call(
        halo_kernel,
        in_specs=[SMEM] + [VMEM] * PLANE,
        out_specs=[VMEM] * 2,
        out_shape=[jax.ShapeDtypeStruct((HALO * slots, *rest), jnp.bfloat16)] * 2,
        compiler_params=LIMIT,
        cost_estimate=moved_cost(pieces),
    )(place, *pieces)


def attend_kernel(place, widths, sections, *refs, first, slot, group, picked, remote, blocks, aliased):
    pairs, (graded, with_next, with_last) = refs[:PLANE], refs[PLANE : PLANE + 3]
    rest = refs[PLANE + 3 :]
    if remote:
        far_in, rest = rest[0], rest[1:]
    rest = rest[aliased:]
    rows, rest = rest[:PLANE], rest[PLANE:]
    (to_next, to_last, part), rest = rest[:3], rest[3:]
    lead = PLANE if remote else 0
    if remote and 1 in picked:
        to_other, rest = rest[0], rest[1:]
    keys, values, far_keys, far_values, attended, dq = rest[:6]
    accs, far_accs = rest[6:8], rest[8:10]
    me = seat(place)
    scales = (1.0 / math.sqrt(keys.shape[-1]), 1.0)
    slots = with_next.shape[0] // HALO
    next_at = jnp.where(plane(place) % 2 == 0, HALO + PLANE, 0)
    last_at = HALO + PLANE - next_at
    for n, k in enumerate(picked):
        width = widths[sections[first + k, me]]
        bit = 1 << first + k
        far_bias = jnp.where(bit >= width, 0.0, blocked_score).astype(jnp.float32)
        for m in range(PLANE):
            keys[rows_of(HALO + (me ^ m))] = pairs[m][slot + k, 0]
            values[rows_of(HALO + (me ^ m))] = pairs[m][slot + k, 1]
        for m in range(HALO):
            b = (me % HALO) ^ m
            at = m * slots + slot + k
            keys[rows_of(next_at + b)] = with_next[at, 0]
            values[rows_of(next_at + b)] = with_next[at, 1]
            keys[rows_of(last_at + b)] = with_last[at, 0]
            values[rows_of(last_at + b)] = with_last[at, 1]
        if remote:
            for m in range(PLANE):
                far_keys[rows_of(me ^ m)] = far_in[m, 0]
                far_values[rows_of(me ^ m)] = far_in[m, 1]
        for acc in accs:
            acc[...] = jnp.zeros_like(acc)
        for b in range(0, PLANE, 2):
            own = slice(b * BLK, (b + 2) * BLK)
            seen = slice(b * BLK, (b + 2 * HALO + 2) * BLK)
            one = [slice((b + r) * BLK, (b + r + 1) * BLK) for r in range(2)]
            if remote:
                kf, vf = [[ref[at] for at in one] for ref in (far_keys, far_values)]
            else:
                there = [HALO + ((b + r) ^ bit) for r in range(2)]
                kf, vf = [
                    [ref[at * BLK : (at + 1) * BLK] for at in there] for ref in (keys, values)
                ]
            o, d, key_near, value_near, key_far, value_far = attend_pair(
                jnp.concatenate([graded[b, slot + k, 0], graded[b + 1, slot + k, 0]], axis=0),
                jnp.concatenate([graded[b, slot + k, 1], graded[b + 1, slot + k, 1]], axis=0),
                keys[seen],
                values[seen],
                kf,
                vf,
                near_biases(plane(place) * PLANE + b, width, 0, blocks),
                far_bias,
            )
            attended[own] = o
            dq[own] = d
            for acc, near in zip(accs, (key_near, value_near)):
                acc[:, seen] += near
            for acc, far_acc, far in zip(accs, far_accs, (key_far, value_far)):
                for r in range(2):
                    if remote:
                        far_acc[:, one[r]] = far[r]
                    else:
                        acc[:, there[r] * BLK : (there[r] + 1) * BLK] += far[r]
        for i, (acc, far_acc) in enumerate(zip(accs, far_accs)):
            if remote:
                target = to_other if k else to_next
                for m in range(PLANE):
                    owed = far_acc[:, rows_of(me ^ m)] * scales[i]
                    target[m, i] = owed.astype(jnp.bfloat16)
            for m in range(PLANE):
                part[n, m, i] = acc[:, rows_of(HALO + (me ^ m))] * scales[i]
            for m in range(HALO):
                b = (me % HALO) ^ m
                at = m * group + k
                to_next[lead + at, i] = (acc[:, rows_of(next_at + b)] * scales[i]).astype(
                    jnp.bfloat16
                )
                to_last[at, i] = (acc[:, rows_of(last_at + b)] * scales[i]).astype(jnp.bfloat16)
        for m in range(PLANE):
            rows[m][slot + k, 0] = attended[rows_of(me ^ m)]
            rows[m][slot + k, 1] = dq[rows_of(me ^ m)]


def attend(place, widths, sections, pairs, graded, halos, far, group, first, slot, blocks, picked, shared=()):
    count, _, width = pairs[0].shape[1:]
    tile = (BLK, width)
    bf16 = jnp.bfloat16
    inputs = (*pairs, graded, *halos, *far, *shared)
    sizes = [HALO * group + (PLANE if far else 0), HALO * group]
    outs = [jax.ShapeDtypeStruct((pairs[0].shape[0] + group, count, *tile), bf16)] * PLANE
    outs += [jax.ShapeDtypeStruct((size, count, *tile), bf16) for size in sizes]
    outs.append(jax.ShapeDtypeStruct((len(picked), PLANE, count, *tile), jnp.float32))
    if far and 1 in picked:
        outs.append(jax.ShapeDtypeStruct((PLANE, count, *tile), bf16))
    outs = pl.pallas_call(
        functools.partial(
            attend_kernel,
            first=first,
            slot=slot,
            group=group,
            picked=picked,
            remote=len(far),
            blocks=blocks,
            aliased=len(shared),
        ),
        in_specs=[SMEM] * 3 + [VMEM] * len(inputs),
        out_specs=[VMEM] * len(outs),
        out_shape=outs,
        scratch_shapes=[pltpu.VMEM((PADDED * BLK, width), bf16)] * 2
        + [pltpu.VMEM((PLANE * BLK, width), bf16)] * 4
        + [pltpu.VMEM((width, PADDED * BLK), jnp.float32)] * 2
        + [pltpu.VMEM((width, PLANE * BLK), jnp.float32)] * 2,
        input_output_aliases={3 + len(inputs) - len(shared) + m: m for m in range(len(shared))},
        compiler_params=LIMIT,
        cost_estimate=pl.CostEstimate(
            flops=len(picked) * PLANE * 12 * BLK * LINKED * width,
            transcendentals=len(picked) * PLANE * BLK * LINKED,
            bytes_accessed=40 * len(picked) * PLANE * BLK * width,
        ),
    )(place, widths, sections, *inputs)
    return outs[:PLANE], outs[PLANE : PLANE + 2], outs[PLANE + 2 :]


def combine_kernel(place, *refs, parts, remote, base, aliased):
    pieces, rest = refs[:parts], refs[parts:]
    if remote:
        with_other, rest = rest[0], rest[1:]
    (with_next, with_last), outs = rest[:2], rest[2 + aliased :]
    each = pieces[0].shape[0]
    group = each * parts
    lead = PLANE if remote else 0
    for m in range(PLANE):
        own_chip = m < HALO
        next_side = facing(place) if own_chip else jnp.logical_not(facing(place))
        for k in range(group):
            slot = (m % HALO) * group + k
            for i in range(pieces[0].shape[2]):
                owed = jnp.where(next_side, with_next[lead + slot, i], with_last[slot, i])
                total = pieces[k // each][k % each, m, i] + owed.astype(jnp.float32)
                if remote:
                    far = (with_next, with_other)[k]
                    total += far[m, i].astype(jnp.float32)
                outs[m][base + k, i] = jnp.transpose(total.astype(jnp.bfloat16))


def combine(place, parts, owed, rows=(), base=0):
    each, _, *rest = parts[0].shape
    inputs = (*parts, *owed, *rows)
    shape = rows[0].shape if rows else (each * len(parts), *rest)
    return pl.pallas_call(
        functools.partial(
            combine_kernel, parts=len(parts), remote=len(owed) > 2, base=base, aliased=len(rows)
        ),
        in_specs=[SMEM] + [VMEM] * len(inputs),
        out_specs=[VMEM] * PLANE,
        out_shape=[jax.ShapeDtypeStruct(shape, jnp.bfloat16)] * PLANE,
        input_output_aliases={1 + len(inputs) - len(rows) + m: m for m in range(len(rows))},
        compiler_params=LIMIT,
        cost_estimate=moved_cost([*parts, *owed]),
    )(place, *inputs)


def partner(value, axis, apart):
    return lax.ppermute(value, axis, [(i, i ^ 1 << apart) for i in range(lax.axis_size(axis))])


def passed_along(value, axis, by):
    peers = lax.axis_size(axis)
    pairs = [(i, i + by) for i in range(peers) if 0 <= i + by < peers]
    return lax.ppermute(value, axis, pairs)


def to_slots(values, picker):
    return jnp.sum(jnp.where(picker[None, :, :, None], values[:, None, :, :], 0.0), axis=2)


def slots_to_heads(values, picker, filler):
    covered = jnp.any(picker, axis=0)
    summed = jnp.sum(jnp.where(picker[None, :, :, None], values[:, :, None, :], 0.0), axis=1)
    return jnp.where(covered[None, :, None], summed, filler)


def rows_slots_to_heads(values, picker):
    return jnp.einsum(
        "jqid,ih->jqhd", values, picker.astype(jnp.float32), precision=lax.Precision.HIGHEST
    )


def pick_heads(values, picker):
    chooser = picker.astype(jnp.bfloat16)
    return jnp.einsum("ih,jqhd->jqid", chooser, values, preferred_element_type=jnp.float32).astype(
        jnp.bfloat16
    )


def partner_route(values, section_index, low_bits):
    return partner(values, "seq", section_index - low_bits)


def partner_back(values, section_index, low_bits):
    return partner(values, "seq", section_index - low_bits)


def extend_blocks(values, reach, halo_blocks, blocks_dev, mover):
    pieces = [mover(values, distance) for distance in range(reach, 0, -1)]
    pieces = pieces + [values] + [mover(values, -distance) for distance in range(1, reach + 1)]
    start = reach * blocks_dev - halo_blocks
    whole = jnp.concatenate(pieces, axis=1)
    return whole


def move_keys(values, distance):
    return passed_along(values, "seq", distance)


def window_sets(extended, blocks_dev, spread):
    return jnp.stack(
        [extended[:, offset : offset + blocks_dev] for offset in range(spread)], axis=2
    )


def per_device(query_rows, key_rows, value_rows, out_grad, window_blocks, section_heads):
    tokens_dev, head_count, head_width = query_rows.shape
    blocks_dev = tokens_dev // BLK
    low_bits = blocks_dev.bit_length() - 1
    seq_count = lax.axis_size("seq")
    section_total = low_bits + seq_count.bit_length() - 1
    halo_blocks = WB - 1
    reach = (halo_blocks + blocks_dev - 1) // blocks_dev
    padding = reach * blocks_dev
    spread = 2 * WB - 1
    score_scale = 1.0 / math.sqrt(head_width)
    first_block = lax.axis_index("seq") * blocks_dev + jnp.arange(blocks_dev, dtype=jnp.int32)
    all_blocks = blocks_dev * seq_count
    query_blocks = query_rows.reshape(blocks_dev, BLK, head_count, head_width)
    key_blocks = key_rows.reshape(blocks_dev, BLK, head_count, head_width)
    value_blocks = value_rows.reshape(blocks_dev, BLK, head_count, head_width)
    grad_blocks = out_grad.reshape(blocks_dev, BLK, head_count, head_width)
    offsets = jnp.arange(spread, dtype=jnp.int32) - halo_blocks
    near_block = first_block[:, None] + offsets[None, :]
    in_range = (near_block >= 0) & (near_block < all_blocks)
    near_mask = in_range[:, None, :] & (
        jnp.abs(offsets)[None, None, :] < window_blocks[None, :, None]
    )
    wide_mask = near_mask[:, :, None, :, None]
    head_ids = jnp.arange(head_count, dtype=jnp.int32)
    paired = jnp.stack([key_blocks, value_blocks])
    extended = extend_blocks(paired, reach, halo_blocks, blocks_dev, move_keys)
    near_sets = window_sets(extended, blocks_dev, spread)
    near_keys = near_sets[0]
    near_values = near_sets[1]
    near_scores = (
        jnp.einsum("jqhd,jckhd->jhqck", query_blocks, near_keys, preferred_element_type=jnp.float32)
        * score_scale
    )
    near_scores = jnp.where(wide_mask, near_scores, blocked_score)
    top_score = jnp.max(near_scores, axis=(3, 4))
    records = []
    for section_index in range(section_total):
        picker = section_heads[section_index][:, None] == head_ids[None, :]
        slot_width = jnp.sum(jnp.where(picker, window_blocks[None, :], 0), axis=1)
        slot_valid = 2**section_index >= slot_width
        chosen_query = pick_heads(query_blocks, picker)
        chosen_grad = pick_heads(grad_blocks, picker)
        chosen_pair = jnp.stack([pick_heads(key_blocks, picker), pick_heads(value_blocks, picker)])
        partner_pair = partner_route(chosen_pair, section_index, low_bits)
        far_scores = (
            jnp.einsum(
                "jqid,jkid->jiqk", chosen_query, partner_pair[0], preferred_element_type=jnp.float32
            )
            * score_scale
        )
        far_scores = jnp.where(slot_valid[None, :, None, None], far_scores, blocked_score)
        top_score = jnp.maximum(
            top_score, slots_to_heads(jnp.max(far_scores, axis=3), picker, blocked_score)
        )
        records.append(
            (
                section_index,
                picker,
                slot_valid,
                chosen_query,
                chosen_grad,
                chosen_pair,
                partner_pair,
                far_scores,
            )
        )
    row_total = jnp.sum(
        jnp.where(wide_mask, jnp.exp(near_scores - top_score[:, :, :, None, None]), 0.0),
        axis=(3, 4),
    )
    for record in records:
        picker = record[1]
        slot_top = to_slots(top_score, picker)
        far_sum = jnp.sum(
            jnp.where(
                record[2][None, :, None, None], jnp.exp(record[7] - slot_top[:, :, :, None]), 0.0
            ),
            axis=3,
        )
        row_total = row_total + slots_to_heads(far_sum, picker, 0.0)
    log_total = top_score + jnp.log(row_total)
    near_probs = jnp.where(
        wide_mask, jnp.exp(near_scores - log_total[:, :, :, None, None]), 0.0
    ).astype(jnp.bfloat16)
    attended_sum = jnp.einsum(
        "jhqck,jckhd->jqhd", near_probs, near_values, preferred_element_type=jnp.float32
    )
    far_probs_list = []
    for record in records:
        picker = record[1]
        slot_lse = to_slots(log_total, picker)
        far_probs = jnp.where(
            record[2][None, :, None, None], jnp.exp(record[7] - slot_lse[:, :, :, None]), 0.0
        ).astype(jnp.bfloat16)
        far_probs_list.append((far_probs, slot_lse))
        attended_sum = attended_sum + rows_slots_to_heads(
            jnp.einsum(
                "jiqk,jkid->jqid", far_probs, record[6][1], preferred_element_type=jnp.float32
            ),
            picker,
        )
    attended = attended_sum.astype(jnp.bfloat16)
    row_delta = jnp.transpose(
        jnp.sum(grad_blocks.astype(jnp.float32) * attended.astype(jnp.float32), axis=-1), (0, 2, 1)
    )
    near_dprob = jnp.einsum(
        "jqhd,jckhd->jhqck", grad_blocks, near_values, preferred_element_type=jnp.float32
    )
    near_dscore = (
        near_probs.astype(jnp.float32) * (near_dprob - row_delta[:, :, :, None, None])
    ).astype(jnp.bfloat16)
    query_sum = jnp.einsum(
        "jhqck,jckhd->jqhd", near_dscore, near_keys, preferred_element_type=jnp.float32
    )
    far_dscores = []
    for record, probs_pair in zip(records, far_probs_list):
        picker = record[1]
        slot_delta = to_slots(row_delta, picker)
        far_dprob = jnp.einsum(
            "jqid,jkid->jiqk", record[4], record[6][1], preferred_element_type=jnp.float32
        )
        far_dscore = (
            probs_pair[0].astype(jnp.float32) * (far_dprob - slot_delta[:, :, :, None])
        ).astype(jnp.bfloat16)
        far_dscores.append((far_dscore, slot_delta))
        query_sum = query_sum + rows_slots_to_heads(
            jnp.einsum(
                "jiqk,jkid->jqid", far_dscore, record[6][0], preferred_element_type=jnp.float32
            ),
            picker,
        )
    query_grad = (
        (query_sum * score_scale).astype(jnp.bfloat16).reshape(tokens_dev, head_count, head_width)
    )
    near_key_part = (
        jnp.einsum(
            "jhqck,jqhd->jckhd", near_dscore, query_blocks, preferred_element_type=jnp.float32
        )
        * score_scale
    )
    near_value_part = jnp.einsum(
        "jhqck,jqhd->jckhd", near_probs, grad_blocks, preferred_element_type=jnp.float32
    )
    stacked_parts = jnp.stack([near_key_part, near_value_part])
    extended_count = blocks_dev + 2 * padding
    base = padding - halo_blocks
    extended_ids = jnp.arange(extended_count, dtype=jnp.int32)
    own_ids = jnp.arange(blocks_dev, dtype=jnp.int32)
    spread_ids = jnp.arange(spread, dtype=jnp.int32)
    placer = (
        extended_ids[:, None, None] == base + own_ids[None, :, None] + spread_ids[None, None, :]
    ).astype(jnp.float32)
    gathered = jnp.einsum(
        "ejc,xjckhd->xekhd", placer, stacked_parts, precision=lax.Precision.HIGHEST
    )
    own_grads = gathered[:, padding : padding + blocks_dev]
    for distance in range(1, reach + 1):
        lower_slab = gathered[
            :, padding - distance * blocks_dev : padding - (distance - 1) * blocks_dev
        ]
        own_grads = own_grads + passed_along(
            lower_slab.astype(jnp.bfloat16), "seq", -distance
        ).astype(lower_slab.dtype)
        upper_start = padding + blocks_dev + (distance - 1) * blocks_dev
        upper_slab = gathered[:, upper_start : upper_start + blocks_dev]
        own_grads = own_grads + passed_along(
            upper_slab.astype(jnp.bfloat16), "seq", distance
        ).astype(upper_slab.dtype)
    for record, probs_pair, dscore_pair in zip(records, far_probs_list, far_dscores):
        picker = record[1]
        key_part = (
            jnp.einsum(
                "jiqk,jqid->jkid", dscore_pair[0], record[3], preferred_element_type=jnp.float32
            )
            * score_scale
        )
        value_part = jnp.einsum(
            "jiqk,jqid->jkid", probs_pair[0], record[4], preferred_element_type=jnp.float32
        )
        returned = partner_back(jnp.stack([key_part, value_part]), record[0], low_bits)
        own_grads = own_grads + jnp.stack(
            [rows_slots_to_heads(returned[0], picker), rows_slots_to_heads(returned[1], picker)]
        )
    key_grad = own_grads[0].astype(jnp.bfloat16).reshape(tokens_dev, head_count, head_width)
    value_grad = own_grads[1].astype(jnp.bfloat16).reshape(tokens_dev, head_count, head_width)
    return (attended.reshape(tokens_dev, head_count, head_width), query_grad, key_grad, value_grad)


def in_plane(pieces, chip_first=False):
    peers = lax.axis_size("seq")
    pieces = list(pieces)
    for m in range(1, PLANE):
        pieces[m] = lax.ppermute(pieces[m], "seq", [(i, i ^ m) for i in range(peers)])
        if chip_first and m == 1:
            pieces = lax.optimization_barrier(pieces)
    return pieces


def with_next_plane(value):
    return partner(value, "seq", PLANE.bit_length() - 1)


def with_other_plane(value):
    return partner(value, "seq", PLANE.bit_length())


def with_last_plane(value):
    peers = lax.axis_size("seq")
    pairs = []
    for i in range(peers):
        other = i + PLANE if i // PLANE % 2 else i - PLANE
        if 0 <= other < peers:
            pairs.append((i, other))
    return lax.ppermute(value, "seq", pairs)


def plane_all_to_all(value):
    peers = lax.axis_size("seq")
    planes = [list(range(i, i + PLANE)) for i in range(0, peers, PLANE)]
    return lax.all_to_all(value, "seq", 0, 0, axis_index_groups=planes, tiled=True)


def sharded_by_plane(query_rows, key_rows, value_rows, out_grad, widths, sections):
    place = lax.axis_index("seq").astype(jnp.int32).reshape(1)
    blocks = lax.axis_size("seq")
    local = PLANE.bit_length() - 1
    total = sections.shape[0]
    groups = [tuple(range(local, total)), tuple(range(local))]
    order = tuple(s for group in groups for s in group)
    tables = (place, widths, sections)
    sent = pack(place, sections, [key_rows, value_rows], order, True)
    (graded_sent,) = pack(place, sections, [query_rows, out_grad], order, False)
    graded = plane_all_to_all(graded_sent)
    pairs = in_plane(sent)
    next_sent, last_sent = halo_parts(place, pairs)
    far_sent = far_parts(pairs, total - local)
    halos = [with_next_plane(next_sent), with_last_plane(last_sent)]
    halos[0], other_sent = lax.optimization_barrier((halos[0], far_sent[1]))
    far = (with_other_plane(other_sent), with_next_plane(far_sent[0]))
    given = (*tables, pairs, graded, halos)
    size = total - local
    rows, owed, (part_near,) = attend(*given, (), local, 0, size, blocks, range(local))
    owed_near = [with_next_plane(owed[0]), with_last_plane(owed[1])]
    rows, owed, (part_next,) = attend(*given, (far[1],), size, local, 0, blocks, (0,), rows)
    rows, owed, (part_other, far_other) = attend(
        *given, (far[0],), size, local, 0, blocks, (1,), (*rows, *owed)
    )
    other_back = with_other_plane(far_other)
    owed_far = [other_back, with_next_plane(owed[0]), with_last_plane(owed[1])]
    rows = in_plane(combine(place, [part_near], owed_near, rows, total), True)
    columns = in_plane(combine(place, [part_next, part_other], owed_far))
    attended, query_grad = unpack(place, sections, [(groups[0], rows, 0), (groups[1], rows, 1)])
    columns, attended, query_grad = lax.optimization_barrier((columns, attended, query_grad))
    key_grad, value_grad = unpack(place, sections, [(groups[0], columns, 0), (groups[1], rows, 2)])
    return attended, query_grad, key_grad, value_grad


def solution(mesh):
    spec = P(("grp", "seq"), None, None)
    peers = mesh.shape["seq"]

    def per_device_any(*args):
        tokens, heads, width = args[0].shape
        sections, listed = args[5].shape
        once = sections * listed == heads
        if tokens == BLK and once and listed == PLANE and 1 << sections == peers == PLANE**2:
            return sharded_by_plane(*args)
        return per_device(*args)

    return jax.shard_map(
        per_device_any,
        mesh=mesh,
        in_specs=(spec, spec, spec, spec, P(), P()),
        out_specs=(spec,) * 4,
        check_vma=False,
    )
```
